256 devices in a mesh: lev: 8 (over z_lo, x), hor: 32 (over z_hi, y, core).
Axes of the slice: x: 4, y: 4, z: 8 (z_hi: 4, z_lo: 2; z = z_hi * 2 + z_lo), core: 2. Of those that a mesh axis runs over, the one named last changes fastest.
Arguments:
- slab_fields: float32 [4, 32, 524288], P(None, 'lev', 'hor'), may hold values from -6 to 6
- sample_index: int32 [32, 1024], P('hor', 'lev'), may hold values from 0 to 2047
- thickness: float32 [32], replicated, may hold values from 0.3 to 3
- level_cuts: int32 [31], replicated, may hold values 0 or 1
Outputs:
- gram: float32 [2176, 2176], P('hor', 'lev')
The draws below stay inside these ranges and needn't reach their ends.
Inputs may be any that keep to these rules, and one draw needn't show every extreme that they name: sample_index[j, k] indexes a column among the 2048 columns that start at j * 16384 + (k // 128) * 2048.
All inputs are finite; a program needn't handle non-finite values.
Results may differ from the reference program's by a relative error of at most 0.00068.
Values may be sent and summed in bfloat16 or wider, within the bound.
No kernel may reach another device: no remote copies, remote signals or barrier semaphores. Data moves between devices by JAX's collectives and lax.ppermute only.
A program may use at most 128 MiB of HBM per device.

```python
import math
import jax
import jax.numpy as jnp
from jax import lax

LEV = 32
CPD = 2048
SAMP = 128
F = 2176
BLOCK_COLS = 16384
COLS = 524288
SAMPLES_ALL = 32768
N_LEV = 8
N_HOR = 32


def place_ends(values, key, least, largest):
    place = [jax.random.randint(jax.random.fold_in(key, axis), (), 0, length) for axis, length in enumerate(values.shape)]
    longest = values.shape.index(max(values.shape))
    next_to = place[:longest] + [(place[longest] + 1) % values.shape[longest]] + place[longest + 1:]
    return values.at[tuple(place)].set(least).at[tuple(next_to)].set(largest)


def with_spikes(entries, own_key, source, target, parts, factor):
    owner, partner = [(jnp.arange(entries.shape[position]) // (entries.shape[position] // parts)).reshape([-1 if axis == position else 1 for axis in range(entries.ndim)]) for position in (source, target)]
    chosen = jax.random.permutation(own_key, parts)[partner]
    strong = (owner == chosen) | (owner == (partner + parts // 2) % parts)
    return jnp.where(strong, factor * entries, entries)


def level_of(own_key, dims, pieces, low, high):
    gain = 1.0
    for dim, blocks in pieces:
        draws = jax.random.uniform(jax.random.fold_in(jax.random.fold_in(own_key, 6), dim), (blocks,), jnp.float32, low / len(pieces), high / len(pieces))
        gain = gain * jnp.repeat(jnp.exp(draws), dims[dim] // blocks).reshape((-1,) + (1,) * (len(dims) - 1 - dim))
    return gain


def gaussian_with(own_key, shape, spread, reach, split, heavy, kind=jnp.bfloat16):
    entries = spread * jax.random.normal(own_key, shape, jnp.float32)
    if split:
        entries = entries * level_of(own_key, shape, split, -0.22, 0.18)
    return jnp.clip(with_spikes(entries, jax.random.fold_in(own_key, 3), *heavy), -reach, reach).astype(kind)


def setup_inputs(seed: int = 0) -> dict:
    streams_of = jax.random.split(jax.random.key(seed), 5)
    slab_fields = gaussian_with(streams_of[0], (4, LEV, COLS), 1.0, 6.0, ((1, 8), (2, 32)), (2, 1, 32, 2.75), jnp.float32)
    sample_index = place_ends(jax.random.randint(streams_of[1], (N_HOR, N_LEV * SAMP), 0, CPD), jax.random.fold_in(streams_of[1], 1), 0, CPD - 1).astype(jnp.int32)
    thickness = jnp.clip(jnp.exp(jax.random.uniform(streams_of[2], (LEV,), jnp.float32, math.log(0.3), math.log(3.0))), 0.3, 3.0)
    level_cuts = place_ends((jax.random.randint(streams_of[3], (LEV - 1,), 0, 4) < 1).astype(jnp.int32), jax.random.fold_in(streams_of[3], 1), 0, 1)
    return {"slab_fields": slab_fields, "sample_index": sample_index, "thickness": thickness, "level_cuts": level_cuts}


def vertical_filter(values, thickness, level_cuts):
    link = 1.0 - level_cuts.astype(jnp.float32)
    zero_one = jnp.zeros((1,), jnp.float32)
    lower_link = jnp.concatenate([zero_one, link])
    upper_link = jnp.concatenate([link, zero_one])
    lower_weight = jnp.concatenate([zero_one, thickness[:-1]]) * lower_link
    upper_weight = jnp.concatenate([thickness[1:], zero_one]) * upper_link
    zero_row = jnp.zeros_like(values[:, :1, :])
    below = jnp.concatenate([zero_row, values[:, :-1, :]], axis=1)
    above = jnp.concatenate([values[:, 1:, :], zero_row], axis=1)
    numer = 2.0 * thickness[None, :, None] * values + lower_weight[None, :, None] * below + upper_weight[None, :, None] * above
    denom = 2.0 * thickness + lower_weight + upper_weight
    return numer / denom[None, :, None]


def quadratic_features(smooth):
    count = smooth.shape[2]
    later = jnp.concatenate([smooth[2], smooth[3]], axis=0)
    earlier = jnp.concatenate([smooth[0], smooth[1]], axis=0)
    product = (later[:, None, :] * smooth[0][None, :, :]).reshape(-1, count)
    return jnp.concatenate([later, earlier, product], axis=0).astype(jnp.bfloat16)


def reference(slab_fields, sample_index, thickness, level_cuts):
    block_base = (jnp.arange(N_HOR) * BLOCK_COLS).astype(jnp.int32)
    group_base = ((jnp.arange(N_LEV * SAMP) // SAMP) * CPD).astype(jnp.int32)
    columns = (block_base[:, None] + group_base[None, :] + sample_index).astype(jnp.int32)

    def add_block(total, index_row):
        picked = jnp.take(slab_fields, index_row, axis=2)
        features = quadratic_features(vertical_filter(picked, thickness, level_cuts)).astype(jnp.float32)
        return total + jnp.dot(features, features.T, precision=lax.Precision.HIGHEST, preferred_element_type=jnp.float32), None

    start = jnp.zeros((F, F), jnp.float32)
    total, _ = lax.scan(add_block, start, columns)
    return total / SAMPLES_ALL
```

```python
import jax
import jax.numpy as jnp
from jax import lax
from jax.experimental import pallas as pl
from jax.experimental.pallas import tpu as pltpu
from jax.sharding import PartitionSpec as P

LEV, SLOTS, LANES = 32, 4, 128
N_X, N_ZLO, N_Y, N_ZHI = 4, 2, 4, 4
N_LEV, N_HOR = N_X * N_ZLO, N_ZHI * N_Y * 2
GROUP, SAMP = 2048, 128
BLOCK = N_LEV * SAMP
FEAT = 4 * LEV + 2 * LEV * LEV
ROWS_OUT, COLS_OUT = FEAT // N_HOR, FEAT // N_LEV
CHUNK, WINDOW = 72, 80
PIECE = N_ZHI * 2 * CHUNK
SENT = PIECE + CHUNK
VMEM = pl.BlockSpec(memory_space=pltpu.VMEM)


def params(mib):
    return pltpu.CompilerParams(vmem_limit_bytes=mib << 20)


def shift_lev(value, step_zlo, step_x):
    pairs = [(i, (i // N_X ^ step_zlo) * N_X + (i + step_x) % N_X) for i in range(N_LEV)]
    return lax.ppermute(value, "lev", pairs)


def shift_hor(value, step_zhi, step_y, step_core):
    pairs = []
    for i in range(N_HOR):
        zhi, y, core = i // (2 * N_Y), i // 2 % N_Y, i % 2
        to = (zhi + step_zhi) % N_ZHI * 2 * N_Y + (y + step_y) % N_Y * 2 + (core ^ step_core)
        pairs.append((i, to))
    return lax.ppermute(value, "hor", pairs)


def pick_kernel(index_ref, slab_ref, out_ref):
    for group in range(N_LEV):
        index = jnp.broadcast_to(index_ref[group : group + 1, :], (8, LANES))
        lane, tile = index % LANES, index // LANES
        hits = [tile == t for t in range(GROUP // LANES)]
        for pair in range(2):
            total = jnp.zeros((8, LANES), jnp.float32)
            for t in range(GROUP // LANES):
                at = pl.ds(group * GROUP + t * LANES, LANES)
                both = jnp.concatenate([slab_ref[2 * pair, :, at], slab_ref[2 * pair + 1, :, at]], axis=0)
                total = jnp.where(hits[t], jnp.take_along_axis(both, lane, axis=1), total)
            out_ref[8 * pair : 8 * pair + 8, group * SAMP : (group + 1) * SAMP] = total


def smooth_kernel(coef_ref, w0_ref, w1_ref, w2_ref, w3_ref, out_ref, raw_ref):
    x = lax.axis_index("lev") % N_X
    for step, ref in enumerate((w0_ref, w1_ref, w2_ref, w3_ref)):
        source = lax.rem(x - step + N_X, N_X)
        for zlo in range(N_ZLO):
            raw_ref[zlo * N_X + source] = ref[zlo]

    def tile(t, carry):
        at = pl.ds(pl.multiple_of(t * LANES, LANES), LANES)
        for slot in range(SLOTS):
            rows = [raw_ref[lev, 4 * slot : 4 * slot + 4, at] for lev in range(N_LEV)]
            value = jnp.concatenate(rows, axis=0)
            below, above = pltpu.roll(value, 1, 0), pltpu.roll(value, LEV - 1, 0)
            out_ref[slot * LEV : (slot + 1) * LEV, at] = (
                coef_ref[0:LEV] * value + coef_ref[LEV : 2 * LEV] * below + coef_ref[2 * LEV :] * above
            )
        return carry

    lax.fori_loop(0, BLOCK // LANES, tile, 0)


def gram_kernel(own_ref, other_ref, s0_ref, s1_ref, s2_ref, s3_ref, feat_ref, left_ref, prod_ref):
    hor, lev = lax.axis_index("hor"), lax.axis_index("lev")
    zhi, y, core = hor // (2 * N_Y), hor // 2 % N_Y, hor % 2
    for block, ref in enumerate((own_ref, other_ref)):

        def tile(t, carry):
            at = pl.ds(pl.multiple_of(t * LANES, LANES), LANES)
            to = pl.ds(pl.multiple_of(block * BLOCK + t * LANES, LANES), LANES)
            early = ref[0 : 2 * LEV, at]
            feat_ref[0 : 2 * LEV, to] = ref[2 * LEV : 4 * LEV, at].astype(jnp.bfloat16)
            feat_ref[2 * LEV : 4 * LEV, to] = early.astype(jnp.bfloat16)
            first = early[0:LEV]
            for m in range(2 * LEV):
                row = jnp.broadcast_to(ref[pl.ds(2 * LEV + m, 1), at], (LEV, LANES))
                feat_ref[4 * LEV + m * LEV : 4 * LEV + (m + 1) * LEV, to] = (row * first).astype(jnp.bfloat16)
            return carry

        lax.fori_loop(0, BLOCK // LANES, tile, 0)

    right = pl.ds(pl.multiple_of(lev * COLS_OUT, 16), COLS_OUT)
    for step_y, out_ref in enumerate((s0_ref, s1_ref, s2_ref, s3_ref)):
        to_y = lax.rem(y + step_y, N_Y)
        skip = 8 * lax.rem(to_y, 2)
        for step_z in range(N_ZHI):
            to_z = lax.rem(zhi + step_z, N_ZHI)
            start = (to_z * N_Y + to_y) * 2 * ROWS_OUT + core * 64 - skip
            left_ref[step_z * WINDOW : (step_z + 1) * WINDOW, :] = feat_ref[pl.ds(pl.multiple_of(start, 16), WINDOW), :]
        prod_ref[...] = lax.dot_general(
            left_ref[...], feat_ref[right, :], (((1,), (1,)), ((), ())), preferred_element_type=jnp.float32
        )
        for step_z in range(N_ZHI):
            rows = pl.ds(pl.multiple_of(step_z * WINDOW + skip, 8), CHUNK)
            for half in range(2):
                place = (2 * step_z + half) * CHUNK
                out_ref[place : place + CHUNK, :] = prod_ref[rows, half * LANES : (half + 1) * LANES]
            out_ref[PIECE:SENT, 16 * step_z : 16 * step_z + 16] = prod_ref[rows, 2 * LANES : COLS_OUT]


def add_kernel(s0_ref, s1_ref, s2_ref, s3_ref, t0_ref, t1_ref, t2_ref, t3_ref):
    def total(rows):
        return (s0_ref[rows, :] + s1_ref[rows, :]) + (s2_ref[rows, :] + s3_ref[rows, :])

    rest = total(slice(PIECE, SENT))
    for step_z, ref in enumerate((t0_ref, t1_ref, t2_ref, t3_ref)):
        ref[0 : 2 * CHUNK, :] = total(slice(step_z * 2 * CHUNK, (step_z + 1) * 2 * CHUNK))
        ref[2 * CHUNK :, :] = rest


def final_kernel(t0_ref, t1_ref, t2_ref, t3_ref, out_ref):
    odd = lax.axis_index("hor") % 2 == 1
    refs = (t0_ref, t1_ref, t2_ref, t3_ref)
    scale = 1.0 / (BLOCK * N_HOR)

    def place(value):
        return jnp.where(odd, value[CHUNK - ROWS_OUT : CHUNK], value[0:ROWS_OUT]) * scale

    for half in range(2):
        rows = slice(half * CHUNK, (half + 1) * CHUNK)
        value = (t0_ref[rows, :] + t1_ref[rows, :]) + (t2_ref[rows, :] + t3_ref[rows, :])
        out_ref[:, half * LANES : (half + 1) * LANES] = place(value)
    rest = [ref[2 * CHUNK :, 16 * k : 16 * k + 16] for k, ref in enumerate(refs)]
    out_ref[:, 2 * LANES :] = place((rest[0] + rest[1]) + (rest[2] + rest[3]))


def filter_coefficients(thickness, level_cuts):
    link = 1.0 - level_cuts.astype(jnp.float32)
    zero_one = jnp.zeros((1,), jnp.float32)
    lower = jnp.concatenate([zero_one, thickness[:-1] * link])
    upper = jnp.concatenate([thickness[1:] * link, zero_one])
    denom = 2.0 * thickness + lower + upper
    coef = jnp.concatenate([2.0 * thickness / denom, lower / denom, upper / denom])
    return jnp.broadcast_to(coef[:, None], (3 * LEV, LANES))


def on_device(slab_fields, sample_index, thickness, level_cuts):
    f32 = jnp.float32
    coef = filter_coefficients(thickness, level_cuts)
    lists = lax.all_to_all(jnp.broadcast_to(sample_index, (N_LEV, SAMP)), "lev", 0, 0, tiled=True)
    picked = pl.pallas_call(
        pick_kernel,
        out_shape=jax.ShapeDtypeStruct((4 * SLOTS, BLOCK), f32),
        in_specs=[VMEM] * 2,
        out_specs=VMEM,
        compiler_params=params(16),
        name="pick",
    )(lists, slab_fields)
    across = shift_lev(picked, 1, 0)
    up = lax.axis_index("lev") // N_X == 1
    near = jnp.stack([jnp.where(up, across, picked), jnp.where(up, picked, across)])
    far = {k: shift_lev(near, 0, k) for k in (2, 1, 3)}
    own = pl.pallas_call(
        smooth_kernel,
        out_shape=jax.ShapeDtypeStruct((SLOTS * LEV, BLOCK), f32),
        in_specs=[VMEM] * 5,
        out_specs=VMEM,
        scratch_shapes=[pltpu.VMEM((N_LEV, 4 * SLOTS, BLOCK), f32)],
        compiler_params=params(16),
        name="smooth",
    )(coef, near, far[1], far[2], far[3])
    other = shift_hor(own, 0, 0, 1)
    parts = pl.pallas_call(
        gram_kernel,
        out_shape=[jax.ShapeDtypeStruct((SENT, LANES), f32)] * N_Y,
        in_specs=[VMEM] * 2,
        out_specs=[VMEM] * N_Y,
        scratch_shapes=[
            pltpu.VMEM((FEAT, 2 * BLOCK), jnp.bfloat16),
            pltpu.VMEM((N_ZHI * WINDOW, 2 * BLOCK), jnp.bfloat16),
            pltpu.VMEM((N_ZHI * WINDOW, COLS_OUT), f32),
        ],
        compiler_params=params(32),
        name="gram",
    )(own, other)
    from_y = {k: shift_hor(parts[k], 0, k, 0) for k in (2, 1, 3)}
    sums = pl.pallas_call(
        add_kernel,
        out_shape=[jax.ShapeDtypeStruct((3 * CHUNK, LANES), f32)] * N_ZHI,
        in_specs=[VMEM] * N_Y,
        out_specs=[VMEM] * N_ZHI,
        compiler_params=params(8),
        name="add",
    )(parts[0], from_y[1], from_y[2], from_y[3])
    from_z = {k: shift_hor(sums[k], k, 0, 0) for k in (2, 1, 3)}
    return pl.pallas_call(
        final_kernel,
        out_shape=jax.ShapeDtypeStruct((ROWS_OUT, COLS_OUT), f32),
        in_specs=[VMEM] * N_ZHI,
        out_specs=VMEM,
        compiler_params=params(8),
        name="final",
    )(sums[0], from_z[1], from_z[2], from_z[3])


def solution(mesh):
    in_specs = (P(None, "lev", "hor"), P("hor", "lev"), P(), P())
    out_specs = P("hor", "lev")
    return jax.shard_map(on_device, mesh=mesh, in_specs=in_specs, out_specs=out_specs, check_vma=False)
```

```python
import functools

import jax
import jax.numpy as jnp
from jax import lax
from jax.experimental import pallas as pl
from jax.experimental.pallas import tpu as pltpu
from jax.sharding import PartitionSpec as P

LEV, SLOTS, LANES = 32, 4, 128
N_X, N_ZLO, N_Y, N_ZHI = 4, 2, 4, 4
N_LEV, N_HOR = N_X * N_ZLO, N_ZHI * N_Y * 2
GROUP, SAMP = 2048, 128
BLOCK = N_LEV * SAMP
FEAT = 4 * LEV + 2 * LEV * LEV
ROWS_OUT, COLS_OUT = FEAT // N_HOR, FEAT // N_LEV
CHUNK, WINDOW = 72, 80
PIECE = N_ZHI * 2 * CHUNK
SENT = PIECE + CHUNK
LAST = 2 * CHUNK + 16
SHARE = 1 << 18
VMEM = pl.BlockSpec(memory_space=pltpu.VMEM)


def params(mib):
    return pltpu.CompilerParams(vmem_limit_bytes=mib << 20)


def cost(flops, moved):
    return pl.CostEstimate(flops=flops, bytes_accessed=moved, transcendentals=0)


def shift_lev(value, step_zlo, step_x):
    pairs = [(i, (i // N_X ^ step_zlo) * N_X + (i + step_x) % N_X) for i in range(N_LEV)]
    return lax.ppermute(value, "lev", pairs)


def shift_hor(value, step_zhi, step_y, step_core):
    pairs = []
    for i in range(N_HOR):
        zhi, y, core = i // (2 * N_Y), i // 2 % N_Y, i % 2
        to = (zhi + step_zhi) % N_ZHI * 2 * N_Y + (y + step_y) % N_Y * 2 + (core ^ step_core)
        pairs.append((i, to))
    return lax.ppermute(value, "hor", pairs)


def repeat_kernel(index_ref, out_ref):
    for lev in range(N_LEV):
        out_ref[lev] = index_ref[...]


def stage_kernel(slab_ref, out_ref):
    for slot in range(SLOTS):
        out_ref[4 * slot : 4 * slot + 4, :] = slab_ref[slot]


def pick_kernel(index_ref, slab_ref, out_ref):
    for group in range(N_LEV):
        index = jnp.broadcast_to(index_ref[group], (8, LANES))
        lane, tile = index % LANES, index // LANES
        hits = [tile == t for t in range(GROUP // LANES)]
        for pair in range(2):
            rows = slice(8 * pair, 8 * pair + 8)
            total = jnp.zeros((8, LANES), jnp.float32)
            for t in range(GROUP // LANES):
                at = slice(group * GROUP + t * LANES, group * GROUP + (t + 1) * LANES)
                total = jnp.where(hits[t], jnp.take_along_axis(slab_ref[rows, at], lane, axis=1), total)
            out_ref[rows, group * SAMP : (group + 1) * SAMP] = total


def smooth_kernel(coef_ref, w0_ref, w1_ref, w2_ref, w3_ref, out_ref, raw_ref):
    x = lax.axis_index("lev") % N_X
    for step, ref in enumerate((w0_ref, w1_ref, w2_ref, w3_ref)):
        source = lax.rem(x - step + N_X, N_X)
        for zlo in range(N_ZLO):
            raw_ref[zlo * N_X + source] = ref[zlo]

    def tile(t, carry):
        at = pl.ds(pl.multiple_of(t * LANES, LANES), LANES)
        for slot in range(SLOTS):
            rows = [raw_ref[lev, 4 * slot : 4 * slot + 4, at] for lev in range(N_LEV)]
            value = jnp.concatenate(rows, axis=0)
            below, above = pltpu.roll(value, 1, 0), pltpu.roll(value, LEV - 1, 0)
            out_ref[slot * LEV : (slot + 1) * LEV, at] = (
                coef_ref[0:LEV] * value + coef_ref[LEV : 2 * LEV] * below + coef_ref[2 * LEV :] * above
            )
        return carry

    lax.fori_loop(0, BLOCK // LANES, tile, 0)


def feature_kernel(smooth_ref, feat_ref):
    def tile(t, carry):
        at = pl.ds(pl.multiple_of(t * LANES, LANES), LANES)
        early = smooth_ref[0 : 2 * LEV, at]
        feat_ref[0 : 2 * LEV, at] = smooth_ref[2 * LEV : 4 * LEV, at].astype(jnp.bfloat16)
        feat_ref[2 * LEV : 4 * LEV, at] = early.astype(jnp.bfloat16)
        first = early[0:LEV]
        for m in range(2 * LEV):
            row = jnp.broadcast_to(smooth_ref[pl.ds(2 * LEV + m, 1), at], (LEV, LANES))
            feat_ref[4 * LEV + m * LEV : 4 * LEV + (m + 1) * LEV, at] = (row * first).astype(jnp.bfloat16)
        return carry

    lax.fori_loop(0, BLOCK // LANES, tile, 0)


def gram_kernel(step_y, own_ref, other_ref, out_ref, left_ref, prod_ref):
    hor, lev = lax.axis_index("hor"), lax.axis_index("lev")
    zhi, y, core = hor // (2 * N_Y), hor // 2 % N_Y, hor % 2
    right = pl.ds(pl.multiple_of(lev * COLS_OUT, 16), COLS_OUT)
    to_y = lax.rem(y + step_y, N_Y)
    skip = 8 * lax.rem(to_y, 2)
    for block, ref in enumerate((own_ref, other_ref)):
        for step_z in range(N_ZHI):
            to_z = lax.rem(zhi + step_z, N_ZHI)
            start = (to_z * N_Y + to_y) * 2 * ROWS_OUT + core * 64 - skip
            rows = pl.ds(pl.multiple_of(start, 16), WINDOW)
            left_ref[step_z * WINDOW : (step_z + 1) * WINDOW, :] = ref[rows, :]
        part = lax.dot_general(
            left_ref[...], ref[right, :], (((1,), (1,)), ((), ())), preferred_element_type=jnp.float32
        )
        prod_ref[...] = part + prod_ref[...] if block else part
    for step_z in range(N_ZHI):
        rows = pl.ds(pl.multiple_of(step_z * WINDOW + skip, 8), CHUNK)
        for half in range(2):
            place = (2 * step_z + half) * CHUNK
            out_ref[place : place + CHUNK, :] = prod_ref[rows, half * LANES : (half + 1) * LANES]
        out_ref[PIECE:SENT, 16 * step_z : 16 * step_z + 16] = prod_ref[rows, 2 * LANES : COLS_OUT]


def add_kernel(a_ref, b_ref, out_ref):
    out_ref[...] = a_ref[...] + b_ref[...]


def split_kernel(a_ref, b_ref, t0_ref, t1_ref, t2_ref, t3_ref):
    rest = a_ref[PIECE:SENT, :] + b_ref[PIECE:SENT, :]
    strip = lax.broadcasted_iota(jnp.int32, (8, LANES), 1) // 16
    for step_z, ref in enumerate((t0_ref, t1_ref, t2_ref, t3_ref)):
        rows = slice(step_z * 2 * CHUNK, (step_z + 1) * 2 * CHUNK)
        ref[0 : 2 * CHUNK, :] = a_ref[rows, :] + b_ref[rows, :]
        packed = jnp.zeros((8, LANES), jnp.float32)
        for group in range(8):
            moved = pltpu.roll(rest[8 * group : 8 * group + 8], 16 * (group - step_z) % LANES, 1)
            packed = jnp.where(strip == group, moved, packed)
        ref[2 * CHUNK : 2 * CHUNK + 8, :] = packed
        ref[2 * CHUNK + 8 : LAST, :] = pltpu.roll(rest[64:CHUNK], -16 * step_z % LANES, 1)


def final_kernel(t0_ref, t1_ref, t2_ref, t3_ref, out_ref):
    odd = lax.axis_index("hor") % 2 == 1
    scale = 1.0 / (BLOCK * N_HOR)

    def total(rows):
        return (t0_ref[rows, :] + t1_ref[rows, :]) + (t2_ref[rows, :] + t3_ref[rows, :])

    def place(value):
        return jnp.where(odd, value[CHUNK - ROWS_OUT : CHUNK], value[0:ROWS_OUT]) * scale

    for half in range(2):
        value = total(slice(half * CHUNK, (half + 1) * CHUNK))
        out_ref[:, half * LANES : (half + 1) * LANES] = place(value)
    packed = total(slice(2 * CHUNK, 2 * CHUNK + 8))
    rest = [pltpu.roll(packed, -16 * group % LANES, 1) for group in range(8)]
    rest.append(total(slice(2 * CHUNK + 8, LAST)))
    out_ref[:, 2 * LANES :] = place(jnp.concatenate(rest, axis=0))[:, :16]


def filter_coefficients(thickness, level_cuts):
    link = 1.0 - level_cuts.astype(jnp.float32)
    zero_one = jnp.zeros((1,), jnp.float32)
    lower = jnp.concatenate([zero_one, thickness[:-1] * link])
    upper = jnp.concatenate([thickness[1:] * link, zero_one])
    denom = 2.0 * thickness + lower + upper
    coef = jnp.concatenate([2.0 * thickness / denom, lower / denom, upper / denom])
    return jnp.broadcast_to(coef[:, None], (3 * LEV, LANES))


def features(smoothed):
    return pl.pallas_call(
        feature_kernel,
        out_shape=jax.ShapeDtypeStruct((FEAT, BLOCK), jnp.bfloat16),
        in_specs=[VMEM],
        out_specs=VMEM,
        compiler_params=params(12),
        cost_estimate=cost(FEAT * BLOCK, 5 << 20),
        name="features",
    )(smoothed)


def on_device(slab_fields, sample_index, thickness, level_cuts):
    f32 = jnp.float32
    coef = filter_coefficients(thickness, level_cuts)
    repeated = pl.pallas_call(
        repeat_kernel,
        out_shape=jax.ShapeDtypeStruct((N_LEV, 1, SAMP), jnp.int32),
        in_specs=[VMEM],
        out_specs=VMEM,
        compiler_params=params(1),
        name="repeat",
    )(sample_index)
    lists = lax.all_to_all(repeated, "lev", 0, 0, tiled=True)
    staged = pl.pallas_call(
        stage_kernel,
        out_shape=jax.ShapeDtypeStruct((4 * SLOTS, N_LEV * GROUP), f32),
        in_specs=[VMEM],
        out_specs=VMEM,
        compiler_params=params(8),
        cost_estimate=cost(0, 2 << 20),
        name="stage",
    )(slab_fields)
    picked = pl.pallas_call(
        pick_kernel,
        out_shape=jax.ShapeDtypeStruct((4 * SLOTS, BLOCK), f32),
        in_specs=[VMEM] * 2,
        out_specs=VMEM,
        compiler_params=params(8),
        name="pick",
    )(lists, staged)
    across = shift_lev(picked, 1, 0)
    up = lax.axis_index("lev") // N_X == 1
    near = jnp.stack([jnp.where(up, across, picked), jnp.where(up, picked, across)])
    far = {k: shift_lev(near, 0, k) for k in (2, 1, 3)}
    own = pl.pallas_call(
        smooth_kernel,
        out_shape=jax.ShapeDtypeStruct((SLOTS * LEV, BLOCK), f32),
        in_specs=[VMEM] * 5,
        out_specs=VMEM,
        scratch_shapes=[pltpu.VMEM((N_LEV, 4 * SLOTS, BLOCK), f32)],
        compiler_params=params(16),
        name="smooth",
    )(coef, near, far[1], far[2], far[3])
    other = shift_hor(own, 0, 0, 1)
    feats = [features(own), features(other)]
    parts = {}
    for k in (2, 1, 3, 0):
        parts[k] = pl.pallas_call(
            functools.partial(gram_kernel, k),
            out_shape=jax.ShapeDtypeStruct((SENT, LANES), f32),
            in_specs=[VMEM] * 2,
            out_specs=VMEM,
            scratch_shapes=[
                pltpu.VMEM((N_ZHI * WINDOW, BLOCK), jnp.bfloat16),
                pltpu.VMEM((N_ZHI * WINDOW, COLS_OUT), f32),
            ],
            compiler_params=params(16),
            cost_estimate=cost(1, SHARE),
            name="gram",
        )(*feats)
    from_y = {k: shift_hor(parts[k], 0, k, 0) for k in (2, 1, 3)}
    total = parts[0]
    for k in (2, 1):
        total = pl.pallas_call(
            add_kernel,
            out_shape=jax.ShapeDtypeStruct((SENT, LANES), f32),
            in_specs=[VMEM] * 2,
            out_specs=VMEM,
            compiler_params=params(8),
            cost_estimate=cost(1, SHARE),
            name="add",
        )(total, from_y[k])
    sums = pl.pallas_call(
        split_kernel,
        out_shape=[jax.ShapeDtypeStruct((LAST, LANES), f32)] * N_ZHI,
        in_specs=[VMEM] * 2,
        out_specs=[VMEM] * N_ZHI,
        compiler_params=params(8),
        cost_estimate=cost(1, SHARE),
        name="split",
    )(total, from_y[3])
    from_z = {k: shift_hor(sums[k], k, 0, 0) for k in (2, 1, 3)}
    return pl.pallas_call(
        final_kernel,
        out_shape=jax.ShapeDtypeStruct((ROWS_OUT, COLS_OUT), f32),
        in_specs=[VMEM] * N_ZHI,
        out_specs=VMEM,
        compiler_params=params(8),
        name="final",
    )(sums[0], from_z[1], from_z[2], from_z[3])


def solution(mesh):
    in_specs = (P(None, "lev", "hor"), P("hor", "lev"), P(), P())
    out_specs = P("hor", "lev")
    return jax.shard_map(on_device, mesh=mesh, in_specs=in_specs, out_specs=out_specs, check_vma=False)
```

```python
import functools

import jax
import jax.numpy as jnp
from jax import lax
from jax.experimental import pallas as pl
from jax.experimental.pallas import tpu as pltpu
from jax.sharding import PartitionSpec as P

LEV, SLOTS, LANES = 32, 4, 128
N_X, N_ZLO, N_Y, N_ZHI = 4, 2, 4, 4
N_LEV, N_HOR = N_X * N_ZLO, N_ZHI * N_Y * 2
GROUP, SAMP = 2048, 128
BLOCK = N_LEV * SAMP
FEAT = 4 * LEV + 2 * LEV * LEV
ROWS_OUT, COLS_OUT = FEAT // N_HOR, FEAT // N_LEV
CHUNK, WINDOW, CHUNKS = 72, 80, 4
PIECE = CHUNKS * 2 * CHUNK
SENT = PIECE + CHUNK
LAST = 2 * CHUNK + 16
SHARE = 1 << 18
VMEM = pl.BlockSpec(memory_space=pltpu.VMEM)


def params(mib):
    return pltpu.CompilerParams(vmem_limit_bytes=mib << 20)


def cost(flops, moved):
    return pl.CostEstimate(flops=flops, bytes_accessed=moved, transcendentals=0)


def shift_lev(value, step_zlo, step_x):
    pairs = [(i, (i // N_X ^ step_zlo) * N_X + (i + step_x) % N_X) for i in range(N_LEV)]
    return lax.ppermute(value, "lev", pairs)


def swap_cores(value):
    return lax.ppermute(value, "hor", [(i, i ^ 1) for i in range(N_HOR)])


def hop(value, axis, cross):
    pairs = []
    for i in range(N_HOR):
        zhi, y, core = i // (2 * N_Y), i // 2 % N_Y, i % 2
        ahead = 1 - 2 * core
        if axis == "y":
            y = (y + ahead) % N_Y
        else:
            zhi = (zhi + ahead) % N_ZHI
        pairs.append((i, zhi * 2 * N_Y + y * 2 + (core ^ cross)))
    return lax.ppermute(value, "hor", pairs)


def repeat_kernel(index_ref, out_ref):
    for lev in range(N_LEV):
        out_ref[lev] = index_ref[...]


def stage_kernel(slab_ref, out_ref):
    for slot in range(SLOTS):
        out_ref[4 * slot : 4 * slot + 4, :] = slab_ref[slot]


def pick_kernel(index_ref, slab_ref, out_ref):
    for group in range(N_LEV):
        index = jnp.broadcast_to(index_ref[group], (8, LANES))
        lane, tile = index % LANES, index // LANES
        hits = [tile == t for t in range(GROUP // LANES)]
        for pair in range(2):
            rows = slice(8 * pair, 8 * pair + 8)
            total = jnp.zeros((8, LANES), jnp.float32)
            for t in range(GROUP // LANES):
                at = slice(group * GROUP + t * LANES, group * GROUP + (t + 1) * LANES)
                total = jnp.where(hits[t], jnp.take_along_axis(slab_ref[rows, at], lane, axis=1), total)
            out_ref[rows, group * SAMP : (group + 1) * SAMP] = total


def smooth_kernel(coef_ref, w0_ref, w1_ref, w2_ref, w3_ref, out_ref, raw_ref):
    x = lax.axis_index("lev") % N_X
    for step, ref in enumerate((w0_ref, w1_ref, w2_ref, w3_ref)):
        source = lax.rem(x - step + N_X, N_X)
        for zlo in range(N_ZLO):
            raw_ref[zlo * N_X + source] = ref[zlo]

    def tile(t, carry):
        at = pl.ds(pl.multiple_of(t * LANES, LANES), LANES)
        for slot in range(SLOTS):
            rows = [raw_ref[lev, 4 * slot : 4 * slot + 4, at] for lev in range(N_LEV)]
            value = jnp.concatenate(rows, axis=0)
            below, above = pltpu.roll(value, 1, 0), pltpu.roll(value, LEV - 1, 0)
            out_ref[slot * LEV : (slot + 1) * LEV, at] = (
                coef_ref[0:LEV] * value + coef_ref[LEV : 2 * LEV] * below + coef_ref[2 * LEV :] * above
            )
        return carry

    lax.fori_loop(0, BLOCK // LANES, tile, 0)


def feature_kernel(smooth_ref, feat_ref):
    def tile(t, carry):
        at = pl.ds(pl.multiple_of(t * LANES, LANES), LANES)
        early = smooth_ref[0 : 2 * LEV, at]
        feat_ref[0 : 2 * LEV, at] = smooth_ref[2 * LEV : 4 * LEV, at].astype(jnp.bfloat16)
        feat_ref[2 * LEV : 4 * LEV, at] = early.astype(jnp.bfloat16)
        first = early[0:LEV]
        for m in range(2 * LEV):
            row = jnp.broadcast_to(smooth_ref[pl.ds(2 * LEV + m, 1), at], (LEV, LANES))
            feat_ref[4 * LEV + m * LEV : 4 * LEV + (m + 1) * LEV, at] = (row * first).astype(jnp.bfloat16)
        return carry

    lax.fori_loop(0, BLOCK // LANES, tile, 0)


def gram_kernel(place, own_ref, other_ref, out_ref, left_ref, prod_ref):
    hor, lev = lax.axis_index("hor"), lax.axis_index("lev")
    zhi, y, core = hor // (2 * N_Y), hor // 2 % N_Y, hor % 2
    right = pl.ds(pl.multiple_of(lev * COLS_OUT, 16), COLS_OUT)
    to_y = {"far": y + 2, "cross": y + 5 - 2 * core, "near": y + 5 - 2 * core, "own": y}[place]
    to_y = lax.rem(to_y, N_Y)
    to_core = 1 - core if place == "cross" else core
    next_z = lax.rem(zhi + 5 - 2 * to_core, N_ZHI)
    chunks = ((zhi, to_core), (next_z, to_core), (next_z, 1 - to_core), (lax.rem(zhi + 2, N_ZHI), to_core))
    skip = 8 * lax.rem(to_y, 2)
    for block, ref in enumerate((own_ref, other_ref)):
        for chunk, (to_z, row_core) in enumerate(chunks):
            start = (to_z * N_Y + to_y) * 2 * ROWS_OUT + row_core * 64 - skip
            rows = pl.ds(pl.multiple_of(start, 16), WINDOW)
            left_ref[chunk * WINDOW : (chunk + 1) * WINDOW, :] = ref[rows, :]
        part = lax.dot_general(
            left_ref[...], ref[right, :], (((1,), (1,)), ((), ())), preferred_element_type=jnp.float32
        )
        prod_ref[...] = part + prod_ref[...] if block else part
    for chunk in range(CHUNKS):
        rows = pl.ds(pl.multiple_of(chunk * WINDOW + skip, 8), CHUNK)
        for half in range(2):
            base = (2 * chunk + half) * CHUNK
            out_ref[base : base + CHUNK, :] = prod_ref[rows, half * LANES : (half + 1) * LANES]
        out_ref[PIECE:SENT, 16 * chunk : 16 * chunk + 16] = prod_ref[rows, 2 * LANES : COLS_OUT]


def add_kernel(a_ref, b_ref, out_ref):
    out_ref[...] = a_ref[...] + b_ref[...]


def split_kernel(a_ref, b_ref, t0_ref, t1_ref, t2_ref, t3_ref):
    rest = a_ref[PIECE:SENT, :] + b_ref[PIECE:SENT, :]
    strip = lax.broadcasted_iota(jnp.int32, (8, LANES), 1) // 16
    for chunk, ref in enumerate((t0_ref, t1_ref, t2_ref, t3_ref)):
        rows = slice(chunk * 2 * CHUNK, (chunk + 1) * 2 * CHUNK)
        ref[0 : 2 * CHUNK, :] = a_ref[rows, :] + b_ref[rows, :]
        packed = jnp.zeros((8, LANES), jnp.float32)
        for group in range(8):
            moved = pltpu.roll(rest[8 * group : 8 * group + 8], 16 * (group - chunk) % LANES, 1)
            packed = jnp.where(strip == group, moved, packed)
        ref[2 * CHUNK : 2 * CHUNK + 8, :] = packed
        ref[2 * CHUNK + 8 : LAST, :] = pltpu.roll(rest[64:CHUNK], -16 * chunk % LANES, 1)


def final_kernel(t0_ref, t1_ref, t2_ref, out_ref):
    odd = lax.axis_index("hor") % 2 == 1
    scale = 1.0 / (BLOCK * N_HOR)

    def total(rows):
        return (t0_ref[rows, :] + t1_ref[rows, :]) + t2_ref[rows, :]

    def place(value):
        return jnp.where(odd, value[CHUNK - ROWS_OUT : CHUNK], value[0:ROWS_OUT]) * scale

    for half in range(2):
        value = total(slice(half * CHUNK, (half + 1) * CHUNK))
        out_ref[:, half * LANES : (half + 1) * LANES] = place(value)
    packed = total(slice(2 * CHUNK, 2 * CHUNK + 8))
    rest = [pltpu.roll(packed, -16 * group % LANES, 1) for group in range(8)]
    rest.append(total(slice(2 * CHUNK + 8, LAST)))
    out_ref[:, 2 * LANES :] = place(jnp.concatenate(rest, axis=0))[:, :16]


def filter_coefficients(thickness, level_cuts):
    link = 1.0 - level_cuts.astype(jnp.float32)
    zero_one = jnp.zeros((1,), jnp.float32)
    lower = jnp.concatenate([zero_one, thickness[:-1] * link])
    upper = jnp.concatenate([thickness[1:] * link, zero_one])
    denom = 2.0 * thickness + lower + upper
    coef = jnp.concatenate([2.0 * thickness / denom, lower / denom, upper / denom])
    return jnp.broadcast_to(coef[:, None], (3 * LEV, LANES))


def features(smoothed):
    return pl.pallas_call(
        feature_kernel,
        out_shape=jax.ShapeDtypeStruct((FEAT, BLOCK), jnp.bfloat16),
        in_specs=[VMEM],
        out_specs=VMEM,
        compiler_params=params(12),
        cost_estimate=cost(FEAT * BLOCK, 5 << 20),
        name="features",
    )(smoothed)


def add(a, b):
    return pl.pallas_call(
        add_kernel,
        out_shape=jax.ShapeDtypeStruct(a.shape, a.dtype),
        in_specs=[VMEM] * 2,
        out_specs=VMEM,
        compiler_params=params(4),
        cost_estimate=cost(1, SHARE),
        name="add",
    )(a, b)


def on_device(slab_fields, sample_index, thickness, level_cuts):
    f32 = jnp.float32
    coef = filter_coefficients(thickness, level_cuts)
    repeated = pl.pallas_call(
        repeat_kernel,
        out_shape=jax.ShapeDtypeStruct((N_LEV, 1, SAMP), jnp.int32),
        in_specs=[VMEM],
        out_specs=VMEM,
        compiler_params=params(1),
        name="repeat",
    )(sample_index)
    lists = lax.all_to_all(repeated, "lev", 0, 0, tiled=True)
    staged = pl.pallas_call(
        stage_kernel,
        out_shape=jax.ShapeDtypeStruct((4 * SLOTS, N_LEV * GROUP), f32),
        in_specs=[VMEM],
        out_specs=VMEM,
        compiler_params=params(8),
        cost_estimate=cost(0, 2 << 20),
        name="stage",
    )(slab_fields)
    picked = pl.pallas_call(
        pick_kernel,
        out_shape=jax.ShapeDtypeStruct((4 * SLOTS, BLOCK), f32),
        in_specs=[VMEM] * 2,
        out_specs=VMEM,
        compiler_params=params(8),
        name="pick",
    )(lists, staged)
    across = shift_lev(picked, 1, 0)
    up = lax.axis_index("lev") // N_X == 1
    near = jnp.stack([jnp.where(up, across, picked), jnp.where(up, picked, across)])
    far = {k: shift_lev(near, 0, k) for k in (2, 1, 3)}
    own = pl.pallas_call(
        smooth_kernel,
        out_shape=jax.ShapeDtypeStruct((SLOTS * LEV, BLOCK), f32),
        in_specs=[VMEM] * 5,
        out_specs=VMEM,
        scratch_shapes=[pltpu.VMEM((N_LEV, 4 * SLOTS, BLOCK), f32)],
        compiler_params=params(16),
        name="smooth",
    )(coef, near, far[1], far[2], far[3])
    other = swap_cores(own)
    feats = [features(own), features(other)]
    parts = {}
    for k in ("far", "cross", "near", "own"):
        parts[k] = pl.pallas_call(
            functools.partial(gram_kernel, k),
            out_shape=jax.ShapeDtypeStruct((SENT, LANES), f32),
            in_specs=[VMEM] * 2,
            out_specs=VMEM,
            scratch_shapes=[
                pltpu.VMEM((CHUNKS * WINDOW, BLOCK), jnp.bfloat16),
                pltpu.VMEM((CHUNKS * WINDOW, COLS_OUT), f32),
            ],
            compiler_params=params(16),
            cost_estimate=cost(1, SHARE),
            name="gram",
        )(*feats)
        if k == "cross":
            feats, parts[k] = lax.optimization_barrier((feats, parts[k]))
    two_back = hop(parts["far"], "y", 0)
    from_cross = hop(parts["cross"], "y", 1)
    from_near = hop(add(parts["near"], two_back), "y", 0)
    sums = pl.pallas_call(
        split_kernel,
        out_shape=[jax.ShapeDtypeStruct((LAST, LANES), f32)] * CHUNKS,
        in_specs=[VMEM] * 2,
        out_specs=[VMEM] * CHUNKS,
        compiler_params=params(8),
        cost_estimate=cost(1, SHARE),
        name="split",
    )(add(parts["own"], from_cross), from_near)
    two_back = hop(sums[3], "z_hi", 0)
    from_cross = hop(sums[2], "z_hi", 1)
    from_near = hop(add(sums[1], two_back), "z_hi", 0)
    return pl.pallas_call(
        final_kernel,
        out_shape=jax.ShapeDtypeStruct((ROWS_OUT, COLS_OUT), f32),
        in_specs=[VMEM] * 3,
        out_specs=VMEM,
        compiler_params=params(8),
        cost_estimate=cost(1, SHARE),
        name="final",
    )(sums[0], from_cross, from_near)


def solution(mesh):
    in_specs = (P(None, "lev", "hor"), P("hor", "lev"), P(), P())
    out_specs = P("hor", "lev")
    return jax.shard_map(on_device, mesh=mesh, in_specs=in_specs, out_specs=out_specs, check_vma=False)
```

```python
import functools

import jax
import jax.numpy as jnp
from jax import lax
from jax.experimental import pallas as pl
from jax.experimental.pallas import tpu as pltpu
from jax.sharding import PartitionSpec as P

LEV, SLOTS, LANES = 32, 4, 128
N_X, N_ZLO, N_Y, N_ZHI = 4, 2, 4, 4
N_LEV, N_HOR = N_X * N_ZLO, N_ZHI * N_Y * 2
GROUP, SAMP = 2048, 128
BLOCK = N_LEV * SAMP
FEAT = 4 * LEV + 2 * LEV * LEV
ROWS_OUT, COLS_OUT = FEAT // N_HOR, FEAT // N_LEV
CHUNK, WINDOW, CHUNKS = 72, 80, 4
PIECE = CHUNKS * 2 * CHUNK
SENT = PIECE + CHUNK
LAST = 2 * CHUNK + 16
SHARE = 1 << 18
VMEM = pl.BlockSpec(memory_space=pltpu.VMEM)


def params(mib):
    return pltpu.CompilerParams(vmem_limit_bytes=mib << 20)


def cost(flops, moved):
    return pl.CostEstimate(flops=flops, bytes_accessed=moved, transcendentals=0)


def shift_lev(value, step_zlo, step_x):
    pairs = [(i, (i // N_X ^ step_zlo) * N_X + (i + step_x) % N_X) for i in range(N_LEV)]
    return lax.ppermute(value, "lev", pairs)


def swap_cores(value):
    return lax.ppermute(value, "hor", [(i, i ^ 1) for i in range(N_HOR)])


def hop(value, axis, cross):
    pairs = []
    for i in range(N_HOR):
        zhi, y, core = i // (2 * N_Y), i // 2 % N_Y, i % 2
        ahead = 1 - 2 * core
        if axis == "y":
            y = (y + ahead) % N_Y
        else:
            zhi = (zhi + ahead) % N_ZHI
        pairs.append((i, zhi * 2 * N_Y + y * 2 + (core ^ cross)))
    return lax.ppermute(value, "hor", pairs)


def repeat_kernel(index_ref, out_ref, sems):
    copies = [pltpu.make_async_copy(index_ref, out_ref.at[lev], sems.at[lev]) for lev in range(N_LEV)]
    for copy in copies:
        copy.start()
    for copy in copies:
        copy.wait()


def stage_kernel(slab_ref, out_ref):
    for slot in range(SLOTS):
        out_ref[4 * slot : 4 * slot + 4, :] = slab_ref[slot]


def pick_kernel(index_ref, slab_ref, out_ref):
    for group in range(N_LEV):
        index = jnp.broadcast_to(index_ref[group], (8, LANES))
        lane, tile = index % LANES, index // LANES
        hits = [tile == t for t in range(GROUP // LANES)]
        for pair in range(2):
            rows = slice(8 * pair, 8 * pair + 8)
            total = jnp.zeros((8, LANES), jnp.float32)
            for t in range(GROUP // LANES):
                at = slice(group * GROUP + t * LANES, group * GROUP + (t + 1) * LANES)
                total = jnp.where(hits[t], jnp.take_along_axis(slab_ref[rows, at], lane, axis=1), total)
            out_ref[rows, group * SAMP : (group + 1) * SAMP] = total


def smooth_kernel(coef_ref, w0_ref, w1_ref, w2_ref, w3_ref, out_ref, raw_ref):
    x = lax.axis_index("lev") % N_X
    for step, ref in enumerate((w0_ref, w1_ref, w2_ref, w3_ref)):
        source = lax.rem(x - step + N_X, N_X)
        for zlo in range(N_ZLO):
            raw_ref[zlo * N_X + source] = ref[zlo]

    def tile(t, carry):
        at = pl.ds(pl.multiple_of(t * LANES, LANES), LANES)
        for slot in range(SLOTS):
            rows = [raw_ref[lev, 4 * slot : 4 * slot + 4, at] for lev in range(N_LEV)]
            value = jnp.concatenate(rows, axis=0)
            below, above = pltpu.roll(value, 1, 0), pltpu.roll(value, LEV - 1, 0)
            out_ref[slot * LEV : (slot + 1) * LEV, at] = (
                coef_ref[0:LEV] * value + coef_ref[LEV : 2 * LEV] * below + coef_ref[2 * LEV :] * above
            )
        return carry

    lax.fori_loop(0, BLOCK // LANES, tile, 0)


def feature_kernel(smooth_ref, feat_ref):
    def tile(t, carry):
        at = pl.ds(pl.multiple_of(t * LANES, LANES), LANES)
        early = smooth_ref[0 : 2 * LEV, at]
        feat_ref[0 : 2 * LEV, at] = smooth_ref[2 * LEV : 4 * LEV, at].astype(jnp.bfloat16)
        feat_ref[2 * LEV : 4 * LEV, at] = early.astype(jnp.bfloat16)
        first = early[0:LEV]
        for m in range(2 * LEV):
            row = jnp.broadcast_to(smooth_ref[pl.ds(2 * LEV + m, 1), at], (LEV, LANES))
            feat_ref[4 * LEV + m * LEV : 4 * LEV + (m + 1) * LEV, at] = (row * first).astype(jnp.bfloat16)
        return carry

    lax.fori_loop(0, BLOCK // LANES, tile, 0)


def gram_kernel(place, own_ref, other_ref, out_ref, left_ref, prod_ref):
    hor, lev = lax.axis_index("hor"), lax.axis_index("lev")
    zhi, y, core = hor // (2 * N_Y), hor // 2 % N_Y, hor % 2
    right = pl.ds(pl.multiple_of(lev * COLS_OUT, 16), COLS_OUT)
    to_y = {"far": y + 2, "cross": y + 5 - 2 * core, "near": y + 5 - 2 * core, "own": y}[place]
    to_y = lax.rem(to_y, N_Y)
    to_core = 1 - core if place == "cross" else core
    next_z = lax.rem(zhi + 5 - 2 * to_core, N_ZHI)
    chunks = ((zhi, to_core), (next_z, to_core), (next_z, 1 - to_core), (lax.rem(zhi + 2, N_ZHI), to_core))
    skip = 8 * lax.rem(to_y, 2)
    for block, ref in enumerate((own_ref, other_ref)):
        for chunk, (to_z, row_core) in enumerate(chunks):
            start = (to_z * N_Y + to_y) * 2 * ROWS_OUT + row_core * 64 - skip
            rows = pl.ds(pl.multiple_of(start, 16), WINDOW)
            left_ref[chunk * WINDOW : (chunk + 1) * WINDOW, :] = ref[rows, :]
        part = lax.dot_general(
            left_ref[...], ref[right, :], (((1,), (1,)), ((), ())), preferred_element_type=jnp.float32
        )
        prod_ref[...] = part + prod_ref[...] if block else part
    for chunk in range(CHUNKS):
        rows = pl.ds(pl.multiple_of(chunk * WINDOW + skip, 8), CHUNK)
        for half in range(2):
            base = (2 * chunk + half) * CHUNK
            out_ref[base : base + CHUNK, :] = prod_ref[rows, half * LANES : (half + 1) * LANES]
        out_ref[PIECE:SENT, 16 * chunk : 16 * chunk + 16] = prod_ref[rows, 2 * LANES : COLS_OUT]


def add_kernel(a_ref, b_ref, out_ref):
    out_ref[...] = a_ref[...] + b_ref[...]


def split_kernel(a_ref, b_ref, own_ref, next_ref, far_ref):
    rest = a_ref[PIECE:SENT, :] + b_ref[PIECE:SENT, :]
    strip = lax.broadcasted_iota(jnp.int32, (8, LANES), 1) // 16
    places = ((own_ref, 0), (next_ref, 0), (next_ref, LAST), (far_ref, 0))
    for chunk, (ref, base) in enumerate(places):
        rows = slice(chunk * 2 * CHUNK, (chunk + 1) * 2 * CHUNK)
        ref[base : base + 2 * CHUNK, :] = a_ref[rows, :] + b_ref[rows, :]
        packed = jnp.zeros((8, LANES), jnp.float32)
        for group in range(8):
            moved = pltpu.roll(rest[8 * group : 8 * group + 8], 16 * (group - chunk) % LANES, 1)
            packed = jnp.where(strip == group, moved, packed)
        ref[base + 2 * CHUNK : base + 2 * CHUNK + 8, :] = packed
        ref[base + 2 * CHUNK + 8 : base + LAST, :] = pltpu.roll(rest[64:CHUNK], -16 * chunk % LANES, 1)


def final_kernel(own_ref, next_ref, swapped_ref, far_ref, out_ref):
    odd = lax.axis_index("hor") % 2 == 1
    scale = 1.0 / (BLOCK * N_HOR)

    def total(rows):
        return (own_ref[rows, :] + next_ref[rows, :]) + (swapped_ref[rows, :] + far_ref[rows, :])

    def place(value):
        return jnp.where(odd, value[CHUNK - ROWS_OUT : CHUNK], value[0:ROWS_OUT]) * scale

    for half in range(2):
        value = total(slice(half * CHUNK, (half + 1) * CHUNK))
        out_ref[:, half * LANES : (half + 1) * LANES] = place(value)
    packed = total(slice(2 * CHUNK, 2 * CHUNK + 8))
    rest = [pltpu.roll(packed, -16 * group % LANES, 1) for group in range(8)]
    rest.append(total(slice(2 * CHUNK + 8, LAST)))
    out_ref[:, 2 * LANES :] = place(jnp.concatenate(rest, axis=0))[:, :16]


def filter_coefficients(thickness, level_cuts):
    link = 1.0 - level_cuts.astype(jnp.float32)
    zero_one = jnp.zeros((1,), jnp.float32)
    lower = jnp.concatenate([zero_one, thickness[:-1] * link])
    upper = jnp.concatenate([thickness[1:] * link, zero_one])
    denom = 2.0 * thickness + lower + upper
    coef = jnp.concatenate([2.0 * thickness / denom, lower / denom, upper / denom])
    return jnp.broadcast_to(coef[:, None], (3 * LEV, LANES))


def features(smoothed):
    return pl.pallas_call(
        feature_kernel,
        out_shape=jax.ShapeDtypeStruct((FEAT, BLOCK), jnp.bfloat16),
        in_specs=[VMEM],
        out_specs=VMEM,
        compiler_params=params(12),
        cost_estimate=cost(FEAT * BLOCK, 5 << 20),
        name="features",
    )(smoothed)


def add(a, b):
    return pl.pallas_call(
        add_kernel,
        out_shape=jax.ShapeDtypeStruct(a.shape, a.dtype),
        in_specs=[VMEM] * 2,
        out_specs=VMEM,
        compiler_params=params(4),
        cost_estimate=cost(1, SHARE),
        name="add",
    )(a, b)


def on_device(slab_fields, sample_index, thickness, level_cuts):
    f32 = jnp.float32
    coef = filter_coefficients(thickness, level_cuts)
    repeated = pl.pallas_call(
        repeat_kernel,
        out_shape=jax.ShapeDtypeStruct((N_LEV, 1, SAMP), jnp.int32),
        in_specs=[pl.BlockSpec(memory_space=pltpu.HBM)],
        out_specs=pl.BlockSpec(memory_space=pl.ANY),
        scratch_shapes=[pltpu.SemaphoreType.DMA((N_LEV,))],
        compiler_params=params(60),
        name="repeat",
    )(sample_index)
    lists = lax.all_to_all(repeated, "lev", 0, 0, tiled=True)
    staged = pl.pallas_call(
        stage_kernel,
        out_shape=jax.ShapeDtypeStruct((4 * SLOTS, N_LEV * GROUP), f32),
        in_specs=[VMEM],
        out_specs=VMEM,
        compiler_params=params(8),
        cost_estimate=cost(0, 2 << 20),
        name="stage",
    )(slab_fields)
    picked = pl.pallas_call(
        pick_kernel,
        out_shape=jax.ShapeDtypeStruct((4 * SLOTS, BLOCK), f32),
        in_specs=[VMEM] * 2,
        out_specs=VMEM,
        compiler_params=params(8),
        name="pick",
    )(lists, staged)
    across = shift_lev(picked, 1, 0)
    up = lax.axis_index("lev") // N_X == 1
    near = jnp.stack([jnp.where(up, across, picked), jnp.where(up, picked, across)])
    far = {k: shift_lev(near, 0, k) for k in (2, 1, 3)}
    own = pl.pallas_call(
        smooth_kernel,
        out_shape=jax.ShapeDtypeStruct((SLOTS * LEV, BLOCK), f32),
        in_specs=[VMEM] * 5,
        out_specs=VMEM,
        scratch_shapes=[pltpu.VMEM((N_LEV, 4 * SLOTS, BLOCK), f32)],
        compiler_params=params(16),
        name="smooth",
    )(coef, near, far[1], far[2], far[3])
    other = swap_cores(own)
    feats = [features(own), features(other)]
    parts = {}
    for k in ("far", "cross", "near", "own"):
        parts[k] = pl.pallas_call(
            functools.partial(gram_kernel, k),
            out_shape=jax.ShapeDtypeStruct((SENT, LANES), f32),
            in_specs=[VMEM] * 2,
            out_specs=VMEM,
            scratch_shapes=[
                pltpu.VMEM((CHUNKS * WINDOW, BLOCK), jnp.bfloat16),
                pltpu.VMEM((CHUNKS * WINDOW, COLS_OUT), f32),
            ],
            compiler_params=params(16),
            cost_estimate=cost(1, SHARE),
            name="gram",
        )(*feats)
        if k == "cross":
            feats, parts[k] = lax.optimization_barrier((feats, parts[k]))
    two_back = hop(parts["far"], "y", 0)
    from_cross = hop(parts["cross"], "y", 1)
    from_near = hop(add(parts["near"], two_back), "y", 0)
    chunk = jax.ShapeDtypeStruct((LAST, LANES), f32)
    kept, beside, beyond = pl.pallas_call(
        split_kernel,
        out_shape=[chunk, jax.ShapeDtypeStruct((2 * LAST, LANES), f32), chunk],
        in_specs=[VMEM] * 2,
        out_specs=[VMEM] * 3,
        compiler_params=params(8),
        cost_estimate=cost(1, SHARE),
        name="split",
    )(add(parts["own"], from_cross), from_near)
    from_next = hop(beside, "z_hi", 0)
    from_far = lax.ppermute(beyond, "hor", [(i, (i + N_HOR // 2) % N_HOR) for i in range(N_HOR)])
    swapped = swap_cores(from_next[LAST:])
    return pl.pallas_call(
        final_kernel,
        out_shape=jax.ShapeDtypeStruct((ROWS_OUT, COLS_OUT), f32),
        in_specs=[VMEM] * 4,
        out_specs=VMEM,
        compiler_params=params(8),
        cost_estimate=cost(1, SHARE),
        name="final",
    )(kept, from_next, swapped, from_far)


def solution(mesh):
    in_specs = (P(None, "lev", "hor"), P("hor", "lev"), P(), P())
    out_specs = P("hor", "lev")
    return jax.shard_map(on_device, mesh=mesh, in_specs=in_specs, out_specs=out_specs, check_vma=False)
```

```python
import functools

import jax
import jax.numpy as jnp
from jax import lax
from jax.experimental import pallas as pl
from jax.experimental.pallas import tpu as pltpu
from jax.sharding import PartitionSpec as P

LEV, SLOTS, LANES = 32, 4, 128
N_X, N_ZLO, N_Y, N_ZHI = 4, 2, 4, 4
N_LEV, N_HOR = N_X * N_ZLO, N_ZHI * N_Y * 2
GROUP, SAMP = 2048, 128
BLOCK = N_LEV * SAMP
FEAT = 4 * LEV + 2 * LEV * LEV
ROWS_OUT, COLS_OUT = FEAT // N_HOR, FEAT // N_LEV
CHUNK, BOTH, HALF = 72, 2 * ROWS_OUT, 16
WINDOWS = (CHUNK, BOTH, CHUNK)
BUILT = sum(WINDOWS) + 8 * len(WINDOWS)
MAIN = 2 * sum(WINDOWS)
SENT = MAIN + 40
LAST = 2 * CHUNK + 16
SHARE = 1 << 18
VMEM = pl.BlockSpec(memory_space=pltpu.VMEM)


def params(mib):
    return pltpu.CompilerParams(vmem_limit_bytes=mib << 20)


def cost(flops, moved):
    return pl.CostEstimate(flops=flops, bytes_accessed=moved, transcendentals=0)


def shift_lev(value, step_zlo, step_x):
    pairs = [(i, (i // N_X ^ step_zlo) * N_X + (i + step_x) % N_X) for i in range(N_LEV)]
    return lax.ppermute(value, "lev", pairs)


def swap_cores(value):
    return lax.ppermute(value, "hor", [(i, i ^ 1) for i in range(N_HOR)])


def hop(value, axis, cross):
    pairs = []
    for i in range(N_HOR):
        zhi, y, core = i // (2 * N_Y), i // 2 % N_Y, i % 2
        ahead = 1 - 2 * core
        if axis == "y":
            y = (y + ahead) % N_Y
        else:
            zhi = (zhi + ahead) % N_ZHI
        pairs.append((i, zhi * 2 * N_Y + y * 2 + (core ^ cross)))
    return lax.ppermute(value, "hor", pairs)


def repeat_kernel(index_ref, out_ref):
    for lev in range(N_LEV):
        out_ref[lev] = index_ref[...]


def stage_kernel(slab_ref, out_ref):
    for slot in range(SLOTS):
        out_ref[4 * slot : 4 * slot + 4, :] = slab_ref[slot]


def pick_kernel(index_ref, slab_ref, out_ref):
    for group in range(N_LEV):
        index = jnp.broadcast_to(index_ref[group], (8, LANES))
        lane, tile = index % LANES, index // LANES
        hits = [tile == t for t in range(GROUP // LANES)]
        for pair in range(2):
            rows = slice(8 * pair, 8 * pair + 8)
            total = jnp.zeros((8, LANES), jnp.float32)
            for t in range(GROUP // LANES):
                at = slice(group * GROUP + t * LANES, group * GROUP + (t + 1) * LANES)
                total = jnp.where(hits[t], jnp.take_along_axis(slab_ref[rows, at], lane, axis=1), total)
            out_ref[rows, group * SAMP : (group + 1) * SAMP] = total


def smooth_kernel(coef_ref, w0_ref, w1_ref, w2_ref, w3_ref, out_ref, raw_ref):
    x = lax.axis_index("lev") % N_X
    for step, ref in enumerate((w0_ref, w1_ref, w2_ref, w3_ref)):
        source = lax.rem(x - step + N_X, N_X)
        for zlo in range(N_ZLO):
            raw_ref[zlo * N_X + source] = ref[zlo]

    def tile(t, carry):
        at = pl.ds(pl.multiple_of(t * LANES, LANES), LANES)
        for slot in range(SLOTS):
            rows = [raw_ref[lev, 4 * slot : 4 * slot + 4, at] for lev in range(N_LEV)]
            value = jnp.concatenate(rows, axis=0)
            below, above = pltpu.roll(value, 1, 0), pltpu.roll(value, LEV - 1, 0)
            out_ref[slot * LEV : (slot + 1) * LEV, at] = (
                coef_ref[0:LEV] * value + coef_ref[LEV : 2 * LEV] * below + coef_ref[2 * LEV :] * above
            )
        return carry

    lax.fori_loop(0, BLOCK // LANES, tile, 0)


def build_rows(smooth_ref, half, out_ref, at):
    late = 2 * LEV
    m = jnp.maximum(half - 4 * LEV // HALF, 0) // 2
    product = smooth_ref[pl.ds(late + m, 1), :] * smooth_ref[pl.ds(pl.multiple_of(half % 2 * HALF, HALF), HALF), :]
    linear = smooth_ref[pl.ds(pl.multiple_of((late + half * HALF) % (4 * LEV), HALF), HALF), :]
    rows = jnp.where(half < 4 * LEV // HALF, linear, product)
    out_ref[at : at + HALF, :] = rows.astype(jnp.bfloat16)


def right_kernel(smooth_ref, out_ref):
    lev = lax.axis_index("lev")
    for i in range(COLS_OUT // HALF):
        build_rows(smooth_ref, lev * (COLS_OUT // HALF) + i, out_ref, i * HALF)


def windows_of(place):
    hor = lax.axis_index("hor")
    zhi, y, core = hor // (2 * N_Y), hor // 2 % N_Y, hor % 2
    to_y = {"far": y + 2, "cross": y + 5 - 2 * core, "near": y + 5 - 2 * core, "own": y}[place]
    to_y = lax.rem(to_y, N_Y)
    to_core = 1 - core if place == "cross" else core
    skip = 8 * lax.rem(to_y, 2)

    def start(to_z, offset):
        return (lax.rem(to_z, N_ZHI) * N_Y + to_y) * BOTH + offset - skip

    return (start(zhi, 64 * to_core), start(zhi + 5 - 2 * to_core, 0), start(zhi + 2, 64 * to_core)), skip


def product(place, smooth_ref, right_ref, left_ref):
    at = 0
    for first, size in zip(windows_of(place)[0], WINDOWS):
        for i in range((size + 8) // HALF):
            build_rows(smooth_ref, first // HALF + i, left_ref, at)
            at += HALF
    return lax.dot_general(
        left_ref[...], right_ref[...], (((1,), (1,)), ((), ())), preferred_element_type=jnp.float32
    )


def emit(place, prod_ref, out_ref):
    skip = windows_of(place)[1]
    at, base, group = 0, 0, 0
    for size in WINDOWS:
        for half in range(2):
            rows = pl.ds(pl.multiple_of(at + skip, 8), size)
            out_ref[base : base + size, :] = prod_ref[rows, half * LANES : (half + 1) * LANES]
            base += size
        for i in range(size // 8):
            rows = pl.ds(pl.multiple_of(at + 8 * i + skip, 8), 8)
            to = MAIN + 8 * (group // 8)
            strip = 16 * (group % 8)
            out_ref[to : to + 8, strip : strip + 16] = prod_ref[rows, 2 * LANES : COLS_OUT]
            group += 1
        at += size + 8


def begin_kernel(place, smooth_ref, right_ref, out_ref, left_ref):
    out_ref[...] = product(place, smooth_ref, right_ref, left_ref)


def finish_kernel(place, part_ref, smooth_ref, right_ref, out_ref, left_ref, prod_ref):
    prod_ref[...] = part_ref[...] + product(place, smooth_ref, right_ref, left_ref)
    emit(place, prod_ref, out_ref)


def gram_kernel(place, own_ref, own_right_ref, other_ref, other_right_ref, out_ref, left_ref, prod_ref):
    prod_ref[...] = product(place, own_ref, own_right_ref, left_ref)
    prod_ref[...] += product(place, other_ref, other_right_ref, left_ref)
    emit(place, prod_ref, out_ref)


def add_kernel(a_ref, b_ref, out_ref):
    out_ref[...] = a_ref[...] + b_ref[...]


def split_kernel(a_ref, b_ref, own_ref, near_ref, cross_ref, far_ref):
    core = lax.axis_index("hor") % 2
    lane = lax.broadcasted_iota(jnp.int32, (8, LANES), 1)

    def total(start, size):
        rows = pl.ds(start if isinstance(start, int) else pl.multiple_of(start, 8), size)
        return a_ref[rows, :] + b_ref[rows, :]

    ahead = 2 * CHUNK
    places = (
        (own_ref, 0, CHUNK, 0, 0),
        (near_ref, ahead + 64 * core, BOTH, 1 + core, 1),
        (cross_ref, ahead + 64 * (1 - core), BOTH, 2 - core, 1),
        (far_ref, ahead + 2 * BOTH, CHUNK, 3, 2),
    )
    for ref, start, stride, tile, strip in places:
        ref[0:CHUNK, :] = total(start, CHUNK)
        ref[CHUNK : 2 * CHUNK, :] = total(start + stride, CHUNK)
        one, two = total(MAIN + 8 * tile, 8), total(MAIN + 8 * tile + 8, 8)
        if strip:
            one, two = pltpu.roll(one, LANES - 16 * strip, 1), pltpu.roll(two, LANES - 16 * strip, 1)
            one = jnp.where(lane < LANES - 16 * strip, one, two)
        ref[2 * CHUNK : 2 * CHUNK + 8, :] = one
        ref[2 * CHUNK + 8 : LAST, :] = two


def final_kernel(t0_ref, t1_ref, t2_ref, out_ref):
    odd = lax.axis_index("hor") % 2 == 1
    scale = 1.0 / (BLOCK * N_HOR)

    def total(rows):
        return (t0_ref[rows, :] + t1_ref[rows, :]) + t2_ref[rows, :]

    def place(value):
        return jnp.where(odd, value[CHUNK - ROWS_OUT : CHUNK], value[0:ROWS_OUT]) * scale

    for half in range(2):
        value = total(slice(half * CHUNK, (half + 1) * CHUNK))
        out_ref[:, half * LANES : (half + 1) * LANES] = place(value)
    packed = total(slice(2 * CHUNK, 2 * CHUNK + 8))
    rest = [pltpu.roll(packed, -16 * group % LANES, 1) for group in range(8)]
    rest.append(total(slice(2 * CHUNK + 8, LAST)))
    out_ref[:, 2 * LANES :] = place(jnp.concatenate(rest, axis=0))[:, :16]


def filter_coefficients(thickness, level_cuts):
    link = 1.0 - level_cuts.astype(jnp.float32)
    zero_one = jnp.zeros((1,), jnp.float32)
    lower = jnp.concatenate([zero_one, thickness[:-1] * link])
    upper = jnp.concatenate([thickness[1:] * link, zero_one])
    denom = 2.0 * thickness + lower + upper
    coef = jnp.concatenate([2.0 * thickness / denom, lower / denom, upper / denom])
    return jnp.broadcast_to(coef[:, None], (3 * LEV, LANES))


def right_of(smoothed):
    return pl.pallas_call(
        right_kernel,
        out_shape=jax.ShapeDtypeStruct((COLS_OUT, BLOCK), jnp.bfloat16),
        in_specs=[VMEM],
        out_specs=VMEM,
        compiler_params=params(4),
        cost_estimate=cost(1, SHARE),
        name="right",
    )(smoothed)


def gram(kernel, place, out_shape, *operands):
    scratch = [pltpu.VMEM((BUILT, BLOCK), jnp.bfloat16), pltpu.VMEM((BUILT, COLS_OUT), jnp.float32)]
    return pl.pallas_call(
        functools.partial(kernel, place),
        out_shape=jax.ShapeDtypeStruct(out_shape, jnp.float32),
        in_specs=[VMEM] * len(operands),
        out_specs=VMEM,
        scratch_shapes=scratch[:1] if kernel is begin_kernel else scratch,
        compiler_params=params(12),
        cost_estimate=cost(1, SHARE),
        name="gram_" + place,
    )(*operands)


def add(a, b):
    return pl.pallas_call(
        add_kernel,
        out_shape=jax.ShapeDtypeStruct(a.shape, a.dtype),
        in_specs=[VMEM] * 2,
        out_specs=VMEM,
        compiler_params=params(4),
        cost_estimate=cost(1, SHARE),
        name="add",
    )(a, b)


def on_device(slab_fields, sample_index, thickness, level_cuts):
    f32 = jnp.float32
    coef = filter_coefficients(thickness, level_cuts)
    repeated = pl.pallas_call(
        repeat_kernel,
        out_shape=jax.ShapeDtypeStruct((N_LEV, 1, SAMP), jnp.int32),
        in_specs=[VMEM],
        out_specs=VMEM,
        compiler_params=params(1),
        name="repeat",
    )(sample_index)
    lists = lax.all_to_all(repeated, "lev", 0, 0, tiled=True)
    staged = pl.pallas_call(
        stage_kernel,
        out_shape=jax.ShapeDtypeStruct((4 * SLOTS, N_LEV * GROUP), f32),
        in_specs=[VMEM],
        out_specs=VMEM,
        compiler_params=params(8),
        cost_estimate=cost(0, 2 << 20),
        name="stage",
    )(slab_fields)
    picked = pl.pallas_call(
        pick_kernel,
        out_shape=jax.ShapeDtypeStruct((4 * SLOTS, BLOCK), f32),
        in_specs=[VMEM] * 2,
        out_specs=VMEM,
        compiler_params=params(8),
        name="pick",
    )(lists, staged)
    across = shift_lev(picked, 1, 0)
    up = lax.axis_index("lev") // N_X == 1
    near = jnp.stack([jnp.where(up, across, picked), jnp.where(up, picked, across)])
    far = {k: shift_lev(near, 0, k) for k in (2, 1, 3)}
    own = pl.pallas_call(
        smooth_kernel,
        out_shape=jax.ShapeDtypeStruct((SLOTS * LEV, BLOCK), f32),
        in_specs=[VMEM] * 5,
        out_specs=VMEM,
        scratch_shapes=[pltpu.VMEM((N_LEV, 4 * SLOTS, BLOCK), f32)],
        compiler_params=params(16),
        name="smooth",
    )(coef, near, far[1], far[2], far[3])
    other = swap_cores(own)
    own_right = right_of(own)
    begun = gram(begin_kernel, "far", (BUILT, COLS_OUT), own, own_right)
    other_right = right_of(other)
    sent = (SENT, LANES)
    parts = {"far": gram(finish_kernel, "far", sent, begun, other, other_right)}
    both = (own, own_right, other, other_right)
    parts["cross"] = gram(gram_kernel, "cross", sent, *both)
    both, parts["cross"] = lax.optimization_barrier((both, parts["cross"]))
    parts["near"] = gram(gram_kernel, "near", sent, *both)
    parts["own"] = gram(gram_kernel, "own", sent, *both)
    two_back = hop(parts["far"], "y", 0)
    from_cross = hop(parts["cross"], "y", 1)
    from_near = hop(add(parts["near"], two_back), "y", 0)
    kept, near, cross, far = pl.pallas_call(
        split_kernel,
        out_shape=[jax.ShapeDtypeStruct((LAST, LANES), f32)] * 4,
        in_specs=[VMEM] * 2,
        out_specs=[VMEM] * 4,
        compiler_params=params(8),
        cost_estimate=cost(1, SHARE),
        name="split",
    )(add(parts["own"], from_cross), from_near)
    two_back = hop(far, "z_hi", 0)
    from_cross = hop(cross, "z_hi", 1)
    from_near = hop(add(near, two_back), "z_hi", 0)
    return pl.pallas_call(
        final_kernel,
        out_shape=jax.ShapeDtypeStruct((ROWS_OUT, COLS_OUT), f32),
        in_specs=[VMEM] * 3,
        out_specs=VMEM,
        compiler_params=params(8),
        cost_estimate=cost(1, SHARE),
        name="final",
    )(kept, from_cross, from_near)


def solution(mesh):
    in_specs = (P(None, "lev", "hor"), P("hor", "lev"), P(), P())
    out_specs = P("hor", "lev")
    return jax.shard_map(on_device, mesh=mesh, in_specs=in_specs, out_specs=out_specs, check_vma=False)
```

```python
import functools

import jax
import jax.numpy as jnp
from jax import lax
from jax.experimental import pallas as pl
from jax.experimental.pallas import tpu as pltpu
from jax.sharding import PartitionSpec as P

LEV, SLOTS, LANES = 32, 4, 128
N_X, N_ZLO, N_Y, N_ZHI = 4, 2, 4, 4
N_LEV, N_HOR = N_X * N_ZLO, N_ZHI * N_Y * 2
GROUP, SAMP = 2048, 128
BLOCK = N_LEV * SAMP
FEAT = 4 * LEV + 2 * LEV * LEV
ROWS_OUT, COLS_OUT = FEAT // N_HOR, FEAT // N_LEV
CHUNK, BOTH, HALF = 72, 2 * ROWS_OUT, 16
WINDOWS = (CHUNK, CHUNK, BOTH)
BUILT = sum(WINDOWS) + 8 * len(WINDOWS)
LAST = 2 * CHUNK + 16
REST = 2 * (CHUNK + BOTH)
SENT = LAST + REST + 32
SHARE = 1 << 18
VMEM = pl.BlockSpec(memory_space=pltpu.VMEM)


def params(mib):
    return pltpu.CompilerParams(vmem_limit_bytes=mib << 20)


def cost(flops, moved):
    return pl.CostEstimate(flops=flops, bytes_accessed=moved, transcendentals=0)


def shift_lev(value, step_zlo, step_x):
    pairs = [(i, (i // N_X ^ step_zlo) * N_X + (i + step_x) % N_X) for i in range(N_LEV)]
    return lax.ppermute(value, "lev", pairs)


def swap_cores(value):
    return lax.ppermute(value, "hor", [(i, i ^ 1) for i in range(N_HOR)])


def hop(value, axis, cross):
    pairs = []
    for i in range(N_HOR):
        zhi, y, core = i // (2 * N_Y), i // 2 % N_Y, i % 2
        ahead = 1 - 2 * core
        if axis == "y":
            y = (y + ahead) % N_Y
        else:
            zhi = (zhi + ahead) % N_ZHI
        pairs.append((i, zhi * 2 * N_Y + y * 2 + (core ^ cross)))
    return lax.ppermute(value, "hor", pairs)


def repeat_kernel(index_ref, out_ref):
    for lev in range(N_LEV):
        out_ref[lev] = index_ref[...]


def stage_kernel(slab_ref, out_ref):
    for slot in range(SLOTS):
        out_ref[4 * slot : 4 * slot + 4, :] = slab_ref[slot]


def pick_kernel(index_ref, slab_ref, out_ref):
    for group in range(N_LEV):
        index = jnp.broadcast_to(index_ref[group], (8, LANES))
        lane, tile = index % LANES, index // LANES
        hits = [tile == t for t in range(GROUP // LANES)]
        for pair in range(2):
            rows = slice(8 * pair, 8 * pair + 8)
            total = jnp.zeros((8, LANES), jnp.float32)
            for t in range(GROUP // LANES):
                at = slice(group * GROUP + t * LANES, group * GROUP + (t + 1) * LANES)
                total = jnp.where(hits[t], jnp.take_along_axis(slab_ref[rows, at], lane, axis=1), total)
            out_ref[rows, group * SAMP : (group + 1) * SAMP] = total


def smooth_kernel(coef_ref, w0_ref, w1_ref, w2_ref, w3_ref, out_ref, raw_ref):
    x = lax.axis_index("lev") % N_X
    for step, ref in enumerate((w0_ref, w1_ref, w2_ref, w3_ref)):
        source = lax.rem(x - step + N_X, N_X)
        for zlo in range(N_ZLO):
            raw_ref[zlo * N_X + source] = ref[zlo]

    def tile(t, carry):
        at = pl.ds(pl.multiple_of(t * LANES, LANES), LANES)
        for slot in range(SLOTS):
            rows = [raw_ref[lev, 4 * slot : 4 * slot + 4, at] for lev in range(N_LEV)]
            value = jnp.concatenate(rows, axis=0)
            below, above = pltpu.roll(value, 1, 0), pltpu.roll(value, LEV - 1, 0)
            out_ref[slot * LEV : (slot + 1) * LEV, at] = (
                coef_ref[0:LEV] * value + coef_ref[LEV : 2 * LEV] * below + coef_ref[2 * LEV :] * above
            )
        return carry

    lax.fori_loop(0, BLOCK // LANES, tile, 0)


def build_rows(smooth_ref, half, out_ref, at):
    late = 2 * LEV
    m = jnp.maximum(half - 4 * LEV // HALF, 0) // 2
    product = smooth_ref[pl.ds(late + m, 1), :] * smooth_ref[pl.ds(pl.multiple_of(half % 2 * HALF, HALF), HALF), :]
    linear = smooth_ref[pl.ds(pl.multiple_of((late + half * HALF) % (4 * LEV), HALF), HALF), :]
    rows = jnp.where(half < 4 * LEV // HALF, linear, product)
    out_ref[at : at + HALF, :] = rows.astype(jnp.bfloat16)


def right_kernel(smooth_ref, out_ref):
    lev = lax.axis_index("lev")
    for i in range(COLS_OUT // HALF):
        build_rows(smooth_ref, lev * (COLS_OUT // HALF) + i, out_ref, i * HALF)


def windows_of(place):
    hor = lax.axis_index("hor")
    zhi, y, core = hor // (2 * N_Y), hor // 2 % N_Y, hor % 2
    to_y = {"far": y + 2, "cross": y + 5 - 2 * core, "near": y + 5 - 2 * core, "own": y}[place]
    to_y = lax.rem(to_y, N_Y)
    to_core = 1 - core if place == "cross" else core
    skip = 8 * lax.rem(to_y, 2)

    def start(to_z, offset):
        return (lax.rem(to_z, N_ZHI) * N_Y + to_y) * BOTH + offset - skip

    return (start(zhi + 2, 64 * to_core), start(zhi, 64 * to_core), start(zhi + 5 - 2 * to_core, 0)), skip


def product(place, smooth_ref, right_ref, left_ref):
    at = 0
    for first, size in zip(windows_of(place)[0], WINDOWS):
        for i in range((size + 8) // HALF):
            build_rows(smooth_ref, first // HALF + i, left_ref, at)
            at += HALF
    return lax.dot_general(
        left_ref[...], right_ref[...], (((1,), (1,)), ((), ())), preferred_element_type=jnp.float32
    )


def emit(place, prod_ref, out_ref):
    skip = windows_of(place)[1]
    at, base, group, tail = 0, 0, 0, 2 * CHUNK
    for number, size in enumerate(WINDOWS):
        if number == 1:
            base, group, tail = LAST, 0, LAST + REST
        for half in range(2):
            rows = pl.ds(pl.multiple_of(at + skip, 8), size)
            out_ref[base : base + size, :] = prod_ref[rows, half * LANES : (half + 1) * LANES]
            base += size
        for i in range(size // 8):
            rows = pl.ds(pl.multiple_of(at + 8 * i + skip, 8), 8)
            to = tail + 8 * (group // 8)
            strip = 16 * (group % 8)
            out_ref[to : to + 8, strip : strip + 16] = prod_ref[rows, 2 * LANES : COLS_OUT]
            group += 1
        at += size + 8


def begin_kernel(place, smooth_ref, right_ref, out_ref, left_ref):
    out_ref[...] = product(place, smooth_ref, right_ref, left_ref)


def finish_kernel(place, part_ref, smooth_ref, right_ref, out_ref, left_ref, prod_ref):
    prod_ref[...] = part_ref[...] + product(place, smooth_ref, right_ref, left_ref)
    emit(place, prod_ref, out_ref)


def gram_kernel(place, own_ref, own_right_ref, other_ref, other_right_ref, out_ref, left_ref, prod_ref):
    prod_ref[...] = product(place, own_ref, own_right_ref, left_ref)
    prod_ref[...] += product(place, other_ref, other_right_ref, left_ref)
    emit(place, prod_ref, out_ref)


def add_kernel(a_ref, b_ref, out_ref):
    out_ref[...] = a_ref[...] + b_ref[...]


def cut_kernel(a_ref, b_ref, far_ref, rest_ref):
    far_ref[...] = a_ref[0:LAST, :] + b_ref[0:LAST, :]
    rest_ref[...] = a_ref[LAST:SENT, :] + b_ref[LAST:SENT, :]


def split_kernel(a_ref, b_ref, own_ref, near_ref, cross_ref):
    core = lax.axis_index("hor") % 2
    lane = lax.broadcasted_iota(jnp.int32, (8, LANES), 1)

    def total(start, size):
        rows = pl.ds(start if isinstance(start, int) else pl.multiple_of(start, 8), size)
        return a_ref[rows, :] + b_ref[rows, :]

    ahead = 2 * CHUNK
    places = (
        (near_ref, ahead + 64 * core, BOTH, 1 + core, 1),
        (cross_ref, ahead + 64 * (1 - core), BOTH, 2 - core, 1),
        (own_ref, 0, CHUNK, 0, 0),
    )
    for ref, start, stride, tile, strip in places:
        ref[0:CHUNK, :] = total(start, CHUNK)
        ref[CHUNK : 2 * CHUNK, :] = total(start + stride, CHUNK)
        one, two = total(REST + 8 * tile, 8), total(REST + 8 * tile + 8, 8)
        if strip:
            one, two = pltpu.roll(one, LANES - 16 * strip, 1), pltpu.roll(two, LANES - 16 * strip, 1)
            one = jnp.where(lane < LANES - 16 * strip, one, two)
        ref[2 * CHUNK : 2 * CHUNK + 8, :] = one
        ref[2 * CHUNK + 8 : LAST, :] = two


def final_kernel(t0_ref, t1_ref, t2_ref, out_ref):
    odd = lax.axis_index("hor") % 2 == 1
    scale = 1.0 / (BLOCK * N_HOR)

    def total(rows):
        return (t0_ref[rows, :] + t1_ref[rows, :]) + t2_ref[rows, :]

    def place(value):
        return jnp.where(odd, value[CHUNK - ROWS_OUT : CHUNK], value[0:ROWS_OUT]) * scale

    for half in range(2):
        value = total(slice(half * CHUNK, (half + 1) * CHUNK))
        out_ref[:, half * LANES : (half + 1) * LANES] = place(value)
    packed = total(slice(2 * CHUNK, 2 * CHUNK + 8))
    rest = [pltpu.roll(packed, -16 * group % LANES, 1) for group in range(8)]
    rest.append(total(slice(2 * CHUNK + 8, LAST)))
    out_ref[:, 2 * LANES :] = place(jnp.concatenate(rest, axis=0))[:, :16]


def filter_coefficients(thickness, level_cuts):
    link = 1.0 - level_cuts.astype(jnp.float32)
    zero_one = jnp.zeros((1,), jnp.float32)
    lower = jnp.concatenate([zero_one, thickness[:-1] * link])
    upper = jnp.concatenate([thickness[1:] * link, zero_one])
    denom = 2.0 * thickness + lower + upper
    coef = jnp.concatenate([2.0 * thickness / denom, lower / denom, upper / denom])
    return jnp.broadcast_to(coef[:, None], (3 * LEV, LANES))


def right_of(smoothed):
    return pl.pallas_call(
        right_kernel,
        out_shape=jax.ShapeDtypeStruct((COLS_OUT, BLOCK), jnp.bfloat16),
        in_specs=[VMEM],
        out_specs=VMEM,
        compiler_params=params(4),
        cost_estimate=cost(1, SHARE),
        name="right",
    )(smoothed)


def gram(kernel, place, out_shape, *operands):
    scratch = [pltpu.VMEM((BUILT, BLOCK), jnp.bfloat16), pltpu.VMEM((BUILT, COLS_OUT), jnp.float32)]
    return pl.pallas_call(
        functools.partial(kernel, place),
        out_shape=jax.ShapeDtypeStruct(out_shape, jnp.float32),
        in_specs=[VMEM] * len(operands),
        out_specs=VMEM,
        scratch_shapes=scratch[:1] if kernel is begin_kernel else scratch,
        compiler_params=params(12),
        cost_estimate=cost(1, SHARE),
        name="gram_" + place,
    )(*operands)


def add(a, b, share=1):
    return pl.pallas_call(
        add_kernel,
        out_shape=jax.ShapeDtypeStruct(a.shape, a.dtype),
        in_specs=[VMEM] * 2,
        out_specs=VMEM,
        compiler_params=params(4),
        cost_estimate=cost(share, SHARE),
        name="add",
    )(a, b)


def cut(a, b):
    shapes = ((LAST, LANES), (SENT - LAST, LANES))
    return pl.pallas_call(
        cut_kernel,
        out_shape=[jax.ShapeDtypeStruct(shape, a.dtype) for shape in shapes],
        in_specs=[VMEM] * 2,
        out_specs=[VMEM] * 2,
        compiler_params=params(4),
        cost_estimate=cost(1, SHARE),
        name="cut",
    )(a, b)


def on_device(slab_fields, sample_index, thickness, level_cuts):
    f32 = jnp.float32
    coef = filter_coefficients(thickness, level_cuts)
    repeated = pl.pallas_call(
        repeat_kernel,
        out_shape=jax.ShapeDtypeStruct((N_LEV, 1, SAMP), jnp.int32),
        in_specs=[VMEM],
        out_specs=VMEM,
        compiler_params=params(1),
        name="repeat",
    )(sample_index)
    lists = lax.all_to_all(repeated, "lev", 0, 0, tiled=True)
    staged = pl.pallas_call(
        stage_kernel,
        out_shape=jax.ShapeDtypeStruct((4 * SLOTS, N_LEV * GROUP), f32),
        in_specs=[VMEM],
        out_specs=VMEM,
        compiler_params=params(8),
        cost_estimate=cost(0, 2 << 20),
        name="stage",
    )(slab_fields)
    picked = pl.pallas_call(
        pick_kernel,
        out_shape=jax.ShapeDtypeStruct((4 * SLOTS, BLOCK), f32),
        in_specs=[VMEM] * 2,
        out_specs=VMEM,
        compiler_params=params(8),
        name="pick",
    )(lists, staged)
    across = shift_lev(picked, 1, 0)
    up = lax.axis_index("lev") // N_X == 1
    near = jnp.stack([jnp.where(up, across, picked), jnp.where(up, picked, across)])
    far = {k: shift_lev(near, 0, k) for k in (2, 1, 3)}
    own = pl.pallas_call(
        smooth_kernel,
        out_shape=jax.ShapeDtypeStruct((SLOTS * LEV, BLOCK), f32),
        in_specs=[VMEM] * 5,
        out_specs=VMEM,
        scratch_shapes=[pltpu.VMEM((N_LEV, 4 * SLOTS, BLOCK), f32)],
        compiler_params=params(16),
        name="smooth",
    )(coef, near, far[1], far[2], far[3])
    other = swap_cores(own)
    own_right = right_of(own)
    begun = gram(begin_kernel, "far", (BUILT, COLS_OUT), own, own_right)
    other_right = right_of(other)
    sent = (SENT, LANES)
    parts = {"far": gram(finish_kernel, "far", sent, begun, other, other_right)}
    both = (own, own_right, other, other_right)
    parts["cross"] = gram(gram_kernel, "cross", sent, *both)
    both, parts["cross"] = lax.optimization_barrier((both, parts["cross"]))
    parts["near"] = gram(gram_kernel, "near", sent, *both)
    parts["own"] = gram(gram_kernel, "own", sent, *both)
    two_back = hop(parts["far"], "y", 0)
    from_cross = hop(parts["cross"], "y", 1)
    near_far, near_rest = cut(parts["near"], two_back)
    from_near_far, from_near_rest = hop(near_far, "y", 0), hop(near_rest, "y", 0)
    sum_far, sum_rest = cut(parts["own"], from_cross)
    two_back = hop(add(sum_far, from_near_far, 1 << 30), "z_hi", 0)
    kept, near, cross = pl.pallas_call(
        split_kernel,
        out_shape=[jax.ShapeDtypeStruct((LAST, LANES), f32)] * 3,
        in_specs=[VMEM] * 2,
        out_specs=[VMEM] * 3,
        compiler_params=params(8),
        cost_estimate=cost(1, SHARE),
        name="split",
    )(sum_rest, from_near_rest)
    from_cross = hop(cross, "z_hi", 1)
    from_near = hop(add(near, two_back), "z_hi", 0)
    return pl.pallas_call(
        final_kernel,
        out_shape=jax.ShapeDtypeStruct((ROWS_OUT, COLS_OUT), f32),
        in_specs=[VMEM] * 3,
        out_specs=VMEM,
        compiler_params=params(8),
        cost_estimate=cost(1, SHARE),
        name="final",
    )(kept, from_cross, from_near)


def solution(mesh):
    in_specs = (P(None, "lev", "hor"), P("hor", "lev"), P(), P())
    out_specs = P("hor", "lev")
    return jax.shard_map(on_device, mesh=mesh, in_specs=in_specs, out_specs=out_specs, check_vma=False)
```

```python
import functools

import jax
import jax.numpy as jnp
from jax import lax
from jax.experimental import pallas as pl
from jax.experimental.pallas import tpu as pltpu
from jax.sharding import PartitionSpec as P

LEV, SLOTS, LANES = 32, 4, 128
N_X, N_ZLO, N_Y, N_ZHI = 4, 2, 4, 4
N_LEV, N_HOR = N_X * N_ZLO, N_ZHI * N_Y * 2
GROUP, SAMP = 2048, 128
BLOCK = N_LEV * SAMP
FEAT = 4 * LEV + 2 * LEV * LEV
ROWS_OUT, COLS_OUT = FEAT // N_HOR, FEAT // N_LEV
CHUNK, BOTH, HALF = 72, 2 * ROWS_OUT, 16
PLACES = ("far", "cross", "near", "own")
BUILT_A, BUILT_B = 4 * (CHUNK + 8), CHUNK + BOTH + 16
LAST = 2 * CHUNK + 16
REST = 2 * (CHUNK + BOTH)
SENT = REST + 32
SHARE = 1 << 18
VMEM = pl.BlockSpec(memory_space=pltpu.VMEM)


def params(mib):
    return pltpu.CompilerParams(vmem_limit_bytes=mib << 20)


def cost(flops, moved):
    return pl.CostEstimate(flops=flops, bytes_accessed=moved, transcendentals=0)


def shift_lev(value, step_zlo, step_x):
    pairs = [(i, (i // N_X ^ step_zlo) * N_X + (i + step_x) % N_X) for i in range(N_LEV)]
    return lax.ppermute(value, "lev", pairs)


def swap_cores(value):
    return lax.ppermute(value, "hor", [(i, i ^ 1) for i in range(N_HOR)])


def hop(value, axis, cross):
    pairs = []
    for i in range(N_HOR):
        zhi, y, core = i // (2 * N_Y), i // 2 % N_Y, i % 2
        ahead = 1 - 2 * core
        if axis == "y":
            y = (y + ahead) % N_Y
        else:
            zhi = (zhi + ahead) % N_ZHI
        pairs.append((i, zhi * 2 * N_Y + y * 2 + (core ^ cross)))
    return lax.ppermute(value, "hor", pairs)


def repeat_kernel(index_ref, out_ref):
    for lev in range(N_LEV):
        out_ref[lev] = index_ref[...]


def stage_kernel(slab_ref, out_ref):
    for slot in range(SLOTS):
        out_ref[4 * slot : 4 * slot + 4, :] = slab_ref[slot]


def pick_kernel(index_ref, slab_ref, out_ref):
    for group in range(N_LEV):
        index = jnp.broadcast_to(index_ref[group], (8, LANES))
        lane, tile = index % LANES, index // LANES
        hits = [tile == t for t in range(GROUP // LANES)]
        for pair in range(2):
            rows = slice(8 * pair, 8 * pair + 8)
            total = jnp.zeros((8, LANES), jnp.float32)
            for t in range(GROUP // LANES):
                at = slice(group * GROUP + t * LANES, group * GROUP + (t + 1) * LANES)
                total = jnp.where(hits[t], jnp.take_along_axis(slab_ref[rows, at], lane, axis=1), total)
            out_ref[rows, group * SAMP : (group + 1) * SAMP] = total


def smooth_kernel(coef_ref, w0_ref, w1_ref, w2_ref, w3_ref, out_ref, raw_ref):
    x = lax.axis_index("lev") % N_X
    for step, ref in enumerate((w0_ref, w1_ref, w2_ref, w3_ref)):
        source = lax.rem(x - step + N_X, N_X)
        for zlo in range(N_ZLO):
            raw_ref[zlo * N_X + source] = ref[zlo]

    def tile(t, carry):
        at = pl.ds(pl.multiple_of(t * LANES, LANES), LANES)
        for slot in range(SLOTS):
            rows = [raw_ref[lev, 4 * slot : 4 * slot + 4, at] for lev in range(N_LEV)]
            value = jnp.concatenate(rows, axis=0)
            below, above = pltpu.roll(value, 1, 0), pltpu.roll(value, LEV - 1, 0)
            out_ref[slot * LEV : (slot + 1) * LEV, at] = (
                coef_ref[0:LEV] * value + coef_ref[LEV : 2 * LEV] * below + coef_ref[2 * LEV :] * above
            )
        return carry

    lax.fori_loop(0, BLOCK // LANES, tile, 0)


def build_rows(smooth_ref, half, out_ref, at):
    late = 2 * LEV
    m = jnp.maximum(half - 4 * LEV // HALF, 0) // 2
    product = smooth_ref[pl.ds(late + m, 1), :] * smooth_ref[pl.ds(pl.multiple_of(half % 2 * HALF, HALF), HALF), :]
    linear = smooth_ref[pl.ds(pl.multiple_of((late + half * HALF) % (4 * LEV), HALF), HALF), :]
    rows = jnp.where(half < 4 * LEV // HALF, linear, product)
    out_ref[at : at + HALF, :] = rows.astype(jnp.bfloat16)


def right_kernel(smooth_ref, out_ref):
    lev = lax.axis_index("lev")
    for i in range(COLS_OUT // HALF):
        build_rows(smooth_ref, lev * (COLS_OUT // HALF) + i, out_ref, i * HALF)


def windows_of(place):
    hor = lax.axis_index("hor")
    zhi, y, core = hor // (2 * N_Y), hor // 2 % N_Y, hor % 2
    to_y = {"far": y + 2, "cross": y + 5 - 2 * core, "near": y + 5 - 2 * core, "own": y}[place]
    to_y = lax.rem(to_y, N_Y)
    to_core = 1 - core if place == "cross" else core
    skip = 8 * lax.rem(to_y, 2)

    def start(to_z, offset):
        return (lax.rem(to_z, N_ZHI) * N_Y + to_y) * BOTH + offset - skip

    return (start(zhi + 2, 64 * to_core), start(zhi, 64 * to_core), start(zhi + 5 - 2 * to_core, 0)), skip


def pieces_a():
    return [(windows_of(place)[0][0], CHUNK) for place in PLACES]


def pieces_b(place):
    return list(zip(windows_of(place)[0][1:], (CHUNK, BOTH)))


def product(pieces, smooth_ref, right_ref, left_ref):
    at = 0
    for first, size in pieces:
        for i in range((size + 8) // HALF):
            build_rows(smooth_ref, first // HALF + i, left_ref, at)
            at += HALF
    return lax.dot_general(
        left_ref[...], right_ref[...], (((1,), (1,)), ((), ())), preferred_element_type=jnp.float32
    )


def emit(sizes, at, skip, prod_ref, out_ref):
    base, group, tail = 0, 0, 2 * sum(sizes)
    for size in sizes:
        for half in range(2):
            rows = pl.ds(pl.multiple_of(at + skip, 8), size)
            out_ref[base : base + size, :] = prod_ref[rows, half * LANES : (half + 1) * LANES]
            base += size
        for i in range(size // 8):
            rows = pl.ds(pl.multiple_of(at + 8 * i + skip, 8), 8)
            to = tail + 8 * (group // 8)
            strip = 16 * (group % 8)
            out_ref[to : to + 8, strip : strip + 16] = prod_ref[rows, 2 * LANES : COLS_OUT]
            group += 1
        at += size + 8


def emit_a(prod_ref, out_refs):
    for number, (place, ref) in enumerate(zip(PLACES, out_refs)):
        emit((CHUNK,), number * (CHUNK + 8), windows_of(place)[1], prod_ref, ref)


def emit_b(place, prod_ref, out_ref):
    emit((CHUNK, BOTH), 0, windows_of(place)[1], prod_ref, out_ref)


def begin_kernel(place, smooth_ref, right_ref, out_ref, left_ref):
    out_ref[...] = product(pieces_b(place) if place else pieces_a(), smooth_ref, right_ref, left_ref)


def finish_a_kernel(place, part_ref, smooth_ref, right_ref, *refs):
    left_ref, prod_ref = refs[4:]
    prod_ref[...] = part_ref[...] + product(pieces_a(), smooth_ref, right_ref, left_ref)
    emit_a(prod_ref, refs[:4])


def finish_b_kernel(place, part_ref, smooth_ref, right_ref, out_ref, left_ref, prod_ref):
    prod_ref[...] = part_ref[...] + product(pieces_b(place), smooth_ref, right_ref, left_ref)
    emit_b(place, prod_ref, out_ref)


def gram_kernel(place, own_ref, own_right_ref, other_ref, other_right_ref, out_ref, left_ref, prod_ref):
    prod_ref[...] = product(pieces_b(place), own_ref, own_right_ref, left_ref)
    prod_ref[...] += product(pieces_b(place), other_ref, other_right_ref, left_ref)
    emit_b(place, prod_ref, out_ref)


def add_kernel(a_ref, b_ref, out_ref):
    out_ref[...] = a_ref[...] + b_ref[...]


def split_kernel(a_ref, b_ref, own_ref, near_ref, cross_ref):
    core = lax.axis_index("hor") % 2
    lane = lax.broadcasted_iota(jnp.int32, (8, LANES), 1)

    def total(start, size):
        rows = pl.ds(start if isinstance(start, int) else pl.multiple_of(start, 8), size)
        return a_ref[rows, :] + b_ref[rows, :]

    ahead = 2 * CHUNK
    places = (
        (near_ref, ahead + 64 * core, BOTH, 1 + core, 1),
        (cross_ref, ahead + 64 * (1 - core), BOTH, 2 - core, 1),
        (own_ref, 0, CHUNK, 0, 0),
    )
    for ref, start, stride, tile, strip in places:
        ref[0:CHUNK, :] = total(start, CHUNK)
        ref[CHUNK : 2 * CHUNK, :] = total(start + stride, CHUNK)
        one, two = total(REST + 8 * tile, 8), total(REST + 8 * tile + 8, 8)
        if strip:
            one, two = pltpu.roll(one, LANES - 16 * strip, 1), pltpu.roll(two, LANES - 16 * strip, 1)
            one = jnp.where(lane < LANES - 16 * strip, one, two)
        ref[2 * CHUNK : 2 * CHUNK + 8, :] = one
        ref[2 * CHUNK + 8 : LAST, :] = two


def final_kernel(t0_ref, t1_ref, t2_ref, out_ref):
    odd = lax.axis_index("hor") % 2 == 1
    scale = 1.0 / (BLOCK * N_HOR)

    def total(rows):
        return (t0_ref[rows, :] + t1_ref[rows, :]) + t2_ref[rows, :]

    def place(value):
        return jnp.where(odd, value[CHUNK - ROWS_OUT : CHUNK], value[0:ROWS_OUT]) * scale

    for half in range(2):
        value = total(slice(half * CHUNK, (half + 1) * CHUNK))
        out_ref[:, half * LANES : (half + 1) * LANES] = place(value)
    packed = total(slice(2 * CHUNK, 2 * CHUNK + 8))
    rest = [pltpu.roll(packed, -16 * group % LANES, 1) for group in range(8)]
    rest.append(total(slice(2 * CHUNK + 8, LAST)))
    out_ref[:, 2 * LANES :] = place(jnp.concatenate(rest, axis=0))[:, :16]


def filter_coefficients(thickness, level_cuts):
    link = 1.0 - level_cuts.astype(jnp.float32)
    zero_one = jnp.zeros((1,), jnp.float32)
    lower = jnp.concatenate([zero_one, thickness[:-1] * link])
    upper = jnp.concatenate([thickness[1:] * link, zero_one])
    denom = 2.0 * thickness + lower + upper
    coef = jnp.concatenate([2.0 * thickness / denom, lower / denom, upper / denom])
    return jnp.broadcast_to(coef[:, None], (3 * LEV, LANES))


def right_of(smoothed):
    return pl.pallas_call(
        right_kernel,
        out_shape=jax.ShapeDtypeStruct((COLS_OUT, BLOCK), jnp.bfloat16),
        in_specs=[VMEM],
        out_specs=VMEM,
        compiler_params=params(4),
        cost_estimate=cost(1, SHARE),
        name="right",
    )(smoothed)


def gram(kernel, place, out_shape, *operands):
    built = BUILT_B if place else BUILT_A
    scratch = [pltpu.VMEM((built, BLOCK), jnp.bfloat16), pltpu.VMEM((built, COLS_OUT), jnp.float32)]
    return pl.pallas_call(
        functools.partial(kernel, place),
        out_shape=out_shape,
        in_specs=[VMEM] * len(operands),
        out_specs=jax.tree.map(lambda _: VMEM, out_shape),
        scratch_shapes=scratch[:1] if kernel is begin_kernel else scratch,
        compiler_params=params(12),
        cost_estimate=cost(1, SHARE),
        name="gram_" + (place or "a"),
    )(*operands)


def add(a, b, share=1):
    return pl.pallas_call(
        add_kernel,
        out_shape=jax.ShapeDtypeStruct(a.shape, a.dtype),
        in_specs=[VMEM] * 2,
        out_specs=VMEM,
        compiler_params=params(4),
        cost_estimate=cost(share, SHARE),
        name="add",
    )(a, b)


def on_device(slab_fields, sample_index, thickness, level_cuts):
    f32 = jnp.float32
    coef = filter_coefficients(thickness, level_cuts)
    repeated = pl.pallas_call(
        repeat_kernel,
        out_shape=jax.ShapeDtypeStruct((N_LEV, 1, SAMP), jnp.int32),
        in_specs=[VMEM],
        out_specs=VMEM,
        compiler_params=params(1),
        name="repeat",
    )(sample_index)
    lists = lax.all_to_all(repeated, "lev", 0, 0, tiled=True)
    staged = pl.pallas_call(
        stage_kernel,
        out_shape=jax.ShapeDtypeStruct((4 * SLOTS, N_LEV * GROUP), f32),
        in_specs=[VMEM],
        out_specs=VMEM,
        compiler_params=params(8),
        cost_estimate=cost(0, 2 << 20),
        name="stage",
    )(slab_fields)
    picked = pl.pallas_call(
        pick_kernel,
        out_shape=jax.ShapeDtypeStruct((4 * SLOTS, BLOCK), f32),
        in_specs=[VMEM] * 2,
        out_specs=VMEM,
        compiler_params=params(8),
        name="pick",
    )(lists, staged)
    across = shift_lev(picked, 1, 0)
    up = lax.axis_index("lev") // N_X == 1
    near = jnp.stack([jnp.where(up, across, picked), jnp.where(up, picked, across)])
    far = {k: shift_lev(near, 0, k) for k in (2, 1, 3)}
    own = pl.pallas_call(
        smooth_kernel,
        out_shape=jax.ShapeDtypeStruct((SLOTS * LEV, BLOCK), f32),
        in_specs=[VMEM] * 5,
        out_specs=VMEM,
        scratch_shapes=[pltpu.VMEM((N_LEV, 4 * SLOTS, BLOCK), f32)],
        compiler_params=params(16),
        name="smooth",
    )(coef, near, far[1], far[2], far[3])
    other = swap_cores(own)
    def array(*shape):
        return jax.ShapeDtypeStruct(shape, f32)

    own_right = right_of(own)
    begun_a = gram(begin_kernel, None, array(BUILT_A, COLS_OUT), own, own_right)
    begun_a, own, own_right = lax.optimization_barrier((begun_a, own, own_right))
    begun_b = gram(begin_kernel, "far", array(BUILT_B, COLS_OUT), own, own_right)
    other_right = right_of(other)
    chunk, sent = array(LAST, LANES), array(SENT, LANES)
    far_a, cross_a, near_a, own_a = gram(finish_a_kernel, None, [chunk] * 4, begun_a, other, other_right)
    begun_b, far_a = lax.optimization_barrier((begun_b, far_a))
    far_b = gram(finish_b_kernel, "far", sent, begun_b, other, other_right)
    both = (own, own_right, other, other_right)
    cross_b = gram(gram_kernel, "cross", sent, *both)
    both, cross_b = lax.optimization_barrier((both, cross_b))
    near_b = gram(gram_kernel, "near", sent, *both)
    own_b = gram(gram_kernel, "own", sent, *both)

    two_back = hop(far_a, "y", 0)
    from_cross = hop(cross_a, "y", 1)
    from_near = hop(add(near_a, two_back, 1 << 31), "y", 0)
    two_back = hop(add(add(own_a, from_cross), from_near, 1 << 30), "z_hi", 0)
    two_back_b = hop(far_b, "y", 0)
    from_cross = hop(cross_b, "y", 1)
    from_near = hop(add(near_b, two_back_b), "y", 0)
    kept, near, cross = pl.pallas_call(
        split_kernel,
        out_shape=[chunk] * 3,
        in_specs=[VMEM] * 2,
        out_specs=[VMEM] * 3,
        compiler_params=params(8),
        cost_estimate=cost(1, SHARE),
        name="split",
    )(add(own_b, from_cross), from_near)
    from_cross = hop(cross, "z_hi", 1)
    from_near = hop(add(near, two_back), "z_hi", 0)
    return pl.pallas_call(
        final_kernel,
        out_shape=jax.ShapeDtypeStruct((ROWS_OUT, COLS_OUT), f32),
        in_specs=[VMEM] * 3,
        out_specs=VMEM,
        compiler_params=params(8),
        cost_estimate=cost(1, SHARE),
        name="final",
    )(kept, from_cross, from_near)


def solution(mesh):
    in_specs = (P(None, "lev", "hor"), P("hor", "lev"), P(), P())
    out_specs = P("hor", "lev")
    return jax.shard_map(on_device, mesh=mesh, in_specs=in_specs, out_specs=out_specs, check_vma=False)
```

```python
import functools

import jax
import jax.numpy as jnp
from jax import lax
from jax.experimental import pallas as pl
from jax.experimental.pallas import tpu as pltpu
from jax.sharding import PartitionSpec as P

LEV, SLOTS, LANES = 32, 4, 128
N_X, N_ZLO, N_Y, N_ZHI = 4, 2, 4, 4
N_LEV, N_HOR = N_X * N_ZLO, N_ZHI * N_Y * 2
GROUP, SAMP = 2048, 128
BLOCK = N_LEV * SAMP
FEAT = 4 * LEV + 2 * LEV * LEV
ROWS_OUT, COLS_OUT = FEAT // N_HOR, FEAT // N_LEV
CHUNK, BOTH, HALF = 72, 2 * ROWS_OUT, 16
WINDOWS = (CHUNK, CHUNK, BOTH)
BUILT = sum(WINDOWS) + 8 * len(WINDOWS)
LAST = 2 * CHUNK + 16
REST = 2 * (CHUNK + BOTH)
SENT = LAST + REST + 32
SHARE = 1 << 18
VMEM = pl.BlockSpec(memory_space=pltpu.VMEM)


def params(mib):
    return pltpu.CompilerParams(vmem_limit_bytes=mib << 20)


def cost(flops, moved):
    return pl.CostEstimate(flops=flops, bytes_accessed=moved, transcendentals=0)


def shift_lev(value, step_zlo, step_x):
    pairs = [(i, (i // N_X ^ step_zlo) * N_X + (i + step_x) % N_X) for i in range(N_LEV)]
    return lax.ppermute(value, "lev", pairs)


def swap_cores(value):
    return lax.ppermute(value, "hor", [(i, i ^ 1) for i in range(N_HOR)])


def hop(value, axis, cross):
    pairs = []
    for i in range(N_HOR):
        zhi, y, core = i // (2 * N_Y), i // 2 % N_Y, i % 2
        ahead = 1 - 2 * core
        if axis == "y":
            y = (y + ahead) % N_Y
        else:
            zhi = (zhi + ahead) % N_ZHI
        pairs.append((i, zhi * 2 * N_Y + y * 2 + (core ^ cross)))
    return lax.ppermute(value, "hor", pairs)


def repeat_kernel(index_ref, out_ref):
    for lev in range(N_LEV):
        out_ref[lev] = index_ref[...]


def stage_kernel(slab_ref, out_ref):
    for slot in range(SLOTS):
        out_ref[4 * slot : 4 * slot + 4, :] = slab_ref[slot]


def pick_kernel(index_ref, slab_ref, out_ref):
    for group in range(N_LEV):
        index = jnp.broadcast_to(index_ref[group], (8, LANES))
        lane, tile = index % LANES, index // LANES
        hits = [tile == t for t in range(GROUP // LANES)]
        for pair in range(2):
            rows = slice(8 * pair, 8 * pair + 8)
            total = jnp.zeros((8, LANES), jnp.float32)
            for t in range(GROUP // LANES):
                at = slice(group * GROUP + t * LANES, group * GROUP + (t + 1) * LANES)
                total = jnp.where(hits[t], jnp.take_along_axis(slab_ref[rows, at], lane, axis=1), total)
            out_ref[rows, group * SAMP : (group + 1) * SAMP] = total


def smooth_kernel(coef_ref, w0_ref, w1_ref, w2_ref, w3_ref, out_ref, raw_ref):
    x = lax.axis_index("lev") % N_X
    for step, ref in enumerate((w0_ref, w1_ref, w2_ref, w3_ref)):
        source = lax.rem(x - step + N_X, N_X)
        for zlo in range(N_ZLO):
            raw_ref[zlo * N_X + source] = ref[zlo]

    def tile(t, carry):
        at = pl.ds(pl.multiple_of(t * LANES, LANES), LANES)
        for slot in range(SLOTS):
            rows = [raw_ref[lev, 4 * slot : 4 * slot + 4, at] for lev in range(N_LEV)]
            value = jnp.concatenate(rows, axis=0)
            below, above = pltpu.roll(value, 1, 0), pltpu.roll(value, LEV - 1, 0)
            out_ref[slot * LEV : (slot + 1) * LEV, at] = (
                coef_ref[0:LEV] * value + coef_ref[LEV : 2 * LEV] * below + coef_ref[2 * LEV :] * above
            )
        return carry

    lax.fori_loop(0, BLOCK // LANES, tile, 0)


def build_rows(smooth_ref, half, out_ref, at):
    late = 2 * LEV
    m = jnp.maximum(half - 4 * LEV // HALF, 0) // 2
    product = smooth_ref[pl.ds(late + m, 1), :] * smooth_ref[pl.ds(pl.multiple_of(half % 2 * HALF, HALF), HALF), :]
    linear = smooth_ref[pl.ds(pl.multiple_of((late + half * HALF) % (4 * LEV), HALF), HALF), :]
    rows = jnp.where(half < 4 * LEV // HALF, linear, product)
    out_ref[at : at + HALF, :] = rows.astype(jnp.bfloat16)


def right_kernel(smooth_ref, out_ref):
    lev = lax.axis_index("lev")
    for i in range(COLS_OUT // HALF):
        build_rows(smooth_ref, lev * (COLS_OUT // HALF) + i, out_ref, i * HALF)


def windows_of(place):
    hor = lax.axis_index("hor")
    zhi, y, core = hor // (2 * N_Y), hor // 2 % N_Y, hor % 2
    to_y = {"far": y + 2, "cross": y + 5 - 2 * core, "near": y + 5 - 2 * core, "own": y}[place]
    to_y = lax.rem(to_y, N_Y)
    to_core = 1 - core if place == "cross" else core
    skip = 8 * lax.rem(to_y, 2)

    def start(to_z, offset):
        return (lax.rem(to_z, N_ZHI) * N_Y + to_y) * BOTH + offset - skip

    return (start(zhi + 2, 64 * to_core), start(zhi, 64 * to_core), start(zhi + 5 - 2 * to_core, 0)), skip


def product(place, smooth_ref, right_ref, left_ref):
    at = 0
    for first, size in zip(windows_of(place)[0], WINDOWS):
        for i in range((size + 8) // HALF):
            build_rows(smooth_ref, first // HALF + i, left_ref, at)
            at += HALF
    return lax.dot_general(
        left_ref[...], right_ref[...], (((1,), (1,)), ((), ())), preferred_element_type=jnp.float32
    )


def emit(place, prod_ref, out_ref):
    skip = windows_of(place)[1]
    at, base, group, tail = 0, 0, 0, 2 * CHUNK
    for number, size in enumerate(WINDOWS):
        if number == 1:
            base, group, tail = LAST, 0, LAST + REST
        for half in range(2):
            rows = pl.ds(pl.multiple_of(at + skip, 8), size)
            out_ref[base : base + size, :] = prod_ref[rows, half * LANES : (half + 1) * LANES]
            base += size
        for i in range(size // 8):
            rows = pl.ds(pl.multiple_of(at + 8 * i + skip, 8), 8)
            to = tail + 8 * (group // 8)
            strip = 16 * (group % 8)
            out_ref[to : to + 8, strip : strip + 16] = prod_ref[rows, 2 * LANES : COLS_OUT]
            group += 1
        at += size + 8


def begin_kernel(place, smooth_ref, right_ref, out_ref, left_ref):
    out_ref[...] = product(place, smooth_ref, right_ref, left_ref)


def finish_kernel(place, part_ref, smooth_ref, right_ref, out_ref, left_ref, prod_ref):
    prod_ref[...] = part_ref[...] + product(place, smooth_ref, right_ref, left_ref)
    emit(place, prod_ref, out_ref)


def gram_kernel(place, own_ref, own_right_ref, other_ref, other_right_ref, out_ref, left_ref, prod_ref):
    prod_ref[...] = product(place, own_ref, own_right_ref, left_ref)
    prod_ref[...] += product(place, other_ref, other_right_ref, left_ref)
    emit(place, prod_ref, out_ref)


def add_kernel(a_ref, b_ref, out_ref):
    out_ref[...] = a_ref[...] + b_ref[...]


def cut_kernel(a_ref, b_ref, far_ref, rest_ref):
    far_ref[...] = a_ref[0:LAST, :] + b_ref[0:LAST, :]
    rest_ref[...] = a_ref[LAST:SENT, :] + b_ref[LAST:SENT, :]


def split_kernel(a_ref, b_ref, own_ref, near_ref, cross_ref):
    core = lax.axis_index("hor") % 2
    lane = lax.broadcasted_iota(jnp.int32, (8, LANES), 1)

    def total(start, size):
        rows = pl.ds(start if isinstance(start, int) else pl.multiple_of(start, 8), size)
        return a_ref[rows, :] + b_ref[rows, :]

    ahead = 2 * CHUNK
    places = (
        (near_ref, ahead + 64 * core, BOTH, 1 + core, 1),
        (cross_ref, ahead + 64 * (1 - core), BOTH, 2 - core, 1),
        (own_ref, 0, CHUNK, 0, 0),
    )
    for ref, start, stride, tile, strip in places:
        ref[0:CHUNK, :] = total(start, CHUNK)
        ref[CHUNK : 2 * CHUNK, :] = total(start + stride, CHUNK)
        one, two = total(REST + 8 * tile, 8), total(REST + 8 * tile + 8, 8)
        if strip:
            one, two = pltpu.roll(one, LANES - 16 * strip, 1), pltpu.roll(two, LANES - 16 * strip, 1)
            one = jnp.where(lane < LANES - 16 * strip, one, two)
        ref[2 * CHUNK : 2 * CHUNK + 8, :] = one
        ref[2 * CHUNK + 8 : LAST, :] = two


def final_kernel(kept_ref, near_ref, out_ref):
    odd = lax.axis_index("hor") % 2 == 1
    scale = 1.0 / (BLOCK * N_HOR)

    def total(rows):
        return kept_ref[rows, :] + near_ref[rows, :]

    def place(value):
        return jnp.where(odd, value[CHUNK - ROWS_OUT : CHUNK], value[0:ROWS_OUT]) * scale

    for half in range(2):
        value = total(slice(half * CHUNK, (half + 1) * CHUNK))
        out_ref[:, half * LANES : (half + 1) * LANES] = place(value)
    packed = total(slice(2 * CHUNK, 2 * CHUNK + 8))
    rest = [pltpu.roll(packed, -16 * group % LANES, 1) for group in range(8)]
    rest.append(total(slice(2 * CHUNK + 8, LAST)))
    out_ref[:, 2 * LANES :] = place(jnp.concatenate(rest, axis=0))[:, :16]


def filter_coefficients(thickness, level_cuts):
    link = 1.0 - level_cuts.astype(jnp.float32)
    zero_one = jnp.zeros((1,), jnp.float32)
    lower = jnp.concatenate([zero_one, thickness[:-1] * link])
    upper = jnp.concatenate([thickness[1:] * link, zero_one])
    denom = 2.0 * thickness + lower + upper
    coef = jnp.concatenate([2.0 * thickness / denom, lower / denom, upper / denom])
    return jnp.broadcast_to(coef[:, None], (3 * LEV, LANES))


def right_of(smoothed):
    return pl.pallas_call(
        right_kernel,
        out_shape=jax.ShapeDtypeStruct((COLS_OUT, BLOCK), jnp.bfloat16),
        in_specs=[VMEM],
        out_specs=VMEM,
        compiler_params=params(4),
        cost_estimate=cost(1, SHARE),
        name="right",
    )(smoothed)


def gram(kernel, place, out_shape, *operands):
    scratch = [pltpu.VMEM((BUILT, BLOCK), jnp.bfloat16), pltpu.VMEM((BUILT, COLS_OUT), jnp.float32)]
    return pl.pallas_call(
        functools.partial(kernel, place),
        out_shape=jax.ShapeDtypeStruct(out_shape, jnp.float32),
        in_specs=[VMEM] * len(operands),
        out_specs=VMEM,
        scratch_shapes=scratch[:1] if kernel is begin_kernel else scratch,
        compiler_params=params(12),
        cost_estimate=cost(1, SHARE),
        name="gram_" + place,
    )(*operands)


def add(a, b, share=1):
    return pl.pallas_call(
        add_kernel,
        out_shape=jax.ShapeDtypeStruct(a.shape, a.dtype),
        in_specs=[VMEM] * 2,
        out_specs=VMEM,
        compiler_params=params(4),
        cost_estimate=cost(share, SHARE),
        name="add",
    )(a, b)


def cut(a, b):
    shapes = ((LAST, LANES), (SENT - LAST, LANES))
    return pl.pallas_call(
        cut_kernel,
        out_shape=[jax.ShapeDtypeStruct(shape, a.dtype) for shape in shapes],
        in_specs=[VMEM] * 2,
        out_specs=[VMEM] * 2,
        compiler_params=params(4),
        cost_estimate=cost(1, SHARE),
        name="cut",
    )(a, b)


def on_device(slab_fields, sample_index, thickness, level_cuts):
    f32 = jnp.float32
    coef = filter_coefficients(thickness, level_cuts)
    repeated = pl.pallas_call(
        repeat_kernel,
        out_shape=jax.ShapeDtypeStruct((N_LEV, 1, SAMP), jnp.int32),
        in_specs=[VMEM],
        out_specs=VMEM,
        compiler_params=params(1),
        name="repeat",
    )(sample_index)
    lists = lax.all_to_all(repeated, "lev", 0, 0, tiled=True)
    staged = pl.pallas_call(
        stage_kernel,
        out_shape=jax.ShapeDtypeStruct((4 * SLOTS, N_LEV * GROUP), f32),
        in_specs=[VMEM],
        out_specs=VMEM,
        compiler_params=params(8),
        cost_estimate=cost(0, 2 << 20),
        name="stage",
    )(slab_fields)
    picked = pl.pallas_call(
        pick_kernel,
        out_shape=jax.ShapeDtypeStruct((4 * SLOTS, BLOCK), f32),
        in_specs=[VMEM] * 2,
        out_specs=VMEM,
        compiler_params=params(8),
        name="pick",
    )(lists, staged)
    across = shift_lev(picked, 1, 0)
    up = lax.axis_index("lev") // N_X == 1
    near = jnp.stack([jnp.where(up, across, picked), jnp.where(up, picked, across)])
    far = {k: shift_lev(near, 0, k) for k in (2, 1, 3)}
    own = pl.pallas_call(
        smooth_kernel,
        out_shape=jax.ShapeDtypeStruct((SLOTS * LEV, BLOCK), f32),
        in_specs=[VMEM] * 5,
        out_specs=VMEM,
        scratch_shapes=[pltpu.VMEM((N_LEV, 4 * SLOTS, BLOCK), f32)],
        compiler_params=params(16),
        name="smooth",
    )(coef, near, far[1], far[2], far[3])
    other = swap_cores(own)
    own_right = right_of(own)
    begun = gram(begin_kernel, "far", (BUILT, COLS_OUT), own, own_right)
    other_right = right_of(other)
    sent = (SENT, LANES)
    parts = {"far": gram(finish_kernel, "far", sent, begun, other, other_right)}
    both = (own, own_right, other, other_right)
    parts["cross"] = gram(gram_kernel, "cross", sent, *both)
    both, parts["cross"] = lax.optimization_barrier((both, parts["cross"]))
    parts["near"] = gram(gram_kernel, "near", sent, *both)
    parts["own"] = gram(gram_kernel, "own", sent, *both)
    two_back = hop(parts["far"], "y", 0)
    from_cross = hop(parts["cross"], "y", 1)
    parts["near"], parts["own"] = lax.optimization_barrier((parts["near"], parts["own"]))
    near_far, near_rest = cut(parts["near"], two_back)
    from_near_far, from_near_rest = hop(near_far, "y", 0), hop(near_rest, "y", 0)
    sum_far, sum_rest = cut(parts["own"], from_cross)
    two_back = hop(add(sum_far, from_near_far, 1 << 30), "z_hi", 0)
    kept, near, cross = pl.pallas_call(
        split_kernel,
        out_shape=[jax.ShapeDtypeStruct((LAST, LANES), f32)] * 3,
        in_specs=[VMEM] * 2,
        out_specs=[VMEM] * 3,
        compiler_params=params(8),
        cost_estimate=cost(1, SHARE),
        name="split",
    )(sum_rest, from_near_rest)
    from_cross = hop(cross, "z_hi", 1)
    kept = add(kept, from_cross)
    from_near = hop(add(near, two_back), "z_hi", 0)
    return pl.pallas_call(
        final_kernel,
        out_shape=jax.ShapeDtypeStruct((ROWS_OUT, COLS_OUT), f32),
        in_specs=[VMEM] * 2,
        out_specs=VMEM,
        compiler_params=params(8),
        cost_estimate=cost(1, SHARE),
        name="final",
    )(kept, from_near)


def solution(mesh):
    in_specs = (P(None, "lev", "hor"), P("hor", "lev"), P(), P())
    out_specs = P("hor", "lev")
    return jax.shard_map(on_device, mesh=mesh, in_specs=in_specs, out_specs=out_specs, check_vma=False)
```

```python
import functools

import jax
import jax.numpy as jnp
from jax import lax
from jax.experimental import pallas as pl
from jax.experimental.pallas import tpu as pltpu
from jax.sharding import PartitionSpec as P

LEV, SLOTS, LANES = 32, 4, 128
N_X, N_ZLO, N_Y, N_ZHI = 4, 2, 4, 4
N_LEV, N_HOR = N_X * N_ZLO, N_ZHI * N_Y * 2
GROUP, SAMP = 2048, 128
BLOCK = N_LEV * SAMP
FEAT = 4 * LEV + 2 * LEV * LEV
ROWS_OUT, COLS_OUT = FEAT // N_HOR, FEAT // N_LEV
CHUNK, BOTH, HALF = 72, 2 * ROWS_OUT, 16
WINDOWS = (CHUNK, CHUNK, BOTH)
BUILT = sum(WINDOWS) + 8 * len(WINDOWS)
LAST = 2 * CHUNK + 16
REST = 2 * (CHUNK + BOTH)
SENT = LAST + REST + 32
SHARE = 1 << 18
VMEM = pl.BlockSpec(memory_space=pltpu.VMEM)


def params(mib):
    return pltpu.CompilerParams(vmem_limit_bytes=mib << 20)


def cost(flops, moved):
    return pl.CostEstimate(flops=flops, bytes_accessed=moved, transcendentals=0)


def shift_lev(value, step_zlo, step_x):
    pairs = [(i, (i // N_X ^ step_zlo) * N_X + (i + step_x) % N_X) for i in range(N_LEV)]
    return lax.ppermute(value, "lev", pairs)


def swap_cores(value):
    return lax.ppermute(value, "hor", [(i, i ^ 1) for i in range(N_HOR)])


def hop(value, axis, cross):
    pairs = []
    for i in range(N_HOR):
        zhi, y, core = i // (2 * N_Y), i // 2 % N_Y, i % 2
        ahead = 1 - 2 * core
        if axis == "y":
            y = (y + ahead) % N_Y
        else:
            zhi = (zhi + ahead) % N_ZHI
        pairs.append((i, zhi * 2 * N_Y + y * 2 + (core ^ cross)))
    return lax.ppermute(value, "hor", pairs)


def repeat_kernel(index_ref, out_ref):
    for lev in range(N_LEV):
        out_ref[lev] = index_ref[...]


def stage_kernel(slab_ref, out_ref):
    for slot in range(SLOTS):
        out_ref[4 * slot : 4 * slot + 4, :] = slab_ref[slot]


def pick_kernel(index_ref, slab_ref, out_ref):
    for group in range(N_LEV):
        index = jnp.broadcast_to(index_ref[group], (8, LANES))
        lane, tile = index % LANES, index // LANES
        hits = [tile == t for t in range(GROUP // LANES)]
        for pair in range(2):
            rows = slice(8 * pair, 8 * pair + 8)
            total = jnp.zeros((8, LANES), jnp.float32)
            for t in range(GROUP // LANES):
                at = slice(group * GROUP + t * LANES, group * GROUP + (t + 1) * LANES)
                total = jnp.where(hits[t], jnp.take_along_axis(slab_ref[rows, at], lane, axis=1), total)
            out_ref[rows, group * SAMP : (group + 1) * SAMP] = total


def smooth_kernel(coef_ref, w0_ref, w1_ref, w2_ref, w3_ref, out_ref, raw_ref):
    x = lax.axis_index("lev") % N_X
    for step, ref in enumerate((w0_ref, w1_ref, w2_ref, w3_ref)):
        source = lax.rem(x - step + N_X, N_X)
        for zlo in range(N_ZLO):
            raw_ref[zlo * N_X + source] = ref[zlo]

    def tile(t, carry):
        at = pl.ds(pl.multiple_of(t * LANES, LANES), LANES)
        for slot in range(SLOTS):
            rows = [raw_ref[lev, 4 * slot : 4 * slot + 4, at] for lev in range(N_LEV)]
            value = jnp.concatenate(rows, axis=0)
            below, above = pltpu.roll(value, 1, 0), pltpu.roll(value, LEV - 1, 0)
            out_ref[slot * LEV : (slot + 1) * LEV, at] = (
                coef_ref[0:LEV] * value + coef_ref[LEV : 2 * LEV] * below + coef_ref[2 * LEV :] * above
            )
        return carry

    lax.fori_loop(0, BLOCK // LANES, tile, 0)


def build_rows(smooth_ref, half, out_ref, at):
    late = 2 * LEV
    m = jnp.maximum(half - 4 * LEV // HALF, 0) // 2
    product = smooth_ref[pl.ds(late + m, 1), :] * smooth_ref[pl.ds(pl.multiple_of(half % 2 * HALF, HALF), HALF), :]
    linear = smooth_ref[pl.ds(pl.multiple_of((late + half * HALF) % (4 * LEV), HALF), HALF), :]
    rows = jnp.where(half < 4 * LEV // HALF, linear, product)
    out_ref[at : at + HALF, :] = rows.astype(jnp.bfloat16)


def right_kernel(smooth_ref, out_ref):
    lev = lax.axis_index("lev")
    for i in range(COLS_OUT // HALF):
        build_rows(smooth_ref, lev * (COLS_OUT // HALF) + i, out_ref, i * HALF)


def windows_of(place):
    hor = lax.axis_index("hor")
    zhi, y, core = hor // (2 * N_Y), hor // 2 % N_Y, hor % 2
    to_y = {"far": y + 2, "cross": y + 5 - 2 * core, "near": y + 5 - 2 * core, "own": y}[place]
    to_y = lax.rem(to_y, N_Y)
    to_core = 1 - core if place == "cross" else core
    skip = 8 * lax.rem(to_y, 2)

    def start(to_z, offset):
        return (lax.rem(to_z, N_ZHI) * N_Y + to_y) * BOTH + offset - skip

    return (start(zhi + 2, 64 * to_core), start(zhi, 64 * to_core), start(zhi + 5 - 2 * to_core, 0)), skip


def product(place, smooth_ref, right_ref, left_ref):
    at = 0
    for first, size in zip(windows_of(place)[0], WINDOWS):
        for i in range((size + 8) // HALF):
            build_rows(smooth_ref, first // HALF + i, left_ref, at)
            at += HALF
    return lax.dot_general(
        left_ref[...], right_ref[...], (((1,), (1,)), ((), ())), preferred_element_type=jnp.float32
    )


def emit(place, prod_ref, out_ref):
    skip = windows_of(place)[1]
    at, base, group, tail = 0, 0, 0, 2 * CHUNK
    for number, size in enumerate(WINDOWS):
        if number == 1:
            base, group, tail = LAST, 0, LAST + REST
        for half in range(2):
            rows = pl.ds(pl.multiple_of(at + skip, 8), size)
            out_ref[base : base + size, :] = prod_ref[rows, half * LANES : (half + 1) * LANES]
            base += size
        for i in range(size // 8):
            rows = pl.ds(pl.multiple_of(at + 8 * i + skip, 8), 8)
            to = tail + 8 * (group // 8)
            strip = 16 * (group % 8)
            out_ref[to : to + 8, strip : strip + 16] = prod_ref[rows, 2 * LANES : COLS_OUT]
            group += 1
        at += size + 8


def begin_kernel(place, smooth_ref, right_ref, out_ref, left_ref):
    out_ref[...] = product(place, smooth_ref, right_ref, left_ref)


def finish_kernel(place, part_ref, smooth_ref, right_ref, out_ref, left_ref, prod_ref):
    prod_ref[...] = part_ref[...] + product(place, smooth_ref, right_ref, left_ref)
    emit(place, prod_ref, out_ref)


def gram_kernel(place, own_ref, own_right_ref, other_ref, other_right_ref, out_ref, left_ref, prod_ref):
    prod_ref[...] = product(place, own_ref, own_right_ref, left_ref)
    prod_ref[...] += product(place, other_ref, other_right_ref, left_ref)
    emit(place, prod_ref, out_ref)


def add_kernel(a_ref, b_ref, out_ref):
    out_ref[...] = a_ref[...] + b_ref[...]


def cut_kernel(a_ref, b_ref, far_ref, rest_ref):
    far_ref[...] = a_ref[0:LAST, :] + b_ref[0:LAST, :]
    rest_ref[...] = a_ref[LAST:SENT, :] + b_ref[LAST:SENT, :]


def split_kernel(a_ref, b_ref, own_ref, near_ref, cross_ref):
    core = lax.axis_index("hor") % 2
    lane = lax.broadcasted_iota(jnp.int32, (8, LANES), 1)

    def total(start, size):
        rows = pl.ds(start if isinstance(start, int) else pl.multiple_of(start, 8), size)
        return a_ref[rows, :] + b_ref[rows, :]

    ahead = 2 * CHUNK
    places = (
        (near_ref, ahead + 64 * core, BOTH, 1 + core, 1),
        (cross_ref, ahead + 64 * (1 - core), BOTH, 2 - core, 1),
        (own_ref, 0, CHUNK, 0, 0),
    )
    for ref, start, stride, tile, strip in places:
        ref[0:CHUNK, :] = total(start, CHUNK)
        ref[CHUNK : 2 * CHUNK, :] = total(start + stride, CHUNK)
        one, two = total(REST + 8 * tile, 8), total(REST + 8 * tile + 8, 8)
        if strip:
            one, two = pltpu.roll(one, LANES - 16 * strip, 1), pltpu.roll(two, LANES - 16 * strip, 1)
            one = jnp.where(lane < LANES - 16 * strip, one, two)
        ref[2 * CHUNK : 2 * CHUNK + 8, :] = one
        ref[2 * CHUNK + 8 : LAST, :] = two


def final_kernel(kept_ref, near_ref, cross_ref, out_ref):
    odd = lax.axis_index("hor") % 2 == 1
    scale = 1.0 / (BLOCK * N_HOR)

    def total(rows):
        return (kept_ref[rows, :] + near_ref[rows, :]) + cross_ref[rows, :]

    def place(value):
        return jnp.where(odd, value[CHUNK - ROWS_OUT : CHUNK], value[0:ROWS_OUT]) * scale

    for half in range(2):
        value = total(slice(half * CHUNK, (half + 1) * CHUNK))
        out_ref[:, half * LANES : (half + 1) * LANES] = place(value)
    packed = total(slice(2 * CHUNK, 2 * CHUNK + 8))
    rest = [pltpu.roll(packed, -16 * group % LANES, 1) for group in range(8)]
    rest.append(total(slice(2 * CHUNK + 8, LAST)))
    out_ref[:, 2 * LANES :] = place(jnp.concatenate(rest, axis=0))[:, :16]


def filter_coefficients(thickness, level_cuts):
    link = 1.0 - level_cuts.astype(jnp.float32)
    zero_one = jnp.zeros((1,), jnp.float32)
    lower = jnp.concatenate([zero_one, thickness[:-1] * link])
    upper = jnp.concatenate([thickness[1:] * link, zero_one])
    denom = 2.0 * thickness + lower + upper
    coef = jnp.concatenate([2.0 * thickness / denom, lower / denom, upper / denom])
    return jnp.broadcast_to(coef[:, None], (3 * LEV, LANES))


def right_of(smoothed):
    return pl.pallas_call(
        right_kernel,
        out_shape=jax.ShapeDtypeStruct((COLS_OUT, BLOCK), jnp.bfloat16),
        in_specs=[VMEM],
        out_specs=VMEM,
        compiler_params=params(4),
        cost_estimate=cost(1, SHARE),
        name="right",
    )(smoothed)


def gram(kernel, place, out_shape, *operands):
    scratch = [pltpu.VMEM((BUILT, BLOCK), jnp.bfloat16), pltpu.VMEM((BUILT, COLS_OUT), jnp.float32)]
    return pl.pallas_call(
        functools.partial(kernel, place),
        out_shape=jax.ShapeDtypeStruct(out_shape, jnp.float32),
        in_specs=[VMEM] * len(operands),
        out_specs=VMEM,
        scratch_shapes=scratch[:1] if kernel is begin_kernel else scratch,
        compiler_params=params(12),
        cost_estimate=cost(1, SHARE),
        name="gram_" + place,
    )(*operands)


def add(a, b, share=1):
    return pl.pallas_call(
        add_kernel,
        out_shape=jax.ShapeDtypeStruct(a.shape, a.dtype),
        in_specs=[VMEM] * 2,
        out_specs=VMEM,
        compiler_params=params(4),
        cost_estimate=cost(share, SHARE),
        name="add",
    )(a, b)


def cut(a, b):
    shapes = ((LAST, LANES), (SENT - LAST, LANES))
    return pl.pallas_call(
        cut_kernel,
        out_shape=[jax.ShapeDtypeStruct(shape, a.dtype) for shape in shapes],
        in_specs=[VMEM] * 2,
        out_specs=[VMEM] * 2,
        compiler_params=params(4),
        cost_estimate=cost(1, SHARE),
        name="cut",
    )(a, b)


def on_device(slab_fields, sample_index, thickness, level_cuts):
    f32 = jnp.float32
    coef = filter_coefficients(thickness, level_cuts)
    repeated = pl.pallas_call(
        repeat_kernel,
        out_shape=jax.ShapeDtypeStruct((N_LEV, 1, SAMP), jnp.int32),
        in_specs=[VMEM],
        out_specs=VMEM,
        compiler_params=params(1),
        name="repeat",
    )(sample_index)
    lists = lax.all_to_all(repeated, "lev", 0, 0, tiled=True)
    staged = pl.pallas_call(
        stage_kernel,
        out_shape=jax.ShapeDtypeStruct((4 * SLOTS, N_LEV * GROUP), f32),
        in_specs=[VMEM],
        out_specs=VMEM,
        compiler_params=params(8),
        cost_estimate=cost(0, 2 << 20),
        name="stage",
    )(slab_fields)
    picked = pl.pallas_call(
        pick_kernel,
        out_shape=jax.ShapeDtypeStruct((4 * SLOTS, BLOCK), f32),
        in_specs=[VMEM] * 2,
        out_specs=VMEM,
        compiler_params=params(8),
        name="pick",
    )(lists, staged)
    across = shift_lev(picked, 1, 0)
    up = lax.axis_index("lev") // N_X == 1
    near = jnp.stack([jnp.where(up, across, picked), jnp.where(up, picked, across)])
    far = {k: shift_lev(near, 0, k) for k in (2, 1, 3)}
    own = pl.pallas_call(
        smooth_kernel,
        out_shape=jax.ShapeDtypeStruct((SLOTS * LEV, BLOCK), f32),
        in_specs=[VMEM] * 5,
        out_specs=VMEM,
        scratch_shapes=[pltpu.VMEM((N_LEV, 4 * SLOTS, BLOCK), f32)],
        compiler_params=params(16),
        name="smooth",
    )(coef, near, far[1], far[2], far[3])
    other = swap_cores(own)
    own_right = right_of(own)
    begun = gram(begin_kernel, "far", (BUILT, COLS_OUT), own, own_right)
    other_right = right_of(other)
    sent = (SENT, LANES)
    parts = {"far": gram(finish_kernel, "far", sent, begun, other, other_right)}
    both = (own, own_right, other, other_right)
    parts["cross"] = gram(gram_kernel, "cross", sent, *both)
    both, parts["cross"] = lax.optimization_barrier((both, parts["cross"]))
    parts["near"] = gram(gram_kernel, "near", sent, *both)
    parts["own"] = gram(gram_kernel, "own", sent, *both)
    two_back = hop(parts["far"], "y", 0)
    from_cross = hop(parts["cross"], "y", 1)
    parts["near"], parts["own"] = lax.optimization_barrier((parts["near"], parts["own"]))
    near_far, near_rest = cut(parts["near"], two_back)
    from_near_far, from_near_rest = hop(near_far, "y", 0), hop(near_rest, "y", 0)
    sum_far, sum_rest = cut(parts["own"], from_cross)
    straight = [(i, (i + N_HOR // 2) % N_HOR) for i in range(N_HOR)]
    from_far = lax.ppermute(add(sum_far, from_near_far, 1 << 30), "hor", straight)
    kept, near, cross = pl.pallas_call(
        split_kernel,
        out_shape=[jax.ShapeDtypeStruct((LAST, LANES), f32)] * 3,
        in_specs=[VMEM] * 2,
        out_specs=[VMEM] * 3,
        compiler_params=params(8),
        cost_estimate=cost(1, SHARE),
        name="split",
    )(sum_rest, from_near_rest)
    from_near = hop(near, "z_hi", 0)
    from_cross = hop(cross, "z_hi", 1)
    kept = add(kept, from_far, 1 << 30)
    return pl.pallas_call(
        final_kernel,
        out_shape=jax.ShapeDtypeStruct((ROWS_OUT, COLS_OUT), f32),
        in_specs=[VMEM] * 3,
        out_specs=VMEM,
        compiler_params=params(8),
        cost_estimate=cost(1, SHARE),
        name="final",
    )(kept, from_near, from_cross)


def solution(mesh):
    in_specs = (P(None, "lev", "hor"), P("hor", "lev"), P(), P())
    out_specs = P("hor", "lev")
    return jax.shard_map(on_device, mesh=mesh, in_specs=in_specs, out_specs=out_specs, check_vma=False)
```

```python
import functools

import jax
import jax.numpy as jnp
from jax import lax
from jax.experimental import pallas as pl
from jax.experimental.pallas import tpu as pltpu
from jax.sharding import PartitionSpec as P

LEV, SLOTS, LANES = 32, 4, 128
N_X, N_ZLO, N_Y, N_ZHI = 4, 2, 4, 4
N_LEV, N_HOR = N_X * N_ZLO, N_ZHI * N_Y * 2
GROUP, SAMP = 2048, 128
BLOCK = N_LEV * SAMP
FEAT = 4 * LEV + 2 * LEV * LEV
ROWS_OUT, COLS_OUT = FEAT // N_HOR, FEAT // N_LEV
CHUNK, BOTH, HALF = 72, 2 * ROWS_OUT, 16
WINDOWS = (CHUNK, CHUNK, BOTH)
BUILT = sum(WINDOWS) + 8 * len(WINDOWS)
LAST = 2 * CHUNK + 16
REST = 2 * (CHUNK + BOTH)
SENT = LAST + REST + 32
SHARE = 1 << 18
VMEM = pl.BlockSpec(memory_space=pltpu.VMEM)


def params(mib):
    return pltpu.CompilerParams(vmem_limit_bytes=mib << 20)


def cost(flops, moved):
    return pl.CostEstimate(flops=flops, bytes_accessed=moved, transcendentals=0)


def shift_lev(value, step_zlo, step_x):
    pairs = [(i, (i // N_X ^ step_zlo) * N_X + (i + step_x) % N_X) for i in range(N_LEV)]
    return lax.ppermute(value, "lev", pairs)


def swap_cores(value):
    return lax.ppermute(value, "hor", [(i, i ^ 1) for i in range(N_HOR)])


def hop(value, axis, cross):
    pairs = []
    for i in range(N_HOR):
        zhi, y, core = i // (2 * N_Y), i // 2 % N_Y, i % 2
        ahead = 1 - 2 * core
        if axis == "y":
            y = (y + ahead) % N_Y
        else:
            zhi = (zhi + ahead) % N_ZHI
        pairs.append((i, zhi * 2 * N_Y + y * 2 + (core ^ cross)))
    return lax.ppermute(value, "hor", pairs)


def repeat_kernel(index_ref, out_ref):
    for lev in range(N_LEV):
        out_ref[lev] = index_ref[...]


def stage_kernel(slab_ref, out_ref):
    for slot in range(SLOTS):
        out_ref[4 * slot : 4 * slot + 4, :] = slab_ref[slot]


def pick_kernel(index_ref, slab_ref, out_ref):
    for group in range(N_LEV):
        index = jnp.broadcast_to(index_ref[group], (8, LANES))
        lane, tile = index % LANES, index // LANES
        hits = [tile == t for t in range(GROUP // LANES)]
        for pair in range(2):
            rows = slice(8 * pair, 8 * pair + 8)
            total = jnp.zeros((8, LANES), jnp.float32)
            for t in range(GROUP // LANES):
                at = slice(group * GROUP + t * LANES, group * GROUP + (t + 1) * LANES)
                total = jnp.where(hits[t], jnp.take_along_axis(slab_ref[rows, at], lane, axis=1), total)
            out_ref[rows, group * SAMP : (group + 1) * SAMP] = total


def smooth_kernel(coef_ref, w0_ref, w1_ref, w2_ref, w3_ref, out_ref, raw_ref):
    x = lax.axis_index("lev") % N_X
    for step, ref in enumerate((w0_ref, w1_ref, w2_ref, w3_ref)):
        source = lax.rem(x - step + N_X, N_X)
        for zlo in range(N_ZLO):
            raw_ref[zlo * N_X + source] = ref[zlo]

    def tile(t, carry):
        at = pl.ds(pl.multiple_of(t * LANES, LANES), LANES)
        for slot in range(SLOTS):
            rows = [raw_ref[lev, 4 * slot : 4 * slot + 4, at] for lev in range(N_LEV)]
            value = jnp.concatenate(rows, axis=0)
            below, above = pltpu.roll(value, 1, 0), pltpu.roll(value, LEV - 1, 0)
            out_ref[slot * LEV : (slot + 1) * LEV, at] = (
                coef_ref[0:LEV] * value + coef_ref[LEV : 2 * LEV] * below + coef_ref[2 * LEV :] * above
            )
        return carry

    lax.fori_loop(0, BLOCK // LANES, tile, 0)


def build_rows(smooth_ref, half, out_ref, at):
    late = 2 * LEV
    m = jnp.maximum(half - 4 * LEV // HALF, 0) // 2
    product = smooth_ref[pl.ds(late + m, 1), :] * smooth_ref[pl.ds(pl.multiple_of(half % 2 * HALF, HALF), HALF), :]
    linear = smooth_ref[pl.ds(pl.multiple_of((late + half * HALF) % (4 * LEV), HALF), HALF), :]
    rows = jnp.where(half < 4 * LEV // HALF, linear, product)
    out_ref[at : at + HALF, :] = rows.astype(jnp.bfloat16)


def right_kernel(smooth_ref, out_ref):
    lev = lax.axis_index("lev")
    for i in range(COLS_OUT // HALF):
        build_rows(smooth_ref, lev * (COLS_OUT // HALF) + i, out_ref, i * HALF)


def windows_of(place):
    hor = lax.axis_index("hor")
    zhi, y, core = hor // (2 * N_Y), hor // 2 % N_Y, hor % 2
    to_y = {"far": y + 2, "cross": y + 5 - 2 * core, "near": y + 5 - 2 * core, "own": y}[place]
    to_y = lax.rem(to_y, N_Y)
    to_core = 1 - core if place == "cross" else core
    skip = 8 * lax.rem(to_y, 2)

    def start(to_z, offset):
        return (lax.rem(to_z, N_ZHI) * N_Y + to_y) * BOTH + offset - skip

    return (start(zhi + 2, 64 * to_core), start(zhi, 64 * to_core), start(zhi + 5 - 2 * to_core, 0)), skip


def product(place, smooth_ref, right_ref, left_ref):
    at = 0
    for first, size in zip(windows_of(place)[0], WINDOWS):
        for i in range((size + 8) // HALF):
            build_rows(smooth_ref, first // HALF + i, left_ref, at)
            at += HALF
    return lax.dot_general(
        left_ref[...], right_ref[...], (((1,), (1,)), ((), ())), preferred_element_type=jnp.float32
    )


def emit(place, prod_ref, out_refs):
    skip = windows_of(place)[1]
    at, base, group, tail = 0, 0, 0, 2 * CHUNK
    out_ref = out_refs[0]
    for number, size in enumerate(WINDOWS):
        if number == 1:
            base, group, tail = LAST, 0, LAST + REST
            if len(out_refs) == 2:
                out_ref, base, tail = out_refs[1], 0, REST
        for half in range(2):
            rows = pl.ds(pl.multiple_of(at + skip, 8), size)
            out_ref[base : base + size, :] = prod_ref[rows, half * LANES : (half + 1) * LANES]
            base += size
        for i in range(size // 8):
            rows = pl.ds(pl.multiple_of(at + 8 * i + skip, 8), 8)
            to = tail + 8 * (group // 8)
            strip = 16 * (group % 8)
            out_ref[to : to + 8, strip : strip + 16] = prod_ref[rows, 2 * LANES : COLS_OUT]
            group += 1
        at += size + 8


def begin_kernel(place, smooth_ref, right_ref, out_ref, left_ref):
    out_ref[...] = product(place, smooth_ref, right_ref, left_ref)


def finish_kernel(place, part_ref, smooth_ref, right_ref, *refs):
    left_ref, prod_ref = refs[-2:]
    prod_ref[...] = part_ref[...] + product(place, smooth_ref, right_ref, left_ref)
    emit(place, prod_ref, refs[:-2])


def gram_kernel(place, own_ref, own_right_ref, other_ref, other_right_ref, *refs):
    left_ref, prod_ref = refs[-2:]
    prod_ref[...] = product(place, own_ref, own_right_ref, left_ref)
    prod_ref[...] += product(place, other_ref, other_right_ref, left_ref)
    emit(place, prod_ref, refs[:-2])


def add_kernel(a_ref, b_ref, out_ref):
    out_ref[...] = a_ref[...] + b_ref[...]


def cut_kernel(a_ref, b_ref, far_ref, rest_ref):
    far_ref[...] = a_ref[0:LAST, :] + b_ref[0:LAST, :]
    rest_ref[...] = a_ref[LAST:SENT, :] + b_ref[LAST:SENT, :]


def split_kernel(a_ref, b_ref, own_ref, near_ref, cross_ref):
    core = lax.axis_index("hor") % 2
    lane = lax.broadcasted_iota(jnp.int32, (8, LANES), 1)

    def total(start, size):
        rows = pl.ds(start if isinstance(start, int) else pl.multiple_of(start, 8), size)
        return a_ref[rows, :] + b_ref[rows, :]

    ahead = 2 * CHUNK
    places = (
        (near_ref, ahead + 64 * core, BOTH, 1 + core, 1),
        (cross_ref, ahead + 64 * (1 - core), BOTH, 2 - core, 1),
        (own_ref, 0, CHUNK, 0, 0),
    )
    for ref, start, stride, tile, strip in places:
        ref[0:CHUNK, :] = total(start, CHUNK)
        ref[CHUNK : 2 * CHUNK, :] = total(start + stride, CHUNK)
        one, two = total(REST + 8 * tile, 8), total(REST + 8 * tile + 8, 8)
        if strip:
            one, two = pltpu.roll(one, LANES - 16 * strip, 1), pltpu.roll(two, LANES - 16 * strip, 1)
            one = jnp.where(lane < LANES - 16 * strip, one, two)
        ref[2 * CHUNK : 2 * CHUNK + 8, :] = one
        ref[2 * CHUNK + 8 : LAST, :] = two


def final_kernel(kept_ref, near_ref, out_ref):
    odd = lax.axis_index("hor") % 2 == 1
    scale = 1.0 / (BLOCK * N_HOR)

    def total(rows):
        return kept_ref[rows, :] + near_ref[rows, :]

    def place(value):
        return jnp.where(odd, value[CHUNK - ROWS_OUT : CHUNK], value[0:ROWS_OUT]) * scale

    for half in range(2):
        value = total(slice(half * CHUNK, (half + 1) * CHUNK))
        out_ref[:, half * LANES : (half + 1) * LANES] = place(value)
    packed = total(slice(2 * CHUNK, 2 * CHUNK + 8))
    rest = [pltpu.roll(packed, -16 * group % LANES, 1) for group in range(8)]
    rest.append(total(slice(2 * CHUNK + 8, LAST)))
    out_ref[:, 2 * LANES :] = place(jnp.concatenate(rest, axis=0))[:, :16]


def filter_coefficients(thickness, level_cuts):
    link = 1.0 - level_cuts.astype(jnp.float32)
    zero_one = jnp.zeros((1,), jnp.float32)
    lower = jnp.concatenate([zero_one, thickness[:-1] * link])
    upper = jnp.concatenate([thickness[1:] * link, zero_one])
    denom = 2.0 * thickness + lower + upper
    coef = jnp.concatenate([2.0 * thickness / denom, lower / denom, upper / denom])
    return jnp.broadcast_to(coef[:, None], (3 * LEV, LANES))


def right_of(smoothed):
    return pl.pallas_call(
        right_kernel,
        out_shape=jax.ShapeDtypeStruct((COLS_OUT, BLOCK), jnp.bfloat16),
        in_specs=[VMEM],
        out_specs=VMEM,
        compiler_params=params(4),
        cost_estimate=cost(1, SHARE),
        name="right",
    )(smoothed)


def gram(kernel, place, out_shapes, *operands):
    scratch = [pltpu.VMEM((BUILT, BLOCK), jnp.bfloat16), pltpu.VMEM((BUILT, COLS_OUT), jnp.float32)]
    return pl.pallas_call(
        functools.partial(kernel, place),
        out_shape=[jax.ShapeDtypeStruct(shape, jnp.float32) for shape in out_shapes],
        in_specs=[VMEM] * len(operands),
        out_specs=[VMEM] * len(out_shapes),
        scratch_shapes=scratch[:1] if kernel is begin_kernel else scratch,
        compiler_params=params(12),
        cost_estimate=cost(1, SHARE),
        name="gram_" + place,
    )(*operands)


def add(a, b, share=1):
    return pl.pallas_call(
        add_kernel,
        out_shape=jax.ShapeDtypeStruct(a.shape, a.dtype),
        in_specs=[VMEM] * 2,
        out_specs=VMEM,
        compiler_params=params(4),
        cost_estimate=cost(share, SHARE),
        name="add",
    )(a, b)


def cut(a, b):
    shapes = ((LAST, LANES), (SENT - LAST, LANES))
    return pl.pallas_call(
        cut_kernel,
        out_shape=[jax.ShapeDtypeStruct(shape, a.dtype) for shape in shapes],
        in_specs=[VMEM] * 2,
        out_specs=[VMEM] * 2,
        compiler_params=params(4),
        cost_estimate=cost(1, SHARE),
        name="cut",
    )(a, b)


def on_device(slab_fields, sample_index, thickness, level_cuts):
    f32 = jnp.float32
    coef = filter_coefficients(thickness, level_cuts)
    repeated = pl.pallas_call(
        repeat_kernel,
        out_shape=jax.ShapeDtypeStruct((N_LEV, 1, SAMP), jnp.int32),
        in_specs=[VMEM],
        out_specs=VMEM,
        compiler_params=params(1),
        name="repeat",
    )(sample_index)
    lists = lax.all_to_all(repeated, "lev", 0, 0, tiled=True)
    staged = pl.pallas_call(
        stage_kernel,
        out_shape=jax.ShapeDtypeStruct((4 * SLOTS, N_LEV * GROUP), f32),
        in_specs=[VMEM],
        out_specs=VMEM,
        compiler_params=params(8),
        cost_estimate=cost(0, 2 << 20),
        name="stage",
    )(slab_fields)
    picked = pl.pallas_call(
        pick_kernel,
        out_shape=jax.ShapeDtypeStruct((4 * SLOTS, BLOCK), f32),
        in_specs=[VMEM] * 2,
        out_specs=VMEM,
        compiler_params=params(8),
        name="pick",
    )(lists, staged)
    across = shift_lev(picked, 1, 0)
    up = lax.axis_index("lev") // N_X == 1
    near = jnp.stack([jnp.where(up, across, picked), jnp.where(up, picked, across)])
    far = {k: shift_lev(near, 0, k) for k in (2, 1, 3)}
    own = pl.pallas_call(
        smooth_kernel,
        out_shape=jax.ShapeDtypeStruct((SLOTS * LEV, BLOCK), f32),
        in_specs=[VMEM] * 5,
        out_specs=VMEM,
        scratch_shapes=[pltpu.VMEM((N_LEV, 4 * SLOTS, BLOCK), f32)],
        compiler_params=params(16),
        name="smooth",
    )(coef, near, far[1], far[2], far[3])
    other = swap_cores(own)
    own_right = right_of(own)
    (begun,) = gram(begin_kernel, "far", [(BUILT, COLS_OUT)], own, own_right)
    other_right = right_of(other)
    whole, apart = [(SENT, LANES)], [(LAST, LANES), (SENT - LAST, LANES)]
    far_far, far_rest = gram(finish_kernel, "far", apart, begun, other, other_right)
    both = (own, own_right, other, other_right)
    (crossing,) = gram(gram_kernel, "cross", whole, *both)
    both, crossing = lax.optimization_barrier((both, crossing))
    near_far, near_rest = gram(gram_kernel, "near", apart, *both)
    (own_part,) = gram(gram_kernel, "own", whole, *both)
    two_back_far, two_back_rest = hop(far_far, "y", 0), hop(far_rest, "y", 0)
    from_cross = hop(crossing, "y", 1)
    near_far = add(near_far, two_back_far, 1 << 31)
    near_rest = add(near_rest, two_back_rest)
    from_near_far, from_near_rest = hop(near_far, "y", 0), hop(near_rest, "y", 0)
    sum_far, sum_rest = cut(own_part, from_cross)
    two_back = hop(add(sum_far, from_near_far, 1 << 31), "z_hi", 0)
    kept, near, cross = pl.pallas_call(
        split_kernel,
        out_shape=[jax.ShapeDtypeStruct((LAST, LANES), f32)] * 3,
        in_specs=[VMEM] * 2,
        out_specs=[VMEM] * 3,
        compiler_params=params(8),
        cost_estimate=cost(1, SHARE),
        name="split",
    )(sum_rest, from_near_rest)
    from_cross = hop(cross, "z_hi", 1)
    kept = add(kept, from_cross)
    from_near = hop(add(near, two_back), "z_hi", 0)
    return pl.pallas_call(
        final_kernel,
        out_shape=jax.ShapeDtypeStruct((ROWS_OUT, COLS_OUT), f32),
        in_specs=[VMEM] * 2,
        out_specs=VMEM,
        compiler_params=params(8),
        cost_estimate=cost(1, SHARE),
        name="final",
    )(kept, from_near)


def solution(mesh):
    in_specs = (P(None, "lev", "hor"), P("hor", "lev"), P(), P())
    out_specs = P("hor", "lev")
    return jax.shard_map(on_device, mesh=mesh, in_specs=in_specs, out_specs=out_specs, check_vma=False)
```

```python
import functools

import jax
import jax.numpy as jnp
from jax import lax
from jax.experimental import pallas as pl
from jax.experimental.pallas import tpu as pltpu
from jax.sharding import PartitionSpec as P

LEV, SLOTS, LANES = 32, 4, 128
N_X, N_ZLO, N_Y, N_ZHI = 4, 2, 4, 4
N_LEV, N_HOR = N_X * N_ZLO, N_ZHI * N_Y * 2
GROUP, SAMP = 2048, 128
BLOCK = N_LEV * SAMP
FEAT = 4 * LEV + 2 * LEV * LEV
ROWS_OUT, COLS_OUT = FEAT // N_HOR, FEAT // N_LEV
CHUNK, BOTH, HALF = 72, 2 * ROWS_OUT, 16
WINDOWS = (CHUNK, CHUNK, BOTH)
BUILT = sum(WINDOWS) + 8 * len(WINDOWS)
LAST = 2 * CHUNK + 16
REST = 2 * (CHUNK + BOTH)
SENT = LAST + REST + 32
SHARE = 1 << 18
VMEM = pl.BlockSpec(memory_space=pltpu.VMEM)


def params(mib):
    return pltpu.CompilerParams(vmem_limit_bytes=mib << 20)


def cost(flops, moved):
    return pl.CostEstimate(flops=flops, bytes_accessed=moved, transcendentals=0)


def shift_lev(value, step_zlo, step_x):
    pairs = [(i, (i // N_X ^ step_zlo) * N_X + (i + step_x) % N_X) for i in range(N_LEV)]
    return lax.ppermute(value, "lev", pairs)


def swap_cores(value):
    return lax.ppermute(value, "hor", [(i, i ^ 1) for i in range(N_HOR)])


def hop(value, axis, cross):
    pairs = []
    for i in range(N_HOR):
        zhi, y, core = i // (2 * N_Y), i // 2 % N_Y, i % 2
        ahead = 1 - 2 * core
        if axis == "y":
            y = (y + ahead) % N_Y
        else:
            zhi = (zhi + ahead) % N_ZHI
        pairs.append((i, zhi * 2 * N_Y + y * 2 + (core ^ cross)))
    return lax.ppermute(value, "hor", pairs)


def repeat_kernel(index_ref, out_ref):
    for lev in range(N_LEV):
        out_ref[lev] = index_ref[...]


def stage_kernel(slab_ref, out_ref):
    for slot in range(SLOTS):
        out_ref[4 * slot : 4 * slot + 4, :] = slab_ref[slot]


def pick_kernel(index_ref, slab_ref, out_ref):
    for group in range(N_LEV):
        index = jnp.broadcast_to(index_ref[group], (8, LANES))
        lane, tile = index % LANES, index // LANES
        hits = [tile == t for t in range(GROUP // LANES)]
        for pair in range(2):
            rows = slice(8 * pair, 8 * pair + 8)
            total = jnp.zeros((8, LANES), jnp.float32)
            for t in range(GROUP // LANES):
                at = slice(group * GROUP + t * LANES, group * GROUP + (t + 1) * LANES)
                total = jnp.where(hits[t], jnp.take_along_axis(slab_ref[rows, at], lane, axis=1), total)
            out_ref[rows, group * SAMP : (group + 1) * SAMP] = total


def smooth_kernel(coef_ref, w0_ref, w2_ref, w1_ref, w3_ref, out_ref, raw_ref):
    x = lax.axis_index("lev") % N_X
    for step, ref in enumerate((w0_ref, w1_ref, w2_ref, w3_ref)):
        source = lax.rem(x - step + N_X, N_X)
        for zlo in range(N_ZLO):
            raw_ref[zlo * N_X + source] = ref[zlo]

    def tile(t, carry):
        at = pl.ds(pl.multiple_of(t * LANES, LANES), LANES)
        for slot in range(SLOTS):
            rows = [raw_ref[lev, 4 * slot : 4 * slot + 4, at] for lev in range(N_LEV)]
            value = jnp.concatenate(rows, axis=0)
            below, above = pltpu.roll(value, 1, 0), pltpu.roll(value, LEV - 1, 0)
            out_ref[slot * LEV : (slot + 1) * LEV, at] = (
                coef_ref[0:LEV] * value + coef_ref[LEV : 2 * LEV] * below + coef_ref[2 * LEV :] * above
            )
        return carry

    lax.fori_loop(0, BLOCK // LANES, tile, 0)


def build_rows(smooth_ref, half, out_ref, at):
    late = 2 * LEV
    m = jnp.maximum(half - 4 * LEV // HALF, 0) // 2
    product = smooth_ref[pl.ds(late + m, 1), :] * smooth_ref[pl.ds(pl.multiple_of(half % 2 * HALF, HALF), HALF), :]
    linear = smooth_ref[pl.ds(pl.multiple_of((late + half * HALF) % (4 * LEV), HALF), HALF), :]
    rows = jnp.where(half < 4 * LEV // HALF, linear, product)
    out_ref[at : at + HALF, :] = rows.astype(jnp.bfloat16)


def right_kernel(smooth_ref, out_ref):
    lev = lax.axis_index("lev")
    for i in range(COLS_OUT // HALF):
        build_rows(smooth_ref, lev * (COLS_OUT // HALF) + i, out_ref, i * HALF)


def windows_of(place):
    hor = lax.axis_index("hor")
    zhi, y, core = hor // (2 * N_Y), hor // 2 % N_Y, hor % 2
    to_y = {"far": y + 2, "cross": y + 5 - 2 * core, "near": y + 5 - 2 * core, "own": y}[place]
    to_y = lax.rem(to_y, N_Y)
    to_core = 1 - core if place == "cross" else core
    skip = 8 * lax.rem(to_y, 2)

    def start(to_z, offset):
        return (lax.rem(to_z, N_ZHI) * N_Y + to_y) * BOTH + offset - skip

    return (start(zhi + 2, 64 * to_core), start(zhi, 64 * to_core), start(zhi + 5 - 2 * to_core, 0)), skip


def product(place, smooth_ref, right_ref, left_ref):
    at = 0
    for first, size in zip(windows_of(place)[0], WINDOWS):
        for i in range((size + 8) // HALF):
            build_rows(smooth_ref, first // HALF + i, left_ref, at)
            at += HALF
    return lax.dot_general(
        left_ref[...], right_ref[...], (((1,), (1,)), ((), ())), preferred_element_type=jnp.float32
    )


def emit(place, prod_ref, out_ref):
    skip = windows_of(place)[1]
    at, base, group, tail = 0, 0, 0, 2 * CHUNK
    for number, size in enumerate(WINDOWS):
        if number == 1:
            base, group, tail = LAST, 0, LAST + REST
        for half in range(2):
            rows = pl.ds(pl.multiple_of(at + skip, 8), size)
            out_ref[base : base + size, :] = prod_ref[rows, half * LANES : (half + 1) * LANES]
            base += size
        for i in range(size // 8):
            rows = pl.ds(pl.multiple_of(at + 8 * i + skip, 8), 8)
            to = tail + 8 * (group // 8)
            strip = 16 * (group % 8)
            out_ref[to : to + 8, strip : strip + 16] = prod_ref[rows, 2 * LANES : COLS_OUT]
            group += 1
        at += size + 8


def begin_kernel(place, smooth_ref, right_ref, out_ref, left_ref):
    out_ref[...] = product(place, smooth_ref, right_ref, left_ref)


def finish_kernel(place, part_ref, smooth_ref, right_ref, out_ref, left_ref, prod_ref):
    prod_ref[...] = part_ref[...] + product(place, smooth_ref, right_ref, left_ref)
    emit(place, prod_ref, out_ref)


def gram_kernel(place, own_ref, own_right_ref, other_ref, other_right_ref, out_ref, left_ref, prod_ref):
    prod_ref[...] = product(place, own_ref, own_right_ref, left_ref)
    prod_ref[...] += product(place, other_ref, other_right_ref, left_ref)
    emit(place, prod_ref, out_ref)


def add_kernel(a_ref, b_ref, out_ref):
    out_ref[...] = a_ref[...] + b_ref[...]


def cut_kernel(a_ref, b_ref, far_ref, rest_ref):
    far_ref[...] = a_ref[0:LAST, :] + b_ref[0:LAST, :]
    rest_ref[...] = a_ref[LAST:SENT, :] + b_ref[LAST:SENT, :]


def split_kernel(a_ref, b_ref, own_ref, near_ref, cross_ref):
    core = lax.axis_index("hor") % 2
    lane = lax.broadcasted_iota(jnp.int32, (8, LANES), 1)

    def total(start, size):
        rows = pl.ds(start if isinstance(start, int) else pl.multiple_of(start, 8), size)
        return a_ref[rows, :] + b_ref[rows, :]

    ahead = 2 * CHUNK
    places = (
        (near_ref, ahead + 64 * core, BOTH, 1 + core, 1),
        (cross_ref, ahead + 64 * (1 - core), BOTH, 2 - core, 1),
        (own_ref, 0, CHUNK, 0, 0),
    )
    for ref, start, stride, tile, strip in places:
        ref[0:CHUNK, :] = total(start, CHUNK)
        ref[CHUNK : 2 * CHUNK, :] = total(start + stride, CHUNK)
        one, two = total(REST + 8 * tile, 8), total(REST + 8 * tile + 8, 8)
        if strip:
            one, two = pltpu.roll(one, LANES - 16 * strip, 1), pltpu.roll(two, LANES - 16 * strip, 1)
            one = jnp.where(lane < LANES - 16 * strip, one, two)
        ref[2 * CHUNK : 2 * CHUNK + 8, :] = one
        ref[2 * CHUNK + 8 : LAST, :] = two


def final_kernel(t0_ref, t1_ref, t2_ref, out_ref):
    odd = lax.axis_index("hor") % 2 == 1
    scale = 1.0 / (BLOCK * N_HOR)

    def total(rows):
        return (t0_ref[rows, :] + t1_ref[rows, :]) + t2_ref[rows, :]

    def place(value):
        return jnp.where(odd, value[CHUNK - ROWS_OUT : CHUNK], value[0:ROWS_OUT]) * scale

    for half in range(2):
        value = total(slice(half * CHUNK, (half + 1) * CHUNK))
        out_ref[:, half * LANES : (half + 1) * LANES] = place(value)
    packed = total(slice(2 * CHUNK, 2 * CHUNK + 8))
    rest = [pltpu.roll(packed, -16 * group % LANES, 1) for group in range(8)]
    rest.append(total(slice(2 * CHUNK + 8, LAST)))
    out_ref[:, 2 * LANES :] = place(jnp.concatenate(rest, axis=0))[:, :16]


def filter_coefficients(thickness, level_cuts):
    link = 1.0 - level_cuts.astype(jnp.float32)
    zero_one = jnp.zeros((1,), jnp.float32)
    lower = jnp.concatenate([zero_one, thickness[:-1] * link])
    upper = jnp.concatenate([thickness[1:] * link, zero_one])
    denom = 2.0 * thickness + lower + upper
    coef = jnp.concatenate([2.0 * thickness / denom, lower / denom, upper / denom])
    return jnp.broadcast_to(coef[:, None], (3 * LEV, LANES))


def right_of(smoothed):
    return pl.pallas_call(
        right_kernel,
        out_shape=jax.ShapeDtypeStruct((COLS_OUT, BLOCK), jnp.bfloat16),
        in_specs=[VMEM],
        out_specs=VMEM,
        compiler_params=params(4),
        cost_estimate=cost(1, SHARE),
        name="right",
    )(smoothed)


def gram(kernel, place, out_shape, *operands):
    scratch = [pltpu.VMEM((BUILT, BLOCK), jnp.bfloat16), pltpu.VMEM((BUILT, COLS_OUT), jnp.float32)]
    return pl.pallas_call(
        functools.partial(kernel, place),
        out_shape=jax.ShapeDtypeStruct(out_shape, jnp.float32),
        in_specs=[VMEM] * len(operands),
        out_specs=VMEM,
        scratch_shapes=scratch[:1] if kernel is begin_kernel else scratch,
        compiler_params=params(12),
        cost_estimate=cost(1, SHARE),
        name="gram_" + place,
    )(*operands)


def add(a, b, share=1):
    return pl.pallas_call(
        add_kernel,
        out_shape=jax.ShapeDtypeStruct(a.shape, a.dtype),
        in_specs=[VMEM] * 2,
        out_specs=VMEM,
        compiler_params=params(4),
        cost_estimate=cost(share, SHARE),
        name="add",
    )(a, b)


def cut(a, b):
    shapes = ((LAST, LANES), (SENT - LAST, LANES))
    return pl.pallas_call(
        cut_kernel,
        out_shape=[jax.ShapeDtypeStruct(shape, a.dtype) for shape in shapes],
        in_specs=[VMEM] * 2,
        out_specs=[VMEM] * 2,
        compiler_params=params(4),
        cost_estimate=cost(1, SHARE),
        name="cut",
    )(a, b)


def on_device(slab_fields, sample_index, thickness, level_cuts):
    f32 = jnp.float32
    coef = filter_coefficients(thickness, level_cuts)
    repeated = pl.pallas_call(
        repeat_kernel,
        out_shape=jax.ShapeDtypeStruct((N_LEV, 1, SAMP), jnp.int32),
        in_specs=[VMEM],
        out_specs=VMEM,
        compiler_params=params(60),
        name="repeat",
    )(sample_index)
    lists = lax.all_to_all(repeated, "lev", 0, 0, tiled=True)
    staged = pl.pallas_call(
        stage_kernel,
        out_shape=jax.ShapeDtypeStruct((4 * SLOTS, N_LEV * GROUP), f32),
        in_specs=[VMEM],
        out_specs=VMEM,
        compiler_params=params(8),
        cost_estimate=cost(0, 2 << 20),
        name="stage",
    )(slab_fields)
    picked = pl.pallas_call(
        pick_kernel,
        out_shape=jax.ShapeDtypeStruct((4 * SLOTS, BLOCK), f32),
        in_specs=[VMEM] * 2,
        out_specs=VMEM,
        compiler_params=params(8),
        name="pick",
    )(lists, staged)
    across = shift_lev(picked, 1, 0)
    up = lax.axis_index("lev") // N_X == 1
    near = jnp.stack([jnp.where(up, across, picked), jnp.where(up, picked, across)])
    far = {k: shift_lev(near, 0, k) for k in (2, 1, 3)}
    own = pl.pallas_call(
        smooth_kernel,
        out_shape=jax.ShapeDtypeStruct((SLOTS * LEV, BLOCK), f32),
        in_specs=[VMEM] * 5,
        out_specs=VMEM,
        scratch_shapes=[pltpu.VMEM((N_LEV, 4 * SLOTS, BLOCK), f32)],
        compiler_params=params(16),
        name="smooth",
    )(coef, near, far[2], far[1], far[3])
    other = swap_cores(own)
    own_right = right_of(own)
    begun = gram(begin_kernel, "far", (BUILT, COLS_OUT), own, own_right)
    other_right = right_of(other)
    sent = (SENT, LANES)
    parts = {"far": gram(finish_kernel, "far", sent, begun, other, other_right)}
    both = (own, own_right, other, other_right)
    parts["cross"] = gram(gram_kernel, "cross", sent, *both)
    both, parts["cross"] = lax.optimization_barrier((both, parts["cross"]))
    parts["near"] = gram(gram_kernel, "near", sent, *both)
    parts["own"] = gram(gram_kernel, "own", sent, *both)
    two_back = hop(parts["far"], "y", 0)
    from_cross = hop(parts["cross"], "y", 1)
    near_far, near_rest = cut(parts["near"], two_back)
    from_near_far, from_near_rest = hop(near_far, "y", 0), hop(near_rest, "y", 0)
    sum_far, sum_rest = cut(parts["own"], from_cross)
    two_back = hop(add(sum_far, from_near_far, 1 << 30), "z_hi", 0)
    kept, near, cross = pl.pallas_call(
        split_kernel,
        out_shape=[jax.ShapeDtypeStruct((LAST, LANES), f32)] * 3,
        in_specs=[VMEM] * 2,
        out_specs=[VMEM] * 3,
        compiler_params=params(8),
        cost_estimate=cost(1, SHARE),
        name="split",
    )(sum_rest, from_near_rest)
    from_cross = hop(cross, "z_hi", 1)
    from_near = hop(add(near, two_back), "z_hi", 0)
    return pl.pallas_call(
        final_kernel,
        out_shape=jax.ShapeDtypeStruct((ROWS_OUT, COLS_OUT), f32),
        in_specs=[VMEM] * 3,
        out_specs=VMEM,
        compiler_params=params(8),
        cost_estimate=cost(1, SHARE),
        name="final",
    )(kept, from_cross, from_near)


def solution(mesh):
    in_specs = (P(None, "lev", "hor"), P("hor", "lev"), P(), P())
    out_specs = P("hor", "lev")
    return jax.shard_map(on_device, mesh=mesh, in_specs=in_specs, out_specs=out_specs, check_vma=False)
```

```python
import functools

import jax
import jax.numpy as jnp
from jax import lax
from jax.experimental import pallas as pl
from jax.experimental.pallas import tpu as pltpu
from jax.sharding import PartitionSpec as P

LEV, SLOTS, LANES = 32, 4, 128
N_X, N_ZLO, N_Y, N_ZHI = 4, 2, 4, 4
N_LEV, N_HOR = N_X * N_ZLO, N_ZHI * N_Y * 2
GROUP, SAMP = 2048, 128
BLOCK = N_LEV * SAMP
FEAT = 4 * LEV + 2 * LEV * LEV
ROWS_OUT, COLS_OUT = FEAT // N_HOR, FEAT // N_LEV
CHUNK, BOTH, HALF = 72, 2 * ROWS_OUT, 16
WINDOWS = (CHUNK, CHUNK, BOTH)
BUILT = sum(WINDOWS) + 8 * len(WINDOWS)
LAST = 2 * CHUNK + 16
REST = 2 * (CHUNK + BOTH)
SENT = LAST + REST + 32
SHARE = 1 << 18
VMEM = pl.BlockSpec(memory_space=pltpu.VMEM)


def params(mib):
    return pltpu.CompilerParams(vmem_limit_bytes=mib << 20)


def cost(flops, moved):
    return pl.CostEstimate(flops=flops, bytes_accessed=moved, transcendentals=0)


def shift_lev(value, step_zlo, step_x):
    pairs = [(i, (i // N_X ^ step_zlo) * N_X + (i + step_x) % N_X) for i in range(N_LEV)]
    return lax.ppermute(value, "lev", pairs)


def swap_cores(value):
    return lax.ppermute(value, "hor", [(i, i ^ 1) for i in range(N_HOR)])


def hop(value, axis, cross):
    pairs = []
    for i in range(N_HOR):
        zhi, y, core = i // (2 * N_Y), i // 2 % N_Y, i % 2
        ahead = 1 - 2 * core
        if axis == "y":
            y = (y + ahead) % N_Y
        else:
            zhi = (zhi + ahead) % N_ZHI
        pairs.append((i, zhi * 2 * N_Y + y * 2 + (core ^ cross)))
    return lax.ppermute(value, "hor", pairs)


def repeat_kernel(index_ref, out_ref):
    for lev in range(N_LEV):
        out_ref[lev] = index_ref[...]


def stage_kernel(slab_ref, out_ref):
    for slot in range(SLOTS):
        out_ref[4 * slot : 4 * slot + 4, :] = slab_ref[slot]


def pick_kernel(index_ref, slab_ref, out_ref):
    for group in range(N_LEV):
        index = jnp.broadcast_to(index_ref[group], (8, LANES))
        lane, tile = index % LANES, index // LANES
        hits = [tile == t for t in range(GROUP // LANES)]
        for pair in range(2):
            rows = slice(8 * pair, 8 * pair + 8)
            total = jnp.zeros((8, LANES), jnp.float32)
            for t in range(GROUP // LANES):
                at = slice(group * GROUP + t * LANES, group * GROUP + (t + 1) * LANES)
                total = jnp.where(hits[t], jnp.take_along_axis(slab_ref[rows, at], lane, axis=1), total)
            out_ref[rows, group * SAMP : (group + 1) * SAMP] = total


def smooth_kernel(coef_ref, w0_ref, w2_ref, w1_ref, w3_ref, out_ref, raw_ref):
    x = lax.axis_index("lev") % N_X
    for step, ref in enumerate((w0_ref, w1_ref, w2_ref, w3_ref)):
        source = lax.rem(x - step + N_X, N_X)
        for zlo in range(N_ZLO):
            raw_ref[zlo * N_X + source] = ref[zlo]

    def tile(t, carry):
        at = pl.ds(pl.multiple_of(t * LANES, LANES), LANES)
        for slot in range(SLOTS):
            rows = [raw_ref[lev, 4 * slot : 4 * slot + 4, at] for lev in range(N_LEV)]
            value = jnp.concatenate(rows, axis=0)
            below, above = pltpu.roll(value, 1, 0), pltpu.roll(value, LEV - 1, 0)
            out_ref[slot * LEV : (slot + 1) * LEV, at] = (
                coef_ref[0:LEV] * value + coef_ref[LEV : 2 * LEV] * below + coef_ref[2 * LEV :] * above
            )
        return carry

    lax.fori_loop(0, BLOCK // LANES, tile, 0)


def build_rows(smooth_ref, half, out_ref, at):
    late = 2 * LEV
    m = jnp.maximum(half - 4 * LEV // HALF, 0) // 2
    product = smooth_ref[pl.ds(late + m, 1), :] * smooth_ref[pl.ds(pl.multiple_of(half % 2 * HALF, HALF), HALF), :]
    linear = smooth_ref[pl.ds(pl.multiple_of((late + half * HALF) % (4 * LEV), HALF), HALF), :]
    rows = jnp.where(half < 4 * LEV // HALF, linear, product)
    out_ref[at : at + HALF, :] = rows.astype(jnp.bfloat16)


def build_right(smooth_ref, out_ref):
    lev = lax.axis_index("lev")
    for i in range(COLS_OUT // HALF):
        build_rows(smooth_ref, lev * (COLS_OUT // HALF) + i, out_ref, i * HALF)


def windows_of(place):
    hor = lax.axis_index("hor")
    zhi, y, core = hor // (2 * N_Y), hor // 2 % N_Y, hor % 2
    to_y = {"far": y + 2, "cross": y + 5 - 2 * core, "near": y + 5 - 2 * core, "own": y}[place]
    to_y = lax.rem(to_y, N_Y)
    to_core = 1 - core if place == "cross" else core
    skip = 8 * lax.rem(to_y, 2)

    def start(to_z, offset):
        return (lax.rem(to_z, N_ZHI) * N_Y + to_y) * BOTH + offset - skip

    return (start(zhi + 2, 64 * to_core), start(zhi, 64 * to_core), start(zhi + 5 - 2 * to_core, 0)), skip


def product(place, smooth_ref, right_ref, left_ref):
    at = 0
    for first, size in zip(windows_of(place)[0], WINDOWS):
        for i in range((size + 8) // HALF):
            build_rows(smooth_ref, first // HALF + i, left_ref, at)
            at += HALF
    return lax.dot_general(
        left_ref[...], right_ref[...], (((1,), (1,)), ((), ())), preferred_element_type=jnp.float32
    )


def emit(place, prod_ref, out_ref):
    skip = windows_of(place)[1]
    at, base, group, tail = 0, 0, 0, 2 * CHUNK
    for number, size in enumerate(WINDOWS):
        if number == 1:
            base, group, tail = LAST, 0, LAST + REST
        for half in range(2):
            rows = pl.ds(pl.multiple_of(at + skip, 8), size)
            out_ref[base : base + size, :] = prod_ref[rows, half * LANES : (half + 1) * LANES]
            base += size
        for i in range(size // 8):
            rows = pl.ds(pl.multiple_of(at + 8 * i + skip, 8), 8)
            to = tail + 8 * (group // 8)
            strip = 16 * (group % 8)
            out_ref[to : to + 8, strip : strip + 16] = prod_ref[rows, 2 * LANES : COLS_OUT]
            group += 1
        at += size + 8


def begin_kernel(place, smooth_ref, out_ref, right_ref, left_ref):
    build_right(smooth_ref, right_ref)
    out_ref[...] = product(place, smooth_ref, right_ref, left_ref)


def finish_kernel(place, part_ref, smooth_ref, out_ref, right_ref, left_ref, prod_ref):
    build_right(smooth_ref, right_ref)
    prod_ref[...] = part_ref[...] + product(place, smooth_ref, right_ref, left_ref)
    emit(place, prod_ref, out_ref)


def gram_kernel(place, own_ref, own_right_ref, other_ref, other_right_ref, out_ref, left_ref, prod_ref):
    prod_ref[...] = product(place, own_ref, own_right_ref, left_ref)
    prod_ref[...] += product(place, other_ref, other_right_ref, left_ref)
    emit(place, prod_ref, out_ref)


def add_kernel(a_ref, b_ref, out_ref):
    out_ref[...] = a_ref[...] + b_ref[...]


def cut_kernel(a_ref, b_ref, far_ref, rest_ref):
    far_ref[...] = a_ref[0:LAST, :] + b_ref[0:LAST, :]
    rest_ref[...] = a_ref[LAST:SENT, :] + b_ref[LAST:SENT, :]


def split_kernel(a_ref, b_ref, own_ref, near_ref, cross_ref):
    core = lax.axis_index("hor") % 2
    lane = lax.broadcasted_iota(jnp.int32, (8, LANES), 1)

    def total(start, size):
        rows = pl.ds(start if isinstance(start, int) else pl.multiple_of(start, 8), size)
        return a_ref[rows, :] + b_ref[rows, :]

    ahead = 2 * CHUNK
    places = (
        (near_ref, ahead + 64 * core, BOTH, 1 + core, 1),
        (cross_ref, ahead + 64 * (1 - core), BOTH, 2 - core, 1),
        (own_ref, 0, CHUNK, 0, 0),
    )
    for ref, start, stride, tile, strip in places:
        ref[0:CHUNK, :] = total(start, CHUNK)
        ref[CHUNK : 2 * CHUNK, :] = total(start + stride, CHUNK)
        one, two = total(REST + 8 * tile, 8), total(REST + 8 * tile + 8, 8)
        if strip:
            one, two = pltpu.roll(one, LANES - 16 * strip, 1), pltpu.roll(two, LANES - 16 * strip, 1)
            one = jnp.where(lane < LANES - 16 * strip, one, two)
        ref[2 * CHUNK : 2 * CHUNK + 8, :] = one
        ref[2 * CHUNK + 8 : LAST, :] = two


def final_kernel(t0_ref, t1_ref, t2_ref, out_ref):
    odd = lax.axis_index("hor") % 2 == 1
    scale = 1.0 / (BLOCK * N_HOR)

    def total(rows):
        return (t0_ref[rows, :] + t1_ref[rows, :]) + t2_ref[rows, :]

    def place(value):
        return jnp.where(odd, value[CHUNK - ROWS_OUT : CHUNK], value[0:ROWS_OUT]) * scale

    for half in range(2):
        value = total(slice(half * CHUNK, (half + 1) * CHUNK))
        out_ref[:, half * LANES : (half + 1) * LANES] = place(value)
    packed = total(slice(2 * CHUNK, 2 * CHUNK + 8))
    rest = [pltpu.roll(packed, -16 * group % LANES, 1) for group in range(8)]
    rest.append(total(slice(2 * CHUNK + 8, LAST)))
    out_ref[:, 2 * LANES :] = place(jnp.concatenate(rest, axis=0))[:, :16]


def filter_coefficients(thickness, level_cuts):
    link = 1.0 - level_cuts.astype(jnp.float32)
    zero_one = jnp.zeros((1,), jnp.float32)
    lower = jnp.concatenate([zero_one, thickness[:-1] * link])
    upper = jnp.concatenate([thickness[1:] * link, zero_one])
    denom = 2.0 * thickness + lower + upper
    coef = jnp.concatenate([2.0 * thickness / denom, lower / denom, upper / denom])
    return jnp.broadcast_to(coef[:, None], (3 * LEV, LANES))


def gram(kernel, place, out_shape, *operands):
    scratch = [pltpu.VMEM((BUILT, BLOCK), jnp.bfloat16), pltpu.VMEM((BUILT, COLS_OUT), jnp.float32)]
    return pl.pallas_call(
        functools.partial(kernel, place),
        out_shape=out_shape,
        in_specs=[VMEM] * len(operands),
        out_specs=jax.tree.map(lambda _: VMEM, out_shape),
        scratch_shapes=scratch[:1] if kernel is begin_kernel else scratch,
        compiler_params=params(12),
        cost_estimate=cost(1, SHARE),
        name="gram_" + place,
    )(*operands)


def add(a, b, share=1):
    return pl.pallas_call(
        add_kernel,
        out_shape=jax.ShapeDtypeStruct(a.shape, a.dtype),
        in_specs=[VMEM] * 2,
        out_specs=VMEM,
        compiler_params=params(4),
        cost_estimate=cost(share, SHARE),
        name="add",
    )(a, b)


def cut(a, b):
    shapes = ((LAST, LANES), (SENT - LAST, LANES))
    return pl.pallas_call(
        cut_kernel,
        out_shape=[jax.ShapeDtypeStruct(shape, a.dtype) for shape in shapes],
        in_specs=[VMEM] * 2,
        out_specs=[VMEM] * 2,
        compiler_params=params(4),
        cost_estimate=cost(1, SHARE),
        name="cut",
    )(a, b)


def on_device(slab_fields, sample_index, thickness, level_cuts):
    f32 = jnp.float32
    coef = filter_coefficients(thickness, level_cuts)
    repeated = pl.pallas_call(
        repeat_kernel,
        out_shape=jax.ShapeDtypeStruct((N_LEV, 1, SAMP), jnp.int32),
        in_specs=[VMEM],
        out_specs=VMEM,
        compiler_params=params(60),
        name="repeat",
    )(sample_index)
    lists = lax.all_to_all(repeated, "lev", 0, 0, tiled=True)
    staged = pl.pallas_call(
        stage_kernel,
        out_shape=jax.ShapeDtypeStruct((4 * SLOTS, N_LEV * GROUP), f32),
        in_specs=[VMEM],
        out_specs=VMEM,
        compiler_params=params(8),
        cost_estimate=cost(0, 2 << 20),
        name="stage",
    )(slab_fields)
    picked = pl.pallas_call(
        pick_kernel,
        out_shape=jax.ShapeDtypeStruct((4 * SLOTS, BLOCK), f32),
        in_specs=[VMEM] * 2,
        out_specs=VMEM,
        compiler_params=params(8),
        name="pick",
    )(lists, staged)
    across = shift_lev(picked, 1, 0)
    up = lax.axis_index("lev") // N_X == 1
    near = jnp.stack([jnp.where(up, across, picked), jnp.where(up, picked, across)])
    far = {k: shift_lev(near, 0, k) for k in (2, 1, 3)}
    own = pl.pallas_call(
        smooth_kernel,
        out_shape=jax.ShapeDtypeStruct((SLOTS * LEV, BLOCK), f32),
        in_specs=[VMEM] * 5,
        out_specs=VMEM,
        scratch_shapes=[pltpu.VMEM((N_LEV, 4 * SLOTS, BLOCK), f32)],
        compiler_params=params(16),
        name="smooth",
    )(coef, near, far[2], far[1], far[3])
    other = swap_cores(own)
    right = jax.ShapeDtypeStruct((COLS_OUT, BLOCK), jnp.bfloat16)
    begun, own_right = gram(begin_kernel, "far", [jax.ShapeDtypeStruct((BUILT, COLS_OUT), f32), right], own)
    sent = jax.ShapeDtypeStruct((SENT, LANES), f32)
    far, other_right = gram(finish_kernel, "far", [sent, right], begun, other)
    parts = {"far": far}
    both = (own, own_right, other, other_right)
    parts["cross"] = gram(gram_kernel, "cross", sent, *both)
    both, parts["cross"] = lax.optimization_barrier((both, parts["cross"]))
    parts["near"] = gram(gram_kernel, "near", sent, *both)
    parts["own"] = gram(gram_kernel, "own", sent, *both)
    two_back = hop(parts["far"], "y", 0)
    from_cross = hop(parts["cross"], "y", 1)
    near_far, near_rest = cut(parts["near"], two_back)
    from_near_far, from_near_rest = hop(near_far, "y", 0), hop(near_rest, "y", 0)
    sum_far, sum_rest = cut(parts["own"], from_cross)
    two_back = hop(add(sum_far, from_near_far, 1 << 30), "z_hi", 0)
    kept, near, cross = pl.pallas_call(
        split_kernel,
        out_shape=[jax.ShapeDtypeStruct((LAST, LANES), f32)] * 3,
        in_specs=[VMEM] * 2,
        out_specs=[VMEM] * 3,
        compiler_params=params(8),
        cost_estimate=cost(1, SHARE),
        name="split",
    )(sum_rest, from_near_rest)
    from_cross = hop(cross, "z_hi", 1)
    from_near = hop(add(near, two_back), "z_hi", 0)
    return pl.pallas_call(
        final_kernel,
        out_shape=jax.ShapeDtypeStruct((ROWS_OUT, COLS_OUT), f32),
        in_specs=[VMEM] * 3,
        out_specs=VMEM,
        compiler_params=params(8),
        cost_estimate=cost(1, SHARE),
        name="final",
    )(kept, from_cross, from_near)


def solution(mesh):
    in_specs = (P(None, "lev", "hor"), P("hor", "lev"), P(), P())
    out_specs = P("hor", "lev")
    return jax.shard_map(on_device, mesh=mesh, in_specs=in_specs, out_specs=out_specs, check_vma=False)
```

```python
import functools

import jax
import jax.numpy as jnp
from jax import lax
from jax.experimental import pallas as pl
from jax.experimental.pallas import tpu as pltpu
from jax.sharding import PartitionSpec as P

LEV, SLOTS, LANES = 32, 4, 128
N_X, N_ZLO, N_Y, N_ZHI = 4, 2, 4, 4
N_LEV, N_HOR = N_X * N_ZLO, N_ZHI * N_Y * 2
GROUP, SAMP = 2048, 128
BLOCK = N_LEV * SAMP
FEAT = 4 * LEV + 2 * LEV * LEV
ROWS_OUT, COLS_OUT = FEAT // N_HOR, FEAT // N_LEV
CHUNK, BOTH, HALF = 72, 2 * ROWS_OUT, 16
WINDOWS = (CHUNK, CHUNK, BOTH)
BUILT = sum(WINDOWS) + 8 * len(WINDOWS)
LAST = 2 * CHUNK + 16
REST = 2 * (CHUNK + BOTH)
SENT = LAST + REST + 32
SHARE = 1 << 18
VMEM = pl.BlockSpec(memory_space=pltpu.VMEM)


def params(mib):
    return pltpu.CompilerParams(vmem_limit_bytes=mib << 20)


def cost(flops, moved):
    return pl.CostEstimate(flops=flops, bytes_accessed=moved, transcendentals=0)


def shift_lev(value, step_zlo, step_x):
    pairs = [(i, (i // N_X ^ step_zlo) * N_X + (i + step_x) % N_X) for i in range(N_LEV)]
    return lax.ppermute(value, "lev", pairs)


def swap_cores(value):
    return lax.ppermute(value, "hor", [(i, i ^ 1) for i in range(N_HOR)])


def hop(value, axis, cross):
    pairs = []
    for i in range(N_HOR):
        zhi, y, core = i // (2 * N_Y), i // 2 % N_Y, i % 2
        ahead = 1 - 2 * core
        if axis == "y":
            y = (y + ahead) % N_Y
        else:
            zhi = (zhi + ahead) % N_ZHI
        pairs.append((i, zhi * 2 * N_Y + y * 2 + (core ^ cross)))
    return lax.ppermute(value, "hor", pairs)


def repeat_kernel(index_ref, out_ref):
    for lev in range(N_LEV):
        out_ref[lev] = index_ref[...]


def stage_kernel(slab_ref, out_ref):
    for slot in range(SLOTS):
        out_ref[4 * slot : 4 * slot + 4, :] = slab_ref[slot]


def pick_kernel(index_ref, slab_ref, out_ref):
    for group in range(N_LEV):
        index = jnp.broadcast_to(index_ref[group], (8, LANES))
        lane, tile = index % LANES, index // LANES
        hits = [tile == t for t in range(GROUP // LANES)]
        for pair in range(2):
            rows = slice(8 * pair, 8 * pair + 8)
            total = jnp.zeros((8, LANES), jnp.float32)
            for t in range(GROUP // LANES):
                at = slice(group * GROUP + t * LANES, group * GROUP + (t + 1) * LANES)
                total = jnp.where(hits[t], jnp.take_along_axis(slab_ref[rows, at], lane, axis=1), total)
            out_ref[rows, group * SAMP : (group + 1) * SAMP] = total


def smooth_kernel(coef_ref, w0_ref, w3_ref, w1_ref, w2_ref, out_ref, raw_ref):
    x = lax.axis_index("lev") % N_X
    for step, ref in enumerate((w0_ref, w1_ref, w2_ref, w3_ref)):
        source = lax.rem(x - step + N_X, N_X)
        for zlo in range(N_ZLO):
            raw_ref[zlo * N_X + source] = ref[zlo]

    def tile(t, carry):
        at = pl.ds(pl.multiple_of(t * LANES, LANES), LANES)
        for slot in range(SLOTS):
            rows = [raw_ref[lev, 4 * slot : 4 * slot + 4, at] for lev in range(N_LEV)]
            value = jnp.concatenate(rows, axis=0)
            below, above = pltpu.roll(value, 1, 0), pltpu.roll(value, LEV - 1, 0)
            out_ref[slot * LEV : (slot + 1) * LEV, at] = (
                coef_ref[0:LEV] * value + coef_ref[LEV : 2 * LEV] * below + coef_ref[2 * LEV :] * above
            )
        return carry

    lax.fori_loop(0, BLOCK // LANES, tile, 0)


def build_rows(smooth_ref, half, out_ref, at):
    late = 2 * LEV
    m = jnp.maximum(half - 4 * LEV // HALF, 0) // 2
    product = smooth_ref[pl.ds(late + m, 1), :] * smooth_ref[pl.ds(pl.multiple_of(half % 2 * HALF, HALF), HALF), :]
    linear = smooth_ref[pl.ds(pl.multiple_of((late + half * HALF) % (4 * LEV), HALF), HALF), :]
    rows = jnp.where(half < 4 * LEV // HALF, linear, product)
    out_ref[at : at + HALF, :] = rows.astype(jnp.bfloat16)


def build_right(smooth_ref, out_ref):
    lev = lax.axis_index("lev")
    for i in range(COLS_OUT // HALF):
        build_rows(smooth_ref, lev * (COLS_OUT // HALF) + i, out_ref, i * HALF)


def windows_of(place):
    hor = lax.axis_index("hor")
    zhi, y, core = hor // (2 * N_Y), hor // 2 % N_Y, hor % 2
    to_y = {"far": y + 2, "cross": y + 5 - 2 * core, "near": y + 5 - 2 * core, "own": y}[place]
    to_y = lax.rem(to_y, N_Y)
    to_core = 1 - core if place == "cross" else core
    skip = 8 * lax.rem(to_y, 2)

    def start(to_z, offset):
        return (lax.rem(to_z, N_ZHI) * N_Y + to_y) * BOTH + offset - skip

    return (start(zhi + 2, 64 * to_core), start(zhi, 64 * to_core), start(zhi + 5 - 2 * to_core, 0)), skip


def product(place, smooth_ref, right_ref, left_ref):
    at = 0
    for first, size in zip(windows_of(place)[0], WINDOWS):
        for i in range((size + 8) // HALF):
            build_rows(smooth_ref, first // HALF + i, left_ref, at)
            at += HALF
    return lax.dot_general(
        left_ref[...], right_ref[...], (((1,), (1,)), ((), ())), preferred_element_type=jnp.float32
    )


def emit(place, prod_ref, out_ref):
    skip = windows_of(place)[1]
    at, base, group, tail = 0, 0, 0, 2 * CHUNK
    for number, size in enumerate(WINDOWS):
        if number == 1:
            base, group, tail = LAST, 0, LAST + REST
        for half in range(2):
            rows = pl.ds(pl.multiple_of(at + skip, 8), size)
            out_ref[base : base + size, :] = prod_ref[rows, half * LANES : (half + 1) * LANES]
            base += size
        for i in range(size // 8):
            rows = pl.ds(pl.multiple_of(at + 8 * i + skip, 8), 8)
            to = tail + 8 * (group // 8)
            strip = 16 * (group % 8)
            out_ref[to : to + 8, strip : strip + 16] = prod_ref[rows, 2 * LANES : COLS_OUT]
            group += 1
        at += size + 8


def begin_kernel(place, smooth_ref, out_ref, right_ref, left_ref):
    build_right(smooth_ref, right_ref)
    out_ref[...] = product(place, smooth_ref, right_ref, left_ref)


def finish_kernel(place, part_ref, smooth_ref, out_ref, right_ref, left_ref, prod_ref):
    build_right(smooth_ref, right_ref)
    prod_ref[...] = part_ref[...] + product(place, smooth_ref, right_ref, left_ref)
    emit(place, prod_ref, out_ref)


def gram_kernel(place, own_ref, own_right_ref, other_ref, other_right_ref, out_ref, left_ref, prod_ref):
    prod_ref[...] = product(place, own_ref, own_right_ref, left_ref)
    prod_ref[...] += product(place, other_ref, other_right_ref, left_ref)
    emit(place, prod_ref, out_ref)


def add_kernel(a_ref, b_ref, out_ref):
    out_ref[...] = a_ref[...] + b_ref[...]


def cut_kernel(a_ref, b_ref, far_ref, rest_ref):
    far_ref[...] = a_ref[0:LAST, :] + b_ref[0:LAST, :]
    rest_ref[...] = a_ref[LAST:SENT, :] + b_ref[LAST:SENT, :]


def split_kernel(a_ref, b_ref, own_ref, near_ref, cross_ref):
    core = lax.axis_index("hor") % 2
    lane = lax.broadcasted_iota(jnp.int32, (8, LANES), 1)

    def total(start, size):
        rows = pl.ds(start if isinstance(start, int) else pl.multiple_of(start, 8), size)
        return a_ref[rows, :] + b_ref[rows, :]

    ahead = 2 * CHUNK
    places = (
        (near_ref, ahead + 64 * core, BOTH, 1 + core, 1),
        (cross_ref, ahead + 64 * (1 - core), BOTH, 2 - core, 1),
        (own_ref, 0, CHUNK, 0, 0),
    )
    for ref, start, stride, tile, strip in places:
        ref[0:CHUNK, :] = total(start, CHUNK)
        ref[CHUNK : 2 * CHUNK, :] = total(start + stride, CHUNK)
        one, two = total(REST + 8 * tile, 8), total(REST + 8 * tile + 8, 8)
        if strip:
            one, two = pltpu.roll(one, LANES - 16 * strip, 1), pltpu.roll(two, LANES - 16 * strip, 1)
            one = jnp.where(lane < LANES - 16 * strip, one, two)
        ref[2 * CHUNK : 2 * CHUNK + 8, :] = one
        ref[2 * CHUNK + 8 : LAST, :] = two


def final_kernel(t0_ref, t1_ref, t2_ref, out_ref):
    odd = lax.axis_index("hor") % 2 == 1
    scale = 1.0 / (BLOCK * N_HOR)

    def total(rows):
        return (t0_ref[rows, :] + t1_ref[rows, :]) + t2_ref[rows, :]

    def place(value):
        return jnp.where(odd, value[CHUNK - ROWS_OUT : CHUNK], value[0:ROWS_OUT]) * scale

    for half in range(2):
        value = total(slice(half * CHUNK, (half + 1) * CHUNK))
        out_ref[:, half * LANES : (half + 1) * LANES] = place(value)
    packed = total(slice(2 * CHUNK, 2 * CHUNK + 8))
    rest = [pltpu.roll(packed, -16 * group % LANES, 1) for group in range(8)]
    rest.append(total(slice(2 * CHUNK + 8, LAST)))
    out_ref[:, 2 * LANES :] = place(jnp.concatenate(rest, axis=0))[:, :16]


def filter_coefficients(thickness, level_cuts):
    link = 1.0 - level_cuts.astype(jnp.float32)
    zero_one = jnp.zeros((1,), jnp.float32)
    lower = jnp.concatenate([zero_one, thickness[:-1] * link])
    upper = jnp.concatenate([thickness[1:] * link, zero_one])
    denom = 2.0 * thickness + lower + upper
    coef = jnp.concatenate([2.0 * thickness / denom, lower / denom, upper / denom])
    return jnp.broadcast_to(coef[:, None], (3 * LEV, LANES))


def gram(kernel, place, out_shape, *operands):
    scratch = [pltpu.VMEM((BUILT, BLOCK), jnp.bfloat16), pltpu.VMEM((BUILT, COLS_OUT), jnp.float32)]
    return pl.pallas_call(
        functools.partial(kernel, place),
        out_shape=out_shape,
        in_specs=[VMEM] * len(operands),
        out_specs=jax.tree.map(lambda _: VMEM, out_shape),
        scratch_shapes=scratch[:1] if kernel is begin_kernel else scratch,
        compiler_params=params(12),
        cost_estimate=cost(1, SHARE),
        name="gram_" + place,
    )(*operands)


def add(a, b, share=1):
    return pl.pallas_call(
        add_kernel,
        out_shape=jax.ShapeDtypeStruct(a.shape, a.dtype),
        in_specs=[VMEM] * 2,
        out_specs=VMEM,
        compiler_params=params(4),
        cost_estimate=cost(share, SHARE),
        name="add",
    )(a, b)


def cut(a, b):
    shapes = ((LAST, LANES), (SENT - LAST, LANES))
    return pl.pallas_call(
        cut_kernel,
        out_shape=[jax.ShapeDtypeStruct(shape, a.dtype) for shape in shapes],
        in_specs=[VMEM] * 2,
        out_specs=[VMEM] * 2,
        compiler_params=params(4),
        cost_estimate=cost(1, SHARE),
        name="cut",
    )(a, b)


def on_device(slab_fields, sample_index, thickness, level_cuts):
    f32 = jnp.float32
    coef = filter_coefficients(thickness, level_cuts)
    repeated = pl.pallas_call(
        repeat_kernel,
        out_shape=jax.ShapeDtypeStruct((N_LEV, 1, SAMP), jnp.int32),
        in_specs=[VMEM],
        out_specs=VMEM,
        compiler_params=params(60),
        name="repeat",
    )(sample_index)
    lists = lax.all_to_all(repeated, "lev", 0, 0, tiled=True)
    staged = pl.pallas_call(
        stage_kernel,
        out_shape=jax.ShapeDtypeStruct((4 * SLOTS, N_LEV * GROUP), f32),
        in_specs=[VMEM],
        out_specs=VMEM,
        compiler_params=params(8),
        cost_estimate=cost(0, 2 << 20),
        name="stage",
    )(slab_fields)
    picked = pl.pallas_call(
        pick_kernel,
        out_shape=jax.ShapeDtypeStruct((4 * SLOTS, BLOCK), f32),
        in_specs=[VMEM] * 2,
        out_specs=VMEM,
        compiler_params=params(8),
        name="pick",
    )(lists, staged)
    across = shift_lev(picked, 1, 0)
    up = lax.axis_index("lev") // N_X == 1
    near = jnp.stack([jnp.where(up, across, picked), jnp.where(up, picked, across)])
    far = {k: shift_lev(near, 0, k) for k in (2, 1, 3)}
    own = pl.pallas_call(
        smooth_kernel,
        out_shape=jax.ShapeDtypeStruct((SLOTS * LEV, BLOCK), f32),
        in_specs=[VMEM] * 5,
        out_specs=VMEM,
        scratch_shapes=[pltpu.VMEM((N_LEV, 4 * SLOTS, BLOCK), f32)],
        compiler_params=params(16),
        name="smooth",
    )(coef, near, far[3], far[1], far[2])
    other = swap_cores(own)
    right = jax.ShapeDtypeStruct((COLS_OUT, BLOCK), jnp.bfloat16)
    begun, own_right = gram(begin_kernel, "far", [jax.ShapeDtypeStruct((BUILT, COLS_OUT), f32), right], own)
    sent = jax.ShapeDtypeStruct((SENT, LANES), f32)
    far, other_right = gram(finish_kernel, "far", [sent, right], begun, other)
    parts = {"far": far}
    both = (own, own_right, other, other_right)
    parts["cross"] = gram(gram_kernel, "cross", sent, *both)
    both, parts["cross"] = lax.optimization_barrier((both, parts["cross"]))
    parts["near"] = gram(gram_kernel, "near", sent, *both)
    parts["own"] = gram(gram_kernel, "own", sent, *both)
    two_back = hop(parts["far"], "y", 0)
    from_cross = hop(parts["cross"], "y", 1)
    near_far, near_rest = cut(parts["near"], two_back)
    from_near_far, from_near_rest = hop(near_far, "y", 0), hop(near_rest, "y", 0)
    sum_far, sum_rest = cut(parts["own"], from_cross)
    two_back = hop(add(sum_far, from_near_far, 1 << 30), "z_hi", 0)
    kept, near, cross = pl.pallas_call(
        split_kernel,
        out_shape=[jax.ShapeDtypeStruct((LAST, LANES), f32)] * 3,
        in_specs=[VMEM] * 2,
        out_specs=[VMEM] * 3,
        compiler_params=params(8),
        cost_estimate=cost(1, SHARE),
        name="split",
    )(sum_rest, from_near_rest)
    from_cross = hop(cross, "z_hi", 1)
    from_near = hop(add(near, two_back), "z_hi", 0)
    return pl.pallas_call(
        final_kernel,
        out_shape=jax.ShapeDtypeStruct((ROWS_OUT, COLS_OUT), f32),
        in_specs=[VMEM] * 3,
        out_specs=VMEM,
        compiler_params=params(8),
        cost_estimate=cost(1, SHARE),
        name="final",
    )(kept, from_cross, from_near)


def solution(mesh):
    in_specs = (P(None, "lev", "hor"), P("hor", "lev"), P(), P())
    out_specs = P("hor", "lev")
    return jax.shard_map(on_device, mesh=mesh, in_specs=in_specs, out_specs=out_specs, check_vma=False)
```

```python
import functools

import jax
import jax.numpy as jnp
from jax import lax
from jax.experimental import pallas as pl
from jax.experimental.pallas import tpu as pltpu
from jax.sharding import PartitionSpec as P

LEV, SLOTS, LANES = 32, 4, 128
N_X, N_ZLO, N_Y, N_ZHI = 4, 2, 4, 4
N_LEV, N_HOR = N_X * N_ZLO, N_ZHI * N_Y * 2
GROUP, SAMP = 2048, 128
BLOCK = N_LEV * SAMP
FEAT = 4 * LEV + 2 * LEV * LEV
ROWS_OUT, COLS_OUT = FEAT // N_HOR, FEAT // N_LEV
CHUNK, BOTH, HALF = 72, 2 * ROWS_OUT, 16
WINDOWS = (CHUNK, CHUNK, BOTH)
BUILT = sum(WINDOWS) + 8 * len(WINDOWS)
LAST = 2 * CHUNK + 16
REST = 2 * (CHUNK + BOTH)
SENT = LAST + REST + 32
SHARE = 1 << 18
VMEM = pl.BlockSpec(memory_space=pltpu.VMEM)


def params(mib):
    return pltpu.CompilerParams(vmem_limit_bytes=mib << 20)


def cost(flops, moved):
    return pl.CostEstimate(flops=flops, bytes_accessed=moved, transcendentals=0)


def shift_lev(value, step_zlo, step_x):
    pairs = [(i, (i // N_X ^ step_zlo) * N_X + (i + step_x) % N_X) for i in range(N_LEV)]
    return lax.ppermute(value, "lev", pairs)


def swap_cores(value):
    return lax.ppermute(value, "hor", [(i, i ^ 1) for i in range(N_HOR)])


def hop(value, axis, cross):
    pairs = []
    for i in range(N_HOR):
        zhi, y, core = i // (2 * N_Y), i // 2 % N_Y, i % 2
        ahead = 1 - 2 * core
        if axis == "y":
            y = (y + ahead) % N_Y
        else:
            zhi = (zhi + ahead) % N_ZHI
        pairs.append((i, zhi * 2 * N_Y + y * 2 + (core ^ cross)))
    return lax.ppermute(value, "hor", pairs)


def repeat_kernel(index_ref, out_ref):
    for lev in range(N_LEV):
        out_ref[lev] = index_ref[...]


def stage_kernel(slab_ref, out_ref):
    for slot in range(SLOTS):
        out_ref[4 * slot : 4 * slot + 4, :] = slab_ref[slot]


def pick_kernel(index_ref, slab_ref, out_ref):
    for group in range(N_LEV):
        index = jnp.broadcast_to(index_ref[group], (8, LANES))
        lane, tile = index % LANES, index // LANES
        hits = [tile == t for t in range(GROUP // LANES)]
        for pair in range(2):
            rows = slice(8 * pair, 8 * pair + 8)
            total = jnp.zeros((8, LANES), jnp.float32)
            for t in range(GROUP // LANES):
                at = slice(group * GROUP + t * LANES, group * GROUP + (t + 1) * LANES)
                total = jnp.where(hits[t], jnp.take_along_axis(slab_ref[rows, at], lane, axis=1), total)
            out_ref[rows, group * SAMP : (group + 1) * SAMP] = total


def smooth_kernel(coef_ref, w0_ref, w3_ref, w1_ref, w2_ref, out_ref, raw_ref):
    x = lax.axis_index("lev") % N_X
    for step, ref in enumerate((w0_ref, w1_ref, w2_ref, w3_ref)):
        source = lax.rem(x - step + N_X, N_X)
        for zlo in range(N_ZLO):
            raw_ref[zlo * N_X + source] = ref[zlo]

    def tile(t, carry):
        at = pl.ds(pl.multiple_of(t * LANES, LANES), LANES)
        for slot in range(SLOTS):
            rows = [raw_ref[lev, 4 * slot : 4 * slot + 4, at] for lev in range(N_LEV)]
            value = jnp.concatenate(rows, axis=0)
            below, above = pltpu.roll(value, 1, 0), pltpu.roll(value, LEV - 1, 0)
            out_ref[slot * LEV : (slot + 1) * LEV, at] = (
                coef_ref[0:LEV] * value + coef_ref[LEV : 2 * LEV] * below + coef_ref[2 * LEV :] * above
            )
        return carry

    lax.fori_loop(0, BLOCK // LANES, tile, 0)


def build_rows(smooth_ref, half, out_ref, at):
    late = 2 * LEV
    m = jnp.maximum(half - 4 * LEV // HALF, 0) // 2
    product = smooth_ref[pl.ds(late + m, 1), :] * smooth_ref[pl.ds(pl.multiple_of(half % 2 * HALF, HALF), HALF), :]
    linear = smooth_ref[pl.ds(pl.multiple_of((late + half * HALF) % (4 * LEV), HALF), HALF), :]
    rows = jnp.where(half < 4 * LEV // HALF, linear, product)
    out_ref[at : at + HALF, :] = rows.astype(jnp.bfloat16)


def build_right(smooth_ref, out_ref):
    lev = lax.axis_index("lev")
    for i in range(COLS_OUT // HALF):
        build_rows(smooth_ref, lev * (COLS_OUT // HALF) + i, out_ref, i * HALF)


def windows_of(place):
    hor = lax.axis_index("hor")
    zhi, y, core = hor // (2 * N_Y), hor // 2 % N_Y, hor % 2
    to_y = {"far": y + 2, "cross": y + 5 - 2 * core, "near": y + 5 - 2 * core, "own": y}[place]
    to_y = lax.rem(to_y, N_Y)
    to_core = 1 - core if place == "cross" else core
    skip = 8 * lax.rem(to_y, 2)

    def start(to_z, offset):
        return (lax.rem(to_z, N_ZHI) * N_Y + to_y) * BOTH + offset - skip

    return (start(zhi + 2, 64 * to_core), start(zhi, 64 * to_core), start(zhi + 5 - 2 * to_core, 0)), skip


def product(place, smooth_ref, right_ref, left_ref):
    at = 0
    for first, size in zip(windows_of(place)[0], WINDOWS):
        for i in range((size + 8) // HALF):
            build_rows(smooth_ref, first // HALF + i, left_ref, at)
            at += HALF
    return lax.dot_general(
        left_ref[...], right_ref[...], (((1,), (1,)), ((), ())), preferred_element_type=jnp.float32
    )


def emit(place, prod_ref, out_ref):
    skip = windows_of(place)[1]
    at, base, group, tail = 0, 0, 0, 2 * CHUNK
    for number, size in enumerate(WINDOWS):
        if number == 1:
            base, group, tail = LAST, 0, LAST + REST
        for half in range(2):
            rows = pl.ds(pl.multiple_of(at + skip, 8), size)
            out_ref[base : base + size, :] = prod_ref[rows, half * LANES : (half + 1) * LANES]
            base += size
        for i in range(size // 8):
            rows = pl.ds(pl.multiple_of(at + 8 * i + skip, 8), 8)
            to = tail + 8 * (group // 8)
            strip = 16 * (group % 8)
            out_ref[to : to + 8, strip : strip + 16] = prod_ref[rows, 2 * LANES : COLS_OUT]
            group += 1
        at += size + 8


def begin_kernel(place, smooth_ref, out_ref, right_ref, left_ref):
    build_right(smooth_ref, right_ref)
    out_ref[...] = product(place, smooth_ref, right_ref, left_ref)


def finish_kernel(place, part_ref, smooth_ref, out_ref, right_ref, left_ref, prod_ref):
    build_right(smooth_ref, right_ref)
    prod_ref[...] = part_ref[...] + product(place, smooth_ref, right_ref, left_ref)
    emit(place, prod_ref, out_ref)


def gram_kernel(place, own_ref, own_right_ref, other_ref, other_right_ref, out_ref, left_ref, prod_ref):
    prod_ref[...] = product(place, own_ref, own_right_ref, left_ref)
    prod_ref[...] += product(place, other_ref, other_right_ref, left_ref)
    emit(place, prod_ref, out_ref)


def add_kernel(a_ref, b_ref, out_ref):
    out_ref[...] = a_ref[...] + b_ref[...]


def cut_kernel(a_ref, b_ref, far_ref, rest_ref):
    far_ref[...] = a_ref[0:LAST, :] + b_ref[0:LAST, :]
    rest_ref[...] = a_ref[LAST:SENT, :] + b_ref[LAST:SENT, :]


def split_kernel(a_ref, b_ref, own_ref, near_ref, cross_ref):
    core = lax.axis_index("hor") % 2
    lane = lax.broadcasted_iota(jnp.int32, (8, LANES), 1)

    def total(start, size):
        rows = pl.ds(start if isinstance(start, int) else pl.multiple_of(start, 8), size)
        return a_ref[rows, :] + b_ref[rows, :]

    ahead = 2 * CHUNK
    places = (
        (near_ref, ahead + 64 * core, BOTH, 1 + core, 1),
        (cross_ref, ahead + 64 * (1 - core), BOTH, 2 - core, 1),
        (own_ref, 0, CHUNK, 0, 0),
    )
    for ref, start, stride, tile, strip in places:
        ref[0:CHUNK, :] = total(start, CHUNK)
        ref[CHUNK : 2 * CHUNK, :] = total(start + stride, CHUNK)
        one, two = total(REST + 8 * tile, 8), total(REST + 8 * tile + 8, 8)
        if strip:
            one, two = pltpu.roll(one, LANES - 16 * strip, 1), pltpu.roll(two, LANES - 16 * strip, 1)
            one = jnp.where(lane < LANES - 16 * strip, one, two)
        ref[2 * CHUNK : 2 * CHUNK + 8, :] = one
        ref[2 * CHUNK + 8 : LAST, :] = two


def final_kernel(kept_ref, near_ref, out_ref):
    odd = lax.axis_index("hor") % 2 == 1
    scale = 1.0 / (BLOCK * N_HOR)

    def total(rows):
        return kept_ref[rows, :] + near_ref[rows, :]

    def place(value):
        return jnp.where(odd, value[CHUNK - ROWS_OUT : CHUNK], value[0:ROWS_OUT]) * scale

    for half in range(2):
        value = total(slice(half * CHUNK, (half + 1) * CHUNK))
        out_ref[:, half * LANES : (half + 1) * LANES] = place(value)
    packed = total(slice(2 * CHUNK, 2 * CHUNK + 8))
    rest = [pltpu.roll(packed, -16 * group % LANES, 1) for group in range(8)]
    rest.append(total(slice(2 * CHUNK + 8, LAST)))
    out_ref[:, 2 * LANES :] = place(jnp.concatenate(rest, axis=0))[:, :16]


def filter_coefficients(thickness, level_cuts):
    link = 1.0 - level_cuts.astype(jnp.float32)
    zero_one = jnp.zeros((1,), jnp.float32)
    lower = jnp.concatenate([zero_one, thickness[:-1] * link])
    upper = jnp.concatenate([thickness[1:] * link, zero_one])
    denom = 2.0 * thickness + lower + upper
    coef = jnp.concatenate([2.0 * thickness / denom, lower / denom, upper / denom])
    return jnp.broadcast_to(coef[:, None], (3 * LEV, LANES))


def gram(kernel, place, out_shape, *operands):
    scratch = [pltpu.VMEM((BUILT, BLOCK), jnp.bfloat16), pltpu.VMEM((BUILT, COLS_OUT), jnp.float32)]
    return pl.pallas_call(
        functools.partial(kernel, place),
        out_shape=out_shape,
        in_specs=[VMEM] * len(operands),
        out_specs=jax.tree.map(lambda _: VMEM, out_shape),
        scratch_shapes=scratch[:1] if kernel is begin_kernel else scratch,
        compiler_params=params(12),
        cost_estimate=cost(1, SHARE),
        name="gram_" + place,
    )(*operands)


def add(a, b, share=1):
    return pl.pallas_call(
        add_kernel,
        out_shape=jax.ShapeDtypeStruct(a.shape, a.dtype),
        in_specs=[VMEM] * 2,
        out_specs=VMEM,
        compiler_params=params(4),
        cost_estimate=cost(share, SHARE),
        name="add",
    )(a, b)


def cut(a, b):
    shapes = ((LAST, LANES), (SENT - LAST, LANES))
    return pl.pallas_call(
        cut_kernel,
        out_shape=[jax.ShapeDtypeStruct(shape, a.dtype) for shape in shapes],
        in_specs=[VMEM] * 2,
        out_specs=[VMEM] * 2,
        compiler_params=params(4),
        cost_estimate=cost(1, SHARE),
        name="cut",
    )(a, b)


def on_device(slab_fields, sample_index, thickness, level_cuts):
    f32 = jnp.float32
    coef = filter_coefficients(thickness, level_cuts)
    repeated = pl.pallas_call(
        repeat_kernel,
        out_shape=jax.ShapeDtypeStruct((N_LEV, 1, SAMP), jnp.int32),
        in_specs=[VMEM],
        out_specs=VMEM,
        compiler_params=params(60),
        name="repeat",
    )(sample_index)
    lists = lax.all_to_all(repeated, "lev", 0, 0, tiled=True)
    staged = pl.pallas_call(
        stage_kernel,
        out_shape=jax.ShapeDtypeStruct((4 * SLOTS, N_LEV * GROUP), f32),
        in_specs=[VMEM],
        out_specs=VMEM,
        compiler_params=params(8),
        cost_estimate=cost(0, 2 << 20),
        name="stage",
    )(slab_fields)
    picked = pl.pallas_call(
        pick_kernel,
        out_shape=jax.ShapeDtypeStruct((4 * SLOTS, BLOCK), f32),
        in_specs=[VMEM] * 2,
        out_specs=VMEM,
        compiler_params=params(8),
        name="pick",
    )(lists, staged)
    across = shift_lev(picked, 1, 0)
    up = lax.axis_index("lev") // N_X == 1
    near = jnp.stack([jnp.where(up, across, picked), jnp.where(up, picked, across)])
    far = {k: shift_lev(near, 0, k) for k in (2, 1, 3)}
    own = pl.pallas_call(
        smooth_kernel,
        out_shape=jax.ShapeDtypeStruct((SLOTS * LEV, BLOCK), f32),
        in_specs=[VMEM] * 5,
        out_specs=VMEM,
        scratch_shapes=[pltpu.VMEM((N_LEV, 4 * SLOTS, BLOCK), f32)],
        compiler_params=params(16),
        name="smooth",
    )(coef, near, far[3], far[1], far[2])
    other = swap_cores(own)
    right = jax.ShapeDtypeStruct((COLS_OUT, BLOCK), jnp.bfloat16)
    begun, own_right = gram(begin_kernel, "far", [jax.ShapeDtypeStruct((BUILT, COLS_OUT), f32), right], own)
    sent = jax.ShapeDtypeStruct((SENT, LANES), f32)
    far, other_right = gram(finish_kernel, "far", [sent, right], begun, other)
    parts = {"far": far}
    both = (own, own_right, other, other_right)
    parts["cross"] = gram(gram_kernel, "cross", sent, *both)
    both, parts["cross"] = lax.optimization_barrier((both, parts["cross"]))
    parts["near"] = gram(gram_kernel, "near", sent, *both)
    parts["own"] = gram(gram_kernel, "own", sent, *both)
    two_back = hop(parts["far"], "y", 0)
    from_cross = hop(parts["cross"], "y", 1)
    parts["near"], parts["own"] = lax.optimization_barrier((parts["near"], parts["own"]))
    near_far, near_rest = cut(parts["near"], two_back)
    from_near_far, from_near_rest = hop(near_far, "y", 0), hop(near_rest, "y", 0)
    sum_far, sum_rest = cut(parts["own"], from_cross)
    two_back = hop(add(sum_far, from_near_far, 1 << 30), "z_hi", 0)
    kept, near, cross = pl.pallas_call(
        split_kernel,
        out_shape=[jax.ShapeDtypeStruct((LAST, LANES), f32)] * 3,
        in_specs=[VMEM] * 2,
        out_specs=[VMEM] * 3,
        compiler_params=params(8),
        cost_estimate=cost(1, SHARE),
        name="split",
    )(sum_rest, from_near_rest)
    from_cross = hop(cross, "z_hi", 1)
    kept = add(kept, from_cross)
    from_near = hop(add(near, two_back), "z_hi", 0)
    return pl.pallas_call(
        final_kernel,
        out_shape=jax.ShapeDtypeStruct((ROWS_OUT, COLS_OUT), f32),
        in_specs=[VMEM] * 2,
        out_specs=VMEM,
        compiler_params=params(8),
        cost_estimate=cost(1, SHARE),
        name="final",
    )(kept, from_near)


def solution(mesh):
    in_specs = (P(None, "lev", "hor"), P("hor", "lev"), P(), P())
    out_specs = P("hor", "lev")
    return jax.shard_map(on_device, mesh=mesh, in_specs=in_specs, out_specs=out_specs, check_vma=False)
```
